32 devices in a mesh: rep: 2 (over y), seq: 16 (over z, x, core).
Axes of the slice: x: 2, y: 2, z: 4, core: 2. Of those that a mesh axis runs over, the one named last changes fastest.
Arguments:
- samples: bfloat16 [2, 8192, 512], P('rep', 'seq'), may hold values from -6 to 6
- clip_lengths: int32 [2, 4], P('rep'), may hold values from 1 to 1536, 4096 in all within a row
- stem_weight: bfloat16 [1536, 512], replicated, may hold values from -0.15625 to 0.15625
- stem_gain: float32 [512], replicated, may hold values from 0.5 to 1.5
- stem_bias: float32 [512], replicated, may hold values from -1.5 to 1.5
- proj_weight: bfloat16 [512, 768], replicated, may hold values from -0.25 to 0.25
- pos_weight: bfloat16 [6144, 768], replicated, may hold values from -0.078125 to 0.078125
- norm_gains: float32 [768, 3], replicated, may hold values from 0.5 to 1.5
- biases: float32 [768, 9], replicated, may hold values from -1.5 to 1.5
- attn_in: bfloat16 [768, 2304], replicated, may hold values from -0.21875 to 0.21875
- attn_out: bfloat16 [768, 768], replicated, may hold values from -1.75 to 1.75
- ffn_in: bfloat16 [768, 3072], replicated, may hold values from -0.21875 to 0.21875
- ffn_in_bias: float32 [3072], replicated, may hold values from -1.5 to 1.5
- ffn_out: bfloat16 [3072, 768], replicated, may hold values from -0.109375 to 0.109375
- out_grad: bfloat16 [2, 4096, 768], P('rep', 'seq'), may hold values from -6 to 6
Outputs:
- layer_out: bfloat16 [2, 4096, 768], P('rep', 'seq')
- sample_grad: float32 [2, 8192, 512], P('rep', 'seq')
- stem_weight_grad: float32 [1536, 512], P('seq')
- stem_gain_grad: float32 [512], P('seq')
- stem_bias_grad: float32 [512], P('seq')
- proj_weight_grad: float32 [512, 768], P('seq')
- pos_weight_grad: float32 [6144, 768], P('seq')
- norm_gains_grad: float32 [768, 3], P('seq')
- biases_grad: float32 [768, 9], P('seq')
- attn_in_grad: float32 [768, 2304], P('seq')
- attn_out_grad: float32 [768, 768], P('seq')
- ffn_in_grad: float32 [768, 3072], P('seq')
- ffn_in_bias_grad: float32 [3072], P('seq')
- ffn_out_grad: float32 [3072, 768], P('seq')
The draws below stay inside these ranges and needn't reach their ends.
Inputs may be any that keep to these rules, and one draw needn't show every extreme that they name: `clip_lengths`: A stream's 4 clip lengths add up to 4096; the longest is exactly 1536.
All inputs are finite; a program needn't handle non-finite values.
Results may differ from the reference program's by a relative error of at most 0.018.
Values may be sent and summed in bfloat16 or wider, within the bound.
No kernel may reach another device: no remote copies, remote signals or barrier semaphores. Data moves between devices by JAX's collectives and lax.ppermute only.
A program may use at most 256 MiB of HBM per device.

```python
import math
import jax
import jax.numpy as jnp
import numpy as np
from jax import lax

C = 512
D = 768
HEADS = 12
HEAD_DIM = 64
FF = 3072
KERNEL = 128
GROUPS = 16
MAXLEN = 1536
TOK = 256
STREAMS = 2
LEN = 4096
CLIPS = 4
REACH = 6
N_SEQ = 16


def spiked(array, own_key, source, target, shards_of, factor):
    owner, partner = [(jnp.arange(array.shape[dim]) // (array.shape[dim] // shards_of)).reshape([-1 if axis == dim else 1 for axis in range(array.ndim)]) for dim in (source, target)]
    chosen = jax.random.permutation(own_key, shards_of)[partner]
    strong = (owner == chosen) | (owner == (partner + shards_of // 2) % shards_of)
    return jnp.where(strong, factor * array, array)


def levels(own_key, dims, split, least, top_value):
    def one(axis_at, parts):
        steps = jax.random.uniform(jax.random.fold_in(jax.random.fold_in(own_key, 6), axis_at), (parts,), jnp.float32, least / len(split), top_value / len(split))
        return jnp.repeat(jnp.exp(steps), dims[axis_at] // parts).reshape((-1,) + (1,) * (len(dims) - axis_at - 1))

    loudness = one(*split[0])
    for cut in split[1:]:
        loudness = loudness * one(*cut)
    return loudness


def split_up(count, total, limit, skew):
    portions = [(1 << 20) // math.isqrt(rank ** skew) + 1 for rank in range(2, count + 1)]
    surplus, holding = total - limit - (count - 1), [1] * (count - 1)
    while surplus > 0:
        candidates = [i for i in range(count - 1) if holding[i] < limit]
        pool, budget = sum([portions[i] for i in candidates]), surplus
        for i in candidates:
            addition = min(limit - holding[i], max(1, budget * portions[i] // pool), surplus)
            holding[i] = holding[i] + addition
            surplus = surplus - addition
    return np.array([limit] + holding)


def uneven(key, count, total, bound, skew):
    if count == 2:
        one = jax.random.randint(key, (), max(1, total - bound), min(bound, total - 1) + 1)
        return jnp.stack([one, total - one])
    tallies = jnp.asarray(split_up(count, total, bound, skew), jnp.int32)
    couples = (count - 1) // 2
    source_of, receiver = tallies[1:1 + 2 * couples:2], tallies[2:2 + 2 * couples:2]
    margin = jnp.minimum(source_of - 1, bound - receiver)
    moved = jax.random.randint(jax.random.fold_in(key, 1), (couples,), 0, 1 << 20) % (margin + 1)
    tallies = tallies.at[1:1 + 2 * couples:2].set(source_of - moved).at[2:2 + 2 * couples:2].set(receiver + moved)
    return tallies[jax.random.permutation(jax.random.fold_in(key, 2), count)]


def centred(stream_key, shape, deviation, most, shards=(), held_as=jnp.bfloat16):
    array = deviation * jax.random.normal(stream_key, shape, jnp.float32)
    if shards:
        array = array * levels(stream_key, shape, shards, -0.22, 0.18)
    return jnp.clip(array, -most, most).astype(held_as)


def gaussian_with(rng, extent, scale, limit, pieces, heavy, kind=jnp.bfloat16):
    values = scale * jax.random.normal(rng, extent, jnp.float32)
    if pieces:
        values = values * levels(rng, extent, pieces, -0.22, 0.18)
    return jnp.clip(spiked(values, jax.random.fold_in(rng, 3), *heavy), -limit, limit).astype(kind)


def setup_inputs(seed: int = 0) -> dict:
    streams_of = jax.random.split(jax.random.key(seed), 16)
    samples = centred(streams_of[0], (STREAMS, 2 * LEN, C), 1.0, 6.0, ((0, 2), (1, 16)))
    clip_lengths = jax.vmap(lambda own: uneven(own, CLIPS, LEN, MAXLEN, 1))(jax.random.split(streams_of[1], STREAMS)).reshape((STREAMS, CLIPS)).astype(jnp.int32)
    stem_weight = centred(streams_of[2], (3 * C, C), (3 * C) ** -0.5, 0.15625)
    stem_gain = jnp.clip(1.0 + 0.1 * jax.random.normal(streams_of[3], (C,), jnp.float32), 0.5, 1.5)
    stem_bias = centred(streams_of[4], (C,), 0.3, 1.5, (), jnp.float32)
    proj_weight = centred(streams_of[5], (C, D), C ** -0.5, 0.25)
    pos_weight = centred(streams_of[6], (KERNEL * (D // GROUPS), D), (KERNEL * (D // GROUPS)) ** -0.5, 0.078125)
    norm_gains = jnp.clip(1.0 + 0.1 * jax.random.normal(streams_of[7], (D, 3), jnp.float32), 0.5, 1.5)
    biases = centred(streams_of[8], (D, 9), 0.3, 1.5, (), jnp.float32)
    attn_in = centred(streams_of[9], (D, 3 * D), D ** -0.5, 0.21875)
    attn_out = centred(streams_of[10], (D, D), (D // 64) ** -0.5, 1.75)
    ffn_in = centred(streams_of[11], (D, FF), D ** -0.5, 0.21875)
    ffn_in_bias = centred(streams_of[12], (FF,), 0.3, 1.5, (), jnp.float32)
    ffn_out = centred(streams_of[13], (FF, D), FF ** -0.5, 0.109375)
    out_grad = gaussian_with(streams_of[14], (STREAMS, LEN, D), 1.0, 6.0, ((0, 2), (1, 16)), (1, 2, 16, 2.0))
    return dict(samples=samples, clip_lengths=clip_lengths, stem_weight=stem_weight, stem_gain=stem_gain, stem_bias=stem_bias, proj_weight=proj_weight, pos_weight=pos_weight, norm_gains=norm_gains, biases=biases, attn_in=attn_in, attn_out=attn_out, ffn_in=ffn_in, ffn_in_bias=ffn_in_bias, ffn_out=ffn_out, out_grad=out_grad)


@jax.custom_vjp
def low(v):
    return lax.optimization_barrier(v.astype(jnp.bfloat16)).astype(jnp.float32)

@jax.custom_vjp
def low_back(v):
    return v

def low_keep(v):
    return (low(v), None)

def low_pass(kept, grad):
    return (grad,)

def back_keep(v):
    return (v, None)

def back_low(kept, grad):
    return (low(grad),)
low.defvjp(low_keep, low_pass)
low_back.defvjp(back_keep, back_low)
HIGH = lax.Precision.HIGHEST

def matmul(left, right):
    return jnp.dot(left, right, precision=HIGH, preferred_element_type=jnp.float32)

def norm_rows(values, scales, shifts):
    center = values - lax.optimization_barrier(jnp.mean(values, axis=-1, keepdims=True))
    spread = lax.optimization_barrier(jnp.mean(center * center, axis=-1, keepdims=True))
    return center * lax.rsqrt(spread + 1e-05) * scales + shifts

def gelu_exact(values):
    return jax.nn.gelu(values, approximate=False)

def clip_ids(lengths):
    ends = jnp.cumsum(lengths).astype(jnp.int32)
    places = jnp.arange(LEN, dtype=jnp.int32)
    return lax.optimization_barrier(jnp.sum((places[:, None] >= ends[None, :]).astype(jnp.int32), axis=1))

def conv_block(padded, padded_ids, own_ids, weight_rows, first):
    group_width = D // GROUPS
    running = jnp.zeros((LEN, GROUPS, group_width), jnp.float32)
    for inner in range(8):
        shifted = lax.dynamic_slice_in_dim(padded, first + inner, LEN, 0)
        keep = lax.dynamic_slice_in_dim(padded_ids, first + inner, LEN, 0) == own_ids
        shifted = jnp.where(keep[:, None], shifted, 0.0).reshape(LEN, GROUPS, group_width)
        kernel = weight_rows[inner * group_width:(inner + 1) * group_width].reshape(group_width, GROUPS, group_width)
        running = running + jnp.einsum('tgi,igo->tgo', shifted, kernel, precision=HIGH)
    return running.reshape(LEN, D)
conv_saved = jax.checkpoint(conv_block, static_argnums=(4,))

def attention(query, keys, values, ids):
    scale = HEAD_DIM ** (-0.5)
    window = (2 * REACH + 1) * TOK
    query3 = query.reshape(LEN, HEADS, HEAD_DIM)
    keys3 = jnp.pad(keys.reshape(LEN, HEADS, HEAD_DIM), ((REACH * TOK, REACH * TOK), (0, 0), (0, 0)))
    values3 = jnp.pad(values.reshape(LEN, HEADS, HEAD_DIM), ((REACH * TOK, REACH * TOK), (0, 0), (0, 0)))
    key_ids = jnp.pad(ids, (REACH * TOK, REACH * TOK), constant_values=-1)

    def one_block(index):
        start = (index * TOK).astype(jnp.int32)
        block_query = lax.dynamic_slice_in_dim(query3, start, TOK, 0)
        block_keys = lax.dynamic_slice_in_dim(keys3, start, window, 0)
        block_values = lax.dynamic_slice_in_dim(values3, start, window, 0)
        query_ids = lax.dynamic_slice_in_dim(ids, start, TOK, 0)
        window_ids = lax.dynamic_slice_in_dim(key_ids, start, window, 0)
        raw = low_back(jnp.einsum('qhd,khd->hqk', block_query, block_keys, precision=HIGH))
        allowed = (query_ids[:, None] == window_ids[None, :])[None]
        scores = jnp.where(allowed, raw * scale, -1e+30)
        probs = low(jax.nn.softmax(scores, axis=-1))
        return jnp.einsum('hqk,khd->qhd', probs, block_values, precision=HIGH)
    blocks = lax.map(jax.checkpoint(one_block), jnp.arange(N_SEQ, dtype=jnp.int32))
    return blocks.reshape(LEN, D)

def stream_forward(sample_rows, ids, params):
    stem_weight, stem_gain, stem_bias, proj_weight, pos_weight, norm_gains, biases, attn_in, attn_out, ffn_in, ffn_in_bias, ffn_out = params
    group_width = D // GROUPS
    half = KERNEL // 2
    frames = sample_rows.reshape(LEN, 2 * C)
    same_next = jnp.concatenate([ids[1:] == ids[:-1], jnp.zeros((1,), bool)])
    following = jnp.concatenate([frames[1:, :C], jnp.zeros((1, C), jnp.float32)], axis=0)
    following = jnp.where(same_next[:, None], following, 0.0)
    unfold = jnp.concatenate([frames, following], axis=1)
    feature = gelu_exact(low_back(matmul(unfold, stem_weight)))
    normed = low(norm_rows(feature, stem_gain, stem_bias))
    start_x = low_back(matmul(normed, proj_weight)) + biases[:, 0]
    start_b = low(start_x)
    padded = jnp.pad(start_b, ((half, half), (0, 0)))
    padded_ids = jnp.pad(ids, (half, half), constant_values=-1)
    conv_sum = jnp.zeros((LEN, D), jnp.float32)
    for first in range(0, KERNEL, 8):
        conv_sum = conv_sum + conv_saved(padded, padded_ids, ids, pos_weight[first * group_width:(first + 8) * group_width], first)
    conv_out = low_back(conv_sum) + biases[:, 1]
    mixed = start_x + gelu_exact(conv_out)
    hidden = norm_rows(mixed, norm_gains[:, 0], biases[:, 2])
    hidden_b = low(hidden)
    project = matmul(hidden_b, attn_in)
    query = low(low_back(project[:, :D]) + biases[:, 3])
    keys = low(low_back(project[:, D:2 * D]))
    values = low(low_back(project[:, 2 * D:]) + biases[:, 4])
    attended_b = low(low_back(attention(query, keys, values, ids)))
    branch = low_back(matmul(attended_b, attn_out)) + biases[:, 5]
    second = norm_rows(hidden + branch, norm_gains[:, 1], biases[:, 6])
    second_b = low(second)
    inner = low_back(matmul(second_b, ffn_in)) + ffn_in_bias
    inner_b = low(gelu_exact(inner))
    outer = low_back(matmul(inner_b, ffn_out)) + biases[:, 7]
    return norm_rows(second + outer, norm_gains[:, 2], biases[:, 8])

def reference(samples, clip_lengths, stem_weight, stem_gain, stem_bias, proj_weight, pos_weight, norm_gains, biases, attn_in, attn_out, ffn_in, ffn_in_bias, ffn_out, out_grad):
    id_rows = [clip_ids(clip_lengths[index]) for index in range(STREAMS)]
    weights = (stem_weight.astype(jnp.float32), stem_gain, stem_bias, proj_weight.astype(jnp.float32), pos_weight.astype(jnp.float32), norm_gains, biases, attn_in.astype(jnp.float32), attn_out.astype(jnp.float32), ffn_in.astype(jnp.float32), ffn_in_bias, ffn_out.astype(jnp.float32))

    def forward(sample_values, params):
        return jnp.stack([stream_forward(sample_values[index], id_rows[index], params) for index in range(STREAMS)])
    result, pullback = jax.vjp(forward, samples.astype(jnp.float32), weights)
    sample_grad, grads = pullback(out_grad.astype(jnp.float32))
    return (result.astype(jnp.bfloat16), sample_grad, grads[0], grads[1], grads[2], grads[3], grads[4], grads[5], grads[6], grads[7], grads[8], grads[9], grads[10], grads[11])
```

```python
import functools

import jax
import jax.numpy as jnp
from jax import lax
from jax.experimental import pallas as pl
from jax.experimental.pallas import tpu as pltpu
from jax.sharding import PartitionSpec as P

HEADS = 12
KERNEL = 128
GROUPS = 16
MAXLEN = 1536
RING = 16

def row_dot(left, right):
    return lax.dot_general(left, right, (((1,), (1,)), ((), ())), preferred_element_type=jnp.float32)


def plain_dot(left, right):
    return lax.dot_general(left, right, (((1,), (0,)), ((), ())), preferred_element_type=jnp.float32)


def over_rows_dot(left, right):
    return lax.dot_general(left, right, (((0,), (0,)), ((), ())), preferred_element_type=jnp.float32)


VMEM_WHOLE = pl.BlockSpec(memory_space=pltpu.VMEM)
SMEM_WHOLE = pl.BlockSpec(memory_space=pltpu.SMEM)
HEAD_DIM = 64
Q_TILE = 512
K_TILE = 512
LOW = -1e30


def unpack_heads(packed_ref, targets, factor):
    blocks, half, lanes = packed_ref.shape
    share = lanes // 2

    def one(block, carry):
        tile = packed_ref[block]
        for side in range(2):
            row = pl.multiple_of(block * 2 * half + side * half, half)
            for place, target in enumerate(targets):
                begin = side * share + place * HEAD_DIM
                piece = tile[:, begin : begin + HEAD_DIM]
                if place == 0 and factor != 1.0:
                    piece = piece * jnp.bfloat16(factor)
                target[pl.ds(row, half), :] = piece
        return carry

    lax.fori_loop(0, blocks, one, 0)


def attend_kernel(
    halo, low_ref, high_ref, packed_ref, query_ids_ref, key_ids_ref, out_ref, wide_ref, log_ref,
    query, keys, values,
):
    scale = HEAD_DIM ** (-0.5)
    unpack_heads(packed_ref, (query, keys, values), scale)
    rows = query_ids_ref.shape[0]
    half = packed_ref.shape[1]
    block = 2 * half

    def query_tile(index, carry):
        first = pl.multiple_of(index * Q_TILE, Q_TILE)
        q = query[pl.ds(halo * block + first, Q_TILE), :]
        q_ids = query_ids_ref[pl.ds(first, Q_TILE), :]

        def key_tile(at, state):
            top, mass, total = state
            column = pl.multiple_of(at * K_TILE, K_TILE)
            scores = row_dot(q, keys[pl.ds(column, K_TILE), :])
            scores = jnp.where(q_ids == key_ids_ref[:, pl.ds(column, K_TILE)], scores, LOW)
            new_top = jnp.maximum(top, jnp.max(scores, axis=1, keepdims=True))
            weight = jnp.exp(scores - new_top)
            fade = jnp.exp(top - new_top)
            mass = fade * mass + jnp.sum(weight, axis=1, keepdims=True)
            total = fade * total + plain_dot(
                weight.astype(jnp.bfloat16), values[pl.ds(column, K_TILE), :]
            )
            return new_top, mass, total

        top, mass, total = lax.fori_loop(
            low_ref[index],
            high_ref[index],
            key_tile,
            (
                jnp.full((Q_TILE, 1), 0.5 * LOW, jnp.float32),
                jnp.zeros((Q_TILE, 1), jnp.float32),
                jnp.zeros((Q_TILE, HEAD_DIM), jnp.float32),
            ),
        )
        mass = jnp.maximum(mass, 1e-37)
        attended = total / mass
        wide_ref[pl.ds(first, Q_TILE), :] = attended
        log_ref[pl.ds(first, Q_TILE), :] = top + jnp.log(mass)
        narrow = attended.astype(jnp.bfloat16)
        for inner in range(Q_TILE // block):
            spot = index * (Q_TILE // block) + inner
            out_ref[spot, :, 0:HEAD_DIM] = narrow[inner * block : inner * block + half]
            out_ref[spot, :, HEAD_DIM:] = narrow[inner * block + half : (inner + 1) * block]
        return carry

    lax.fori_loop(0, rows // Q_TILE, query_tile, 0)


def attend(low, high, packed, query_ids, key_ids, halo):
    blocks, half, _ = packed.shape
    rows = query_ids.shape[0]
    key_rows = blocks * 2 * half
    return pl.pallas_call(
        functools.partial(attend_kernel, halo),
        out_shape=(
            jax.ShapeDtypeStruct((blocks - 2 * halo, half, 2 * HEAD_DIM), jnp.bfloat16),
            jax.ShapeDtypeStruct((rows, HEAD_DIM), jnp.float32),
            jax.ShapeDtypeStruct((rows, 1), jnp.float32),
        ),
        in_specs=[SMEM_WHOLE] * 2 + [VMEM_WHOLE] * 3,
        out_specs=(VMEM_WHOLE,) * 3,
        scratch_shapes=[pltpu.VMEM((key_rows, HEAD_DIM), jnp.bfloat16)] * 3,
        compiler_params=pltpu.CompilerParams(vmem_limit_bytes=56 << 20),
        name="attend",
    )(low, high, packed, query_ids, key_ids)


def attend_back_kernel(
    halo, low_ref, high_ref, packed_ref, grad_ref, wide_ref, log_ref, query_ids_ref, key_ids_ref,
    out_ref, query, keys, values, grads, key_grads, value_grads,
):
    scale = HEAD_DIM ** (-0.5)
    unpack_heads(packed_ref, (query, keys, values), scale)
    unpack_heads(grad_ref, (grads,), 1.0)
    blocks, half, _ = packed_ref.shape
    rows = query_ids_ref.shape[0]
    block = 2 * half
    key_grads[...] = jnp.zeros_like(key_grads)
    value_grads[...] = jnp.zeros_like(value_grads)
    if halo:
        out_ref[...] = jnp.zeros_like(out_ref)

    def query_tile(index, carry):
        first = pl.multiple_of(index * Q_TILE, Q_TILE)
        q = query[pl.ds(halo * block + first, Q_TILE), :]
        g = grads[pl.ds(first, Q_TILE), :]
        q_ids = query_ids_ref[pl.ds(first, Q_TILE), :]
        log_total = log_ref[pl.ds(first, Q_TILE), :]
        delta = jnp.sum(
            g.astype(jnp.float32) * wide_ref[pl.ds(first, Q_TILE), :], axis=1, keepdims=True
        )

        def key_tile(at, running):
            column = pl.multiple_of(at * K_TILE, K_TILE)
            k = keys[pl.ds(column, K_TILE), :]
            v = values[pl.ds(column, K_TILE), :]
            probs = jnp.where(
                q_ids == key_ids_ref[:, pl.ds(column, K_TILE)],
                jnp.exp(row_dot(q, k) - log_total),
                0.0,
            )
            prob_grad = row_dot(g, v)
            score_grad = (probs * (prob_grad - delta) * scale).astype(jnp.bfloat16)
            value_grads[pl.ds(column, K_TILE), :] += over_rows_dot(probs.astype(jnp.bfloat16), g)
            key_grads[pl.ds(column, K_TILE), :] += over_rows_dot(score_grad, q)
            return running + plain_dot(score_grad, k)

        query_grad = lax.fori_loop(
            low_ref[index], high_ref[index], key_tile, jnp.zeros((Q_TILE, HEAD_DIM), jnp.float32)
        ).astype(jnp.bfloat16)
        for inner in range(Q_TILE // block):
            spot = halo + index * (Q_TILE // block) + inner
            out_ref[spot, :, 0:HEAD_DIM] = query_grad[inner * block : inner * block + half]
            out_ref[spot, :, 3 * HEAD_DIM : 4 * HEAD_DIM] = query_grad[
                inner * block + half : (inner + 1) * block
            ]
        return carry

    lax.fori_loop(0, rows // Q_TILE, query_tile, 0)

    def finish(spot, carry):
        for side in range(2):
            row = pl.multiple_of(spot * block + side * half, half)
            begin = (3 * side + 1) * HEAD_DIM
            out_ref[spot, :, begin : begin + HEAD_DIM] = (
                key_grads[pl.ds(row, half), :] * (1.0 / scale)
            ).astype(jnp.bfloat16)
            out_ref[spot, :, begin + HEAD_DIM : begin + 2 * HEAD_DIM] = value_grads[
                pl.ds(row, half), :
            ].astype(jnp.bfloat16)
        return carry

    lax.fori_loop(0, blocks, finish, 0)


def attend_back(low, high, packed, grad, wide, log_total, query_ids, key_ids, halo):
    blocks, half, lanes = packed.shape
    rows = query_ids.shape[0]
    key_rows = blocks * 2 * half
    return pl.pallas_call(
        functools.partial(attend_back_kernel, halo),
        out_shape=jax.ShapeDtypeStruct((blocks, half, lanes), jnp.bfloat16),
        in_specs=[SMEM_WHOLE] * 2 + [VMEM_WHOLE] * 6,
        out_specs=VMEM_WHOLE,
        scratch_shapes=[pltpu.VMEM((key_rows, HEAD_DIM), jnp.bfloat16)] * 3
        + [pltpu.VMEM((rows, HEAD_DIM), jnp.bfloat16)]
        + [pltpu.VMEM((key_rows, HEAD_DIM), jnp.float32)] * 2,
        compiler_params=pltpu.CompilerParams(vmem_limit_bytes=60 << 20),
        name="attend_back",
    )(low, high, packed, grad, wide, log_total, query_ids, key_ids)

TAPS = 16
PARTS = 4


def conv_kernel(back, rows_ref, ids_ref, weight_ref, out_ref, planes, shifted, block, total):
    step = pl.program_id(0)
    rows, width = out_ref.shape
    group_width = width // GROUPS
    part = width // PARTS
    held = GROUPS // PARTS
    long = planes.shape[1]

    @pl.when(step == 0)
    def _():
        for at in range(PARTS):
            planes[at] = rows_ref[:, at * part : (at + 1) * part].astype(jnp.float32)
        planes[PARTS] = jnp.broadcast_to(ids_ref[...], (long, part))

        def plane(at, carry):
            tile = planes[at]

            def pair(two, inner_carry):
                if back:
                    first, second = TAPS - 2 * two, TAPS - 2 * two - 1
                else:
                    first, second = 2 * two, 2 * two + 1
                both = jnp.concatenate(
                    [
                        pltpu.roll(tile, lax.rem(long - first, long), 0),
                        pltpu.roll(tile, lax.rem(long - second, long), 0),
                    ],
                    axis=1,
                ).astype(jnp.bfloat16)
                lanes = pl.multiple_of(two * 2 * part, 128)
                shifted[at, :, pl.ds(lanes, 2 * part)] = both[: long - TAPS]
                return inner_carry

            return lax.fori_loop(0, TAPS // 2, pair, carry)

        lax.fori_loop(0, PARTS + 1, plane, 0)

    turn = (KERNEL // TAPS - 1 - step) if back else step
    base = pl.multiple_of(turn * TAPS, TAPS)
    own = ids_ref[pl.ds(KERNEL // 2, rows), :].astype(jnp.bfloat16)
    keep = shifted[PARTS, pl.ds(base, rows), :] == jnp.broadcast_to(own, (rows, TAPS * part))
    lane = lax.broadcasted_iota(jnp.int32, (group_width, 2 * part), 1)
    lane = jnp.where(lane >= part, lane - part, lane)
    nothing = jnp.bfloat16(0)
    for at in range(PARTS):

        def fill(two, carry):
            row = pl.multiple_of(2 * two * group_width, 16)
            own_lanes = slice(at * part, (at + 1) * part)
            one = weight_ref[pl.ds(row, group_width), own_lanes]
            other = weight_ref[pl.ds(pl.multiple_of(row + group_width, 16), group_width), own_lanes]
            for group in range(held):
                inside = (lane >= group * group_width) & (lane < (group + 1) * group_width)
                if back:
                    both = jnp.concatenate([one, other], axis=1)
                    lanes = pl.multiple_of(two * 2 * part, 128)
                    block[
                        group * group_width : (group + 1) * group_width, pl.ds(lanes, 2 * part)
                    ] = jnp.where(inside, both, nothing)
                else:
                    for side, piece in enumerate((one, other)):
                        place = pl.multiple_of((2 * two + side) * part + group * group_width, 16)
                        block[pl.ds(place, group_width), :] = jnp.where(
                            inside[:, :part], piece, nothing
                        )
            return carry

        lax.fori_loop(0, TAPS // 2, fill, 0)
        taken = jnp.where(keep, shifted[at, pl.ds(base, rows), :], nothing)
        result = (row_dot if back else plain_dot)(taken, block[...])

        @pl.when(step == 0)
        def _():
            total[at] = result

        @pl.when(step > 0)
        def _():
            total[at] += result

    @pl.when(step == pl.num_programs(0) - 1)
    def _():
        for at in range(PARTS):
            out_ref[:, at * part : (at + 1) * part] = total[at]


def conv_rows(back, padded, padded_ids, weight):
    long, width = padded.shape
    rows = long - KERNEL
    part = width // PARTS
    group_width = width // GROUPS
    return pl.pallas_call(
        functools.partial(conv_kernel, back),
        grid=(KERNEL // TAPS,),
        out_shape=jax.ShapeDtypeStruct((rows, width), jnp.float32),
        in_specs=[
            pl.BlockSpec((long, width), lambda step: (0, 0)),
            pl.BlockSpec((long, 1), lambda step: (0, 0)),
            pl.BlockSpec((TAPS * group_width, width), lambda step: (step, 0)),
        ],
        out_specs=pl.BlockSpec((rows, width), lambda step: (0, 0)),
        scratch_shapes=[
            pltpu.VMEM((PARTS + 1, long, part), jnp.float32),
            pltpu.VMEM((PARTS + 1, long - TAPS, TAPS * part), jnp.bfloat16),
            pltpu.VMEM((part, TAPS * part) if back else (TAPS * part, part), jnp.bfloat16),
            pltpu.VMEM((PARTS, rows, part), jnp.float32),
        ],
        compiler_params=pltpu.CompilerParams(vmem_limit_bytes=56 << 20),
        name="conv_back" if back else "conv",
    )(padded, padded_ids, weight)


CHUNKS = 8


def taps_grad_kernel(
    clips, halo, input_ref, grad_ref, input_ids_ref, grad_ids_ref, out_ref,
    inputs, grads, spaced_inputs, spaced_grads, input_cols, grad_cols,
):
    half = KERNEL // 2
    group_width = inputs.shape[1]

    def unpack(packed_ref, target):
        blocks, rows, _ = packed_ref.shape

        def one(block, carry):
            tile = packed_ref[block]
            for chunk in range(CHUNKS):
                row = pl.multiple_of((block * CHUNKS + chunk) * rows, rows)
                target[pl.ds(row, rows), :] = tile[:, chunk * group_width : (chunk + 1) * group_width]
            return carry

        lax.fori_loop(0, blocks, one, 0)

    unpack(input_ref, inputs)
    unpack(grad_ref, grads)
    spaced_inputs[...] = jnp.zeros_like(spaced_inputs)
    spaced_grads[...] = jnp.zeros_like(spaced_grads)
    input_rows, grad_rows = inputs.shape[0], grads.shape[0]
    halo_rows = (input_rows - grad_rows) // 2

    def place(clip, carry):
        at = pl.multiple_of(half + half * clip, half)
        number = clip.astype(jnp.float32)
        spaced_inputs[pl.ds(at, input_rows), :] += jnp.where(
            input_ids_ref[...] == number, inputs[...].astype(jnp.float32), 0.0
        )
        spaced_grads[pl.ds(at + halo_rows, grad_rows), :] += jnp.where(
            grad_ids_ref[...] == number, grads[...].astype(jnp.float32), 0.0
        )
        return carry

    lax.fori_loop(0, clips, place, 0)
    origin = half + halo_rows
    span = input_cols.shape[0]
    spaced = spaced_grads[...]
    for tap in range(TAPS):
        moved = pltpu.roll(spaced, tap, 0) if tap else spaced
        grad_cols[:, tap * group_width : (tap + 1) * group_width] = moved[
            origin : origin + span
        ].astype(jnp.bfloat16)
    for turn in range(KERNEL // TAPS):
        begin = origin - half + turn * TAPS
        input_cols[:, turn * group_width : (turn + 1) * group_width] = spaced_inputs[
            begin : begin + span, :
        ].astype(jnp.bfloat16)
    result = over_rows_dot(input_cols[...], grad_cols[...]).astype(jnp.bfloat16)
    for place_at in range(2 * KERNEL // TAPS):
        turn, side = place_at // 2, place_at % 2
        out_ref[place_at] = result[
            turn * group_width : (turn + 1) * group_width,
            side * CHUNKS * group_width : (side + 1) * CHUNKS * group_width,
        ]


def taps_grad(inputs, grads, input_ids, grad_ids, clips, halo, group_width):
    _, rows, lanes = grads.shape
    half = KERNEL // 2
    grad_rows = grad_ids.shape[0]
    input_rows = input_ids.shape[0]
    long = input_rows + half * clips + KERNEL + (input_rows - grad_rows) // 2
    span = grad_rows + half * clips
    return pl.pallas_call(
        functools.partial(taps_grad_kernel, clips, halo),
        out_shape=jax.ShapeDtypeStruct((2 * KERNEL // TAPS, group_width, lanes), jnp.bfloat16),
        in_specs=[VMEM_WHOLE] * 4,
        out_specs=VMEM_WHOLE,
        scratch_shapes=[
            pltpu.VMEM((input_rows, group_width), jnp.bfloat16),
            pltpu.VMEM((grad_rows, group_width), jnp.bfloat16),
            pltpu.VMEM((long, group_width), jnp.float32),
            pltpu.VMEM((long, group_width), jnp.float32),
            pltpu.VMEM((span, KERNEL // TAPS * group_width), jnp.bfloat16),
            pltpu.VMEM((span, TAPS * group_width), jnp.bfloat16),
        ],
        compiler_params=pltpu.CompilerParams(vmem_limit_bytes=60 << 20),
        name="taps_grad",
    )(inputs, grads, input_ids, grad_ids)


def from_behind(value, axis, steps):
    count = lax.axis_size(axis)
    initial, last = (max(0, -steps), min(count, count - steps))
    return lax.ppermute(value, axis, [(source, source + steps) for source in range(initial, last)])


def padded_2(value, width):
    length = value.shape[0]
    before = from_behind(value[length - width :], "seq", 1)
    after = from_behind(value[:width], "seq", -1)
    return jnp.concatenate([before, value, after], axis=0)


def norm_rows(values, scales, shifts):
    center = values - jnp.mean(values, axis=-1, keepdims=True)
    spread = jnp.mean(center * center, axis=-1, keepdims=True)
    return center * lax.rsqrt(spread + 1e-05) * scales + shifts


def gelu_exact(values):
    return jax.nn.gelu(values, approximate=False)


def clip_span(ends, begin, count, total):
    places = begin + jnp.arange(count, dtype=jnp.int32)
    found = jnp.sum((places[:, None] >= ends[None, :]).astype(jnp.int32), axis=1)
    inside = jnp.logical_and(places >= 0, places < total)
    return jnp.where(inside, found, -1)


def near_groups():
    size = lax.axis_size("seq")
    return [[base + i for i in range(RING)] for base in range(0, size, RING)]


def swap(value):
    groups = None if lax.axis_size("seq") == RING else near_groups()
    return lax.all_to_all(value, "seq", 0, 0, axis_index_groups=groups)


def with_far_blocks(value, count):
    if lax.axis_size("seq") == RING or count == 0:
        return value
    before = from_behind(value[value.shape[0] - count :], "seq", RING)
    after = from_behind(value[:count], "seq", -RING)
    return jnp.concatenate([before, value, after], axis=0)


def fold_far_blocks(value, count):
    if lax.axis_size("seq") == RING or count == 0:
        return value
    own = value[count : value.shape[0] - count]
    to_before = from_behind(value[:count], "seq", -RING)
    to_after = from_behind(value[value.shape[0] - count :], "seq", RING)
    wide = own.astype(jnp.float32)
    wide = wide.at[wide.shape[0] - count :].add(to_before.astype(jnp.float32))
    wide = wide.at[:count].add(to_after.astype(jnp.float32))
    return wide.astype(value.dtype)


def pack_halves(parts):
    frames, heads, _ = parts[0].shape
    joined = jnp.concatenate(parts, axis=2)
    lanes = joined.shape[2]
    moved = joined.reshape(2, frames // 2, heads, lanes).transpose(2, 1, 0, 3)
    moved = moved.reshape(heads, frames // 2, 2 * lanes)
    return jnp.pad(moved, ((0, RING - heads), (0, 0), (0, 0)))


def unpack_halves(packed, heads, count):
    half = packed.shape[1]
    lanes = packed.shape[2] // (2 * count)
    parts = packed[:heads].reshape(heads, half, 2, count, lanes).transpose(2, 1, 3, 0, 4)
    return parts.reshape(2 * half, count * heads * lanes)


def pack_groups(value):
    frames, width = value.shape
    group_width = width // GROUPS
    moved = value.reshape(CHUNKS, frames // CHUNKS, GROUPS, group_width).transpose(2, 1, 0, 3)
    return moved.reshape(GROUPS, frames // CHUNKS, CHUNKS * group_width)


LANES = 256


def flat_share(grad, count):
    rows, columns = grad.shape
    share = grad.astype(jnp.bfloat16).reshape(count, rows // count, columns)
    return [share[:, :, at : at + LANES] for at in range(0, columns, LANES)]


def reduce_shares(grads, extra=None):
    count = lax.axis_size("seq")
    pieces, sizes = [], []
    for grad in grads:
        pieces += flat_share(grad, count)
        sizes.append((grad.shape[0] // count, grad.shape[1]))
    if extra is not None:
        pieces.append(extra.astype(jnp.bfloat16))
    share = lax.psum_scatter(
        jnp.concatenate(pieces, axis=1), "seq", scatter_dimension=0, tiled=False
    ).astype(jnp.bfloat16)
    total = sum_pair(share)
    out, at = [], 0
    for rows, columns in sizes:
        parts = []
        for _ in range(columns // LANES):
            parts.append(total[at : at + rows])
            at += rows
        out.append(jnp.concatenate(parts, axis=1))
    if extra is not None:
        out.append(total[at:])
    return out


def sum_pair(share):
    count = lax.axis_size("rep")
    total = share.astype(jnp.float32)
    if count == 2:
        other = lax.ppermute(share, "rep", [(0, 1), (1, 0)])
        return total + other.astype(jnp.float32)
    return lax.psum(share, "rep").astype(jnp.float32)


def local(
    samples,
    clip_lengths,
    stem_weight,
    stem_gain,
    stem_bias,
    proj_weight,
    pos_weight,
    norm_gains,
    biases,
    attn_in,
    attn_out,
    ffn_in,
    ffn_in_bias,
    ffn_out,
    out_grad,
):
    rows_dev = out_grad.shape[1]
    width = attn_out.shape[0]
    chans = stem_weight.shape[1]
    group_width = width // GROUPS
    count = lax.axis_size("seq")
    place = lax.axis_index("seq")
    total = rows_dev * count
    begin = place * rows_dev
    ends = jnp.cumsum(clip_lengths[0])
    clips = ends.shape[0]
    own_ids = clip_span(ends, begin, rows_dev, total)
    half = KERNEL // 2
    frames = samples[0].reshape(rows_dev, 2 * chans)
    next_row = from_behind(frames[:1, :chans], "seq", -1)
    same_next = clip_span(ends, begin + 1, rows_dev, total) == own_ids
    following = jnp.concatenate([frames[1:, :chans], next_row], axis=0)
    following = jnp.where(same_next[:, None], following, jnp.zeros_like(following))
    unfold = jnp.concatenate([frames, following], axis=1)
    stem_pre = plain_dot(unfold, stem_weight)
    feature = gelu_exact(stem_pre)
    normed_b = norm_rows(feature, stem_gain, stem_bias).astype(jnp.bfloat16)
    start_x = plain_dot(normed_b, proj_weight) + biases[:, 0]
    start_b = start_x.astype(jnp.bfloat16)
    padded = padded_2(start_b, half)
    padded_ids = clip_span(ends, begin - half, rows_dev + 2 * half, total)
    padded_ids = padded_ids.astype(jnp.float32)[:, None]
    start_groups = swap(pack_groups(start_b))
    conv_out = conv_rows(False, padded, padded_ids, pos_weight) + biases[:, 1]
    mixed = start_x + gelu_exact(conv_out)
    hidden = norm_rows(mixed, norm_gains[:, 0], biases[:, 2])
    hidden_b = hidden.astype(jnp.bfloat16)
    project = plain_dot(hidden_b, attn_in)
    query_b = (project[:, :width] + biases[:, 3]).astype(jnp.bfloat16)
    keys_b = project[:, width : 2 * width].astype(jnp.bfloat16)
    values_b = (project[:, 2 * width :] + biases[:, 4]).astype(jnp.bfloat16)
    by_head = [piece.reshape(rows_dev, HEADS, HEAD_DIM) for piece in (query_b, keys_b, values_b)]

    segment = RING * rows_dev
    far = 0 if count == RING else -(-MAXLEN // rows_dev)
    segment_begin = (place // RING) * segment
    key_begin = segment_begin - far * rows_dev
    query_ids = clip_span(ends, segment_begin, segment, total)
    key_ids = clip_span(ends, key_begin, segment + 2 * far * rows_dev, total)
    firsts = segment_begin + Q_TILE * jnp.arange(segment // Q_TILE, dtype=jnp.int32)
    lasts = firsts + (Q_TILE - 1)
    low = jnp.max(jnp.where(ends[None] <= firsts[:, None], ends[None], 0), axis=1)
    high = jnp.min(jnp.where(ends[None] > lasts[:, None], ends[None], total), axis=1)
    low = (low - key_begin) // K_TILE
    high = (high - key_begin + (K_TILE - 1)) // K_TILE
    high = jnp.where(place % RING < HEADS, high, low)
    packed = with_far_blocks(swap(pack_halves(by_head)), far)
    attended_heads, wide, log_total = attend(
        low, high, packed, query_ids[:, None], key_ids[None, :], far
    )
    attended_b = unpack_halves(swap(attended_heads), HEADS, 1)
    pre_second = hidden + plain_dot(attended_b, attn_out) + biases[:, 5]
    second = norm_rows(pre_second, norm_gains[:, 1], biases[:, 6])
    second_b = second.astype(jnp.bfloat16)
    inner = plain_dot(second_b, ffn_in) + ffn_in_bias
    inner_b = gelu_exact(inner).astype(jnp.bfloat16)
    pre_last = second + plain_dot(inner_b, ffn_out) + biases[:, 7]
    layer_out = norm_rows(pre_last, norm_gains[:, 2], biases[:, 8]).astype(jnp.bfloat16)[None]
    grad_last, gain_grad_c, bias_grad_c = jax.vjp(
        norm_rows, pre_last, norm_gains[:, 2], biases[:, 8]
    )[1](out_grad[0].astype(jnp.float32))
    grad_last_b = grad_last.astype(jnp.bfloat16)
    grad_ffn_out = over_rows_dot(inner_b, grad_last_b)
    grad_inner = jax.vjp(gelu_exact, inner)[1](row_dot(grad_last_b, ffn_out))[0]
    grad_inner_b = grad_inner.astype(jnp.bfloat16)
    grad_ffn_in = over_rows_dot(second_b, grad_inner_b)
    ffn_grads = reduce_shares([grad_ffn_in, grad_ffn_out])
    grad_second = grad_last + row_dot(grad_inner_b, ffn_in)
    grad_pre_second, gain_grad_b, bias_grad_b = jax.vjp(
        norm_rows, pre_second, norm_gains[:, 1], biases[:, 6]
    )[1](grad_second)
    grad_branch_b = grad_pre_second.astype(jnp.bfloat16)
    grad_attn_out = over_rows_dot(attended_b, grad_branch_b)
    grad_out = row_dot(grad_branch_b, attn_out).astype(jnp.bfloat16)
    grad_heads = swap(pack_halves([grad_out.reshape(rows_dev, HEADS, HEAD_DIM)]))
    packed_grad = attend_back(
        low, high, packed, grad_heads, wide, log_total, query_ids[:, None], key_ids[None, :], far
    )
    grad_project_b = unpack_halves(swap(fold_far_blocks(packed_grad, far)), HEADS, 3)
    grad_attn_in = over_rows_dot(hidden_b, grad_project_b)
    attn_grads = reduce_shares([grad_attn_in, grad_attn_out])
    grad_hidden = grad_pre_second + row_dot(grad_project_b, attn_in)
    grad_mixed, gain_grad_a, bias_grad_a = jax.vjp(
        norm_rows, mixed, norm_gains[:, 0], biases[:, 2]
    )[1](grad_hidden)
    grad_conv = jax.vjp(gelu_exact, conv_out)[1](grad_mixed)[0]
    grad_conv_b = grad_conv.astype(jnp.bfloat16)
    padded_grad = padded_2(grad_conv_b, half)
    grad_groups = swap(pack_groups(grad_conv_b))
    input_grad = conv_rows(True, padded_grad, padded_ids, pos_weight)

    near = 0 if count == RING else 1
    first_clip = query_ids[0]
    input_ids = clip_span(ends, segment_begin - near * rows_dev, segment + 2 * near * rows_dev, total)
    taps = taps_grad(
        with_far_blocks(start_groups, near),
        grad_groups,
        (input_ids - first_clip).astype(jnp.float32)[:, None],
        (query_ids - first_clip).astype(jnp.float32)[:, None],
        clips,
        near,
        group_width,
    )
    own_taps = KERNEL // count
    if count == RING:
        pos_pieces = swap(taps)
    else:
        segments = count // RING
        by_tap = taps.reshape(2 * KERNEL // TAPS, group_width, CHUNKS, group_width)
        by_tap = by_tap.transpose(0, 2, 1, 3).reshape(segments, -1, LANES)
        across = [[low_at + RING * j for j in range(segments)] for low_at in range(RING)]
        by_tap = lax.all_to_all(by_tap, "seq", 0, 0, axis_index_groups=across)
        by_tap = jnp.sum(by_tap.astype(jnp.float32), axis=0).astype(jnp.bfloat16)
        by_tap = by_tap.reshape(RING, own_taps, group_width, group_width).transpose(0, 2, 1, 3)
        pos_pieces = swap(by_tap.reshape(RING, group_width, own_taps * group_width))
    pos_total = sum_pair(pos_pieces).reshape(GROUPS, group_width, own_taps, group_width)
    pos_grad = pos_total.transpose(2, 1, 0, 3).reshape(own_taps * group_width, width)

    grad_start = grad_mixed + input_grad
    grad_start_b = grad_start.astype(jnp.bfloat16)
    grad_proj = over_rows_dot(normed_b, grad_start_b)
    grad_feature, stem_gain_grad, stem_bias_grad = jax.vjp(
        norm_rows, feature, stem_gain, stem_bias
    )[1](row_dot(grad_start_b, proj_weight))
    grad_pre_b = jax.vjp(gelu_exact, stem_pre)[1](grad_feature)[0].astype(jnp.bfloat16)
    grad_stem = over_rows_dot(unfold, grad_pre_b)
    grad_unfold = row_dot(grad_pre_b, stem_weight)
    grad_follow = jnp.where(same_next[:, None], grad_unfold[:, 2 * chans :], 0.0)
    carried = from_behind(grad_follow[-1:], "seq", 1)
    shifted_back = jnp.concatenate([carried, grad_follow[:-1]], axis=0)
    grad_frames = grad_unfold[:, : 2 * chans] + jnp.concatenate(
        [shifted_back, jnp.zeros((rows_dev, chans), jnp.float32)], axis=1
    )
    sample_grad = grad_frames.reshape(1, 2 * rows_dev, chans)

    gains_grad = jnp.stack([gain_grad_a, gain_grad_b, gain_grad_c], axis=0)
    project_sums = jnp.sum(grad_project_b.astype(jnp.float32), axis=0)
    bias_table = jnp.stack(
        [
            jnp.sum(grad_start, axis=0),
            jnp.sum(grad_conv, axis=0),
            bias_grad_a,
            project_sums[:width],
            project_sums[2 * width :],
            jnp.sum(grad_pre_second, axis=0),
            bias_grad_b,
            jnp.sum(grad_last, axis=0),
            bias_grad_c,
        ],
        axis=0,
    )
    inner_bias_grad = jnp.sum(grad_inner, axis=0)
    small = jnp.concatenate(
        [
            jnp.concatenate([gains_grad, bias_table], axis=0)
            .reshape(12, count, width // count)
            .transpose(1, 0, 2)
            .reshape(count, -1),
            inner_bias_grad.reshape(count, -1),
            stem_gain_grad.reshape(count, -1),
            stem_bias_grad.reshape(count, -1),
        ],
        axis=1,
    )
    length = small.shape[1]
    small = jnp.pad(small, ((0, 0), (0, -length % LANES))).reshape(count, -1, LANES)
    grad_proj_sum, grad_stem_sum, small_sum = reduce_shares([grad_proj, grad_stem], small)
    flat = small_sum.reshape(-1)
    own = width // count
    table = flat[: 12 * own].reshape(12, own)
    at = 12 * own
    own_inner = inner_bias_grad.shape[0] // count
    own_chans = chans // count
    inner_sum = flat[at : at + own_inner]
    at += own_inner
    return (
        layer_out,
        sample_grad,
        grad_stem_sum,
        flat[at : at + own_chans],
        flat[at + own_chans : at + 2 * own_chans],
        grad_proj_sum,
        pos_grad,
        table[:3].T,
        table[3:].T,
        attn_grads[0],
        attn_grads[1],
        ffn_grads[0],
        inner_sum,
        ffn_grads[1],
    )


def solution(mesh):
    streams = P("rep", "seq", None)
    rows = P("seq", None)
    return jax.shard_map(
        local,
        mesh=mesh,
        in_specs=(streams, P("rep", None)) + (P(),) * 12 + (streams,),
        out_specs=(streams, streams, rows, P("seq"), P("seq"))
        + (rows,) * 7
        + (P("seq"), rows),
        check_vma=False,
    )
```

```python
import functools

import jax
import jax.numpy as jnp
from jax import lax
from jax.experimental import pallas as pl
from jax.experimental.pallas import tpu as pltpu
from jax.sharding import PartitionSpec as P

HEADS = 12
KERNEL = 128
GROUPS = 16
MAXLEN = 1536
RING = 16

def row_dot(left, right):
    return lax.dot_general(left, right, (((1,), (1,)), ((), ())), preferred_element_type=jnp.float32)


def plain_dot(left, right):
    return lax.dot_general(left, right, (((1,), (0,)), ((), ())), preferred_element_type=jnp.float32)


def over_rows_dot(left, right):
    return lax.dot_general(left, right, (((0,), (0,)), ((), ())), preferred_element_type=jnp.float32)


VMEM_WHOLE = pl.BlockSpec(memory_space=pltpu.VMEM)
SMEM_WHOLE = pl.BlockSpec(memory_space=pltpu.SMEM)
HEAD_DIM = 64
Q_TILE = 512
K_TILE = 512
LOW = -1e30


def unpack_heads(packed_ref, targets, factor):
    blocks, half, lanes = packed_ref.shape
    share = lanes // 2

    def one(block, carry):
        tile = packed_ref[block]
        for side in range(2):
            row = pl.multiple_of(block * 2 * half + side * half, half)
            for place, target in enumerate(targets):
                begin = side * share + place * HEAD_DIM
                piece = tile[:, begin : begin + HEAD_DIM]
                if place == 0 and factor != 1.0:
                    piece = piece * jnp.bfloat16(factor)
                target[pl.ds(row, half), :] = piece
        return carry

    lax.fori_loop(0, blocks, one, 0)


def attend_kernel(
    halo, low_ref, high_ref, packed_ref, query_ids_ref, key_ids_ref, out_ref, wide_ref, log_ref,
    query, keys, values,
):
    scale = HEAD_DIM ** (-0.5)
    unpack_heads(packed_ref, (query, keys, values), scale)
    rows = query_ids_ref.shape[0]
    half = packed_ref.shape[1]
    block = 2 * half

    def query_tile(index, carry):
        first = pl.multiple_of(index * Q_TILE, Q_TILE)
        q = query[pl.ds(halo * block + first, Q_TILE), :]
        q_ids = query_ids_ref[pl.ds(first, Q_TILE), :]

        def key_tile(at, state):
            top, mass, total = state
            column = pl.multiple_of(at * K_TILE, K_TILE)
            scores = row_dot(q, keys[pl.ds(column, K_TILE), :])
            scores = jnp.where(q_ids == key_ids_ref[:, pl.ds(column, K_TILE)], scores, LOW)
            new_top = jnp.maximum(top, jnp.max(scores, axis=1, keepdims=True))
            weight = jnp.exp(scores - new_top)
            fade = jnp.exp(top - new_top)
            mass = fade * mass + jnp.sum(weight, axis=1, keepdims=True)
            total = fade * total + plain_dot(
                weight.astype(jnp.bfloat16), values[pl.ds(column, K_TILE), :]
            )
            return new_top, mass, total

        top, mass, total = lax.fori_loop(
            low_ref[index],
            high_ref[index],
            key_tile,
            (
                jnp.full((Q_TILE, 1), 0.5 * LOW, jnp.float32),
                jnp.zeros((Q_TILE, 1), jnp.float32),
                jnp.zeros((Q_TILE, HEAD_DIM), jnp.float32),
            ),
        )
        mass = jnp.maximum(mass, 1e-37)
        attended = total / mass
        wide_ref[pl.ds(first, Q_TILE), :] = attended
        log_ref[pl.ds(first, Q_TILE), :] = top + jnp.log(mass)
        narrow = attended.astype(jnp.bfloat16)
        for inner in range(Q_TILE // block):
            spot = index * (Q_TILE // block) + inner
            out_ref[spot, :, 0:HEAD_DIM] = narrow[inner * block : inner * block + half]
            out_ref[spot, :, HEAD_DIM:] = narrow[inner * block + half : (inner + 1) * block]
        return carry

    lax.fori_loop(0, rows // Q_TILE, query_tile, 0)


def attend(low, high, packed, query_ids, key_ids, halo):
    blocks, half, _ = packed.shape
    rows = query_ids.shape[0]
    key_rows = blocks * 2 * half
    return pl.pallas_call(
        functools.partial(attend_kernel, halo),
        out_shape=(
            jax.ShapeDtypeStruct((blocks - 2 * halo, half, 2 * HEAD_DIM), jnp.bfloat16),
            jax.ShapeDtypeStruct((rows, HEAD_DIM), jnp.float32),
            jax.ShapeDtypeStruct((rows, 1), jnp.float32),
        ),
        in_specs=[SMEM_WHOLE] * 2 + [VMEM_WHOLE] * 3,
        out_specs=(VMEM_WHOLE,) * 3,
        scratch_shapes=[pltpu.VMEM((key_rows, HEAD_DIM), jnp.bfloat16)] * 3,
        compiler_params=pltpu.CompilerParams(vmem_limit_bytes=56 << 20),
        name="attend",
    )(low, high, packed, query_ids, key_ids)


def attend_back_kernel(
    halo, low_ref, high_ref, packed_ref, grad_ref, wide_ref, log_ref, query_ids_ref, key_ids_ref,
    out_ref, query, keys, values, grads, key_grads, value_grads,
):
    scale = HEAD_DIM ** (-0.5)
    unpack_heads(packed_ref, (query, keys, values), scale)
    unpack_heads(grad_ref, (grads,), 1.0)
    blocks, half, _ = packed_ref.shape
    rows = query_ids_ref.shape[0]
    block = 2 * half
    key_grads[...] = jnp.zeros_like(key_grads)
    value_grads[...] = jnp.zeros_like(value_grads)
    if halo:
        out_ref[...] = jnp.zeros_like(out_ref)

    def query_tile(index, carry):
        first = pl.multiple_of(index * Q_TILE, Q_TILE)
        q = query[pl.ds(halo * block + first, Q_TILE), :]
        g = grads[pl.ds(first, Q_TILE), :]
        q_ids = query_ids_ref[pl.ds(first, Q_TILE), :]
        log_total = log_ref[pl.ds(first, Q_TILE), :]
        delta = jnp.sum(
            g.astype(jnp.float32) * wide_ref[pl.ds(first, Q_TILE), :], axis=1, keepdims=True
        )

        def key_tile(at, running):
            column = pl.multiple_of(at * K_TILE, K_TILE)
            k = keys[pl.ds(column, K_TILE), :]
            v = values[pl.ds(column, K_TILE), :]
            probs = jnp.where(
                q_ids == key_ids_ref[:, pl.ds(column, K_TILE)],
                jnp.exp(row_dot(q, k) - log_total),
                0.0,
            )
            prob_grad = row_dot(g, v)
            score_grad = (probs * (prob_grad - delta) * scale).astype(jnp.bfloat16)
            value_grads[pl.ds(column, K_TILE), :] += over_rows_dot(probs.astype(jnp.bfloat16), g)
            key_grads[pl.ds(column, K_TILE), :] += over_rows_dot(score_grad, q)
            return running + plain_dot(score_grad, k)

        query_grad = lax.fori_loop(
            low_ref[index], high_ref[index], key_tile, jnp.zeros((Q_TILE, HEAD_DIM), jnp.float32)
        ).astype(jnp.bfloat16)
        for inner in range(Q_TILE // block):
            spot = halo + index * (Q_TILE // block) + inner
            out_ref[spot, :, 0:HEAD_DIM] = query_grad[inner * block : inner * block + half]
            out_ref[spot, :, 3 * HEAD_DIM : 4 * HEAD_DIM] = query_grad[
                inner * block + half : (inner + 1) * block
            ]
        return carry

    lax.fori_loop(0, rows // Q_TILE, query_tile, 0)

    def finish(spot, carry):
        for side in range(2):
            row = pl.multiple_of(spot * block + side * half, half)
            begin = (3 * side + 1) * HEAD_DIM
            out_ref[spot, :, begin : begin + HEAD_DIM] = (
                key_grads[pl.ds(row, half), :] * (1.0 / scale)
            ).astype(jnp.bfloat16)
            out_ref[spot, :, begin + HEAD_DIM : begin + 2 * HEAD_DIM] = value_grads[
                pl.ds(row, half), :
            ].astype(jnp.bfloat16)
        return carry

    lax.fori_loop(0, blocks, finish, 0)


def attend_back(low, high, packed, grad, wide, log_total, query_ids, key_ids, halo):
    blocks, half, lanes = packed.shape
    rows = query_ids.shape[0]
    key_rows = blocks * 2 * half
    return pl.pallas_call(
        functools.partial(attend_back_kernel, halo),
        out_shape=jax.ShapeDtypeStruct((blocks, half, lanes), jnp.bfloat16),
        in_specs=[SMEM_WHOLE] * 2 + [VMEM_WHOLE] * 6,
        out_specs=VMEM_WHOLE,
        scratch_shapes=[pltpu.VMEM((key_rows, HEAD_DIM), jnp.bfloat16)] * 3
        + [pltpu.VMEM((rows, HEAD_DIM), jnp.bfloat16)]
        + [pltpu.VMEM((key_rows, HEAD_DIM), jnp.float32)] * 2,
        compiler_params=pltpu.CompilerParams(vmem_limit_bytes=60 << 20),
        name="attend_back",
    )(low, high, packed, grad, wide, log_total, query_ids, key_ids)

TAPS = 16
SHOT = 384


def conv_weights_kernel(back, weight_ref, out_ref):
    group_width = out_ref.shape[1]
    if back:
        for group in range(GROUPS):
            lanes = slice(group_width * group, group_width * (group + 1))
            out_ref[group] = jnp.concatenate(
                [weight_ref[group_width * tap : group_width * (tap + 1), lanes] for tap in range(TAPS)],
                axis=1,
            )
    else:
        turned = weight_ref[...].T
        for group in range(GROUPS):
            out_ref[group] = turned[group_width * group : group_width * (group + 1)]


def conv_weights(back, weight):
    rows, width = weight.shape
    group_width = width // GROUPS
    turns = KERNEL // TAPS
    return pl.pallas_call(
        functools.partial(conv_weights_kernel, back),
        grid=(turns,),
        out_shape=jax.ShapeDtypeStruct((GROUPS, turns * group_width, TAPS * group_width), weight.dtype),
        in_specs=[pl.BlockSpec((TAPS * group_width, width), lambda turn: (turn, 0))],
        out_specs=pl.BlockSpec((GROUPS, group_width, TAPS * group_width), lambda turn: (0, turn, 0)),
        cost_estimate=pl.CostEstimate(flops=0, bytes_accessed=4 * rows * width, transcendentals=0),
        name="conv_weights_back" if back else "conv_weights",
    )(weight)


def conv_kernel(back, rows_ref, ids_ref, weight_ref, out_ref, spaced, total):
    group = pl.program_id(0)
    long, width = rows_ref.shape
    rows = out_ref.shape[0]
    half = KERNEL // 2
    turns = KERNEL // TAPS
    group_width = width // GROUPS
    room = spaced.shape[1]
    own = ids_ref[:, half : half + rows]
    first = jnp.min(own)
    count = jnp.max(own) - first + 1

    @pl.when(group == 0)
    def _():
        turned = rows_ref[...].astype(jnp.float32).T
        ids = ids_ref[...]
        rest = jnp.zeros((width, room - long), jnp.float32)

        def of_clip(clip):
            return jnp.concatenate([jnp.where(ids == first + clip, turned, 0.0), rest], axis=1)

        spaced[...] = of_clip(0).astype(jnp.bfloat16)

        def place(clip, carry):
            spaced[...] += pltpu.roll(of_clip(clip), clip * half, 1).astype(jnp.bfloat16)
            return carry

        lax.fori_loop(1, count, place, 0)

    row = pl.multiple_of(group * group_width, group_width)
    shots = lax.div(rows + half * (count - 1) + SHOT - 1, SHOT)

    def shot(index, carry):
        base = pl.multiple_of(index * SHOT, 128)
        tile = spaced[pl.ds(row, group_width), pl.ds(base, SHOT + 2 * KERNEL)]
        moved = []
        for tap in range(TAPS):
            begin = TAPS - tap if back else tap
            moved.append(tile[:, begin : begin + SHOT + KERNEL])
        product = plain_dot(weight_ref[0], jnp.concatenate(moved, axis=0))
        result = None
        for turn in range(turns):
            begin = (turns - 1 - turn if back else turn) * TAPS
            piece = product[turn * group_width : (turn + 1) * group_width, begin : begin + SHOT]
            result = piece if result is None else result + piece
        total[pl.ds(row, group_width), pl.ds(base, SHOT)] = result
        return carry

    lax.fori_loop(0, shots, shot, 0)

    @pl.when(group == GROUPS - 1)
    def _():
        wide = total.shape[1]

        def collect(clip, carry):
            moved = pltpu.roll(total[...], lax.rem(wide - clip * half, wide), 1)[:, :rows]
            total[:, :rows] = jnp.where(own == first + clip, moved, total[:, :rows])
            return carry

        lax.fori_loop(1, count, collect, 0)
        out_ref[...] = total[:, :rows].T


def conv_rows(back, padded, padded_ids, weight, clips):
    long, width = padded.shape
    rows = long - KERNEL
    shots = -(-(rows + KERNEL // 2 * (clips - 1)) // SHOT)
    return pl.pallas_call(
        functools.partial(conv_kernel, back),
        grid=(GROUPS,),
        out_shape=jax.ShapeDtypeStruct((rows, width), jnp.float32),
        in_specs=[
            pl.BlockSpec((long, width), lambda group: (0, 0)),
            pl.BlockSpec((1, long), lambda group: (0, 0)),
            pl.BlockSpec((1,) + weight.shape[1:], lambda group: (group, 0, 0)),
        ],
        out_specs=pl.BlockSpec((rows, width), lambda group: (0, 0)),
        scratch_shapes=[
            pltpu.VMEM((width, SHOT * shots + 2 * KERNEL), jnp.bfloat16),
            pltpu.VMEM((width, SHOT * shots), jnp.float32),
        ],
        compiler_params=pltpu.CompilerParams(vmem_limit_bytes=48 << 20),
        cost_estimate=pl.CostEstimate(
            flops=16 * 2 * 384 * 768 * 512, bytes_accessed=2 * weight.size, transcendentals=0
        ),
        name="conv_back" if back else "conv",
    )(padded, padded_ids, weight)


CHUNKS = 8
LANES = 256


def taps_grad_kernel(
    clips, halo, input_ref, grad_ref, input_ids_ref, grad_ids_ref, out_ref,
    inputs, grads, spaced_inputs, spaced_grads, input_cols, grad_cols,
):
    half = KERNEL // 2
    group_width = inputs.shape[1]

    def unpack(packed_ref, target):
        blocks, rows, _ = packed_ref.shape

        def one(block, carry):
            tile = packed_ref[block]
            for chunk in range(CHUNKS):
                row = pl.multiple_of((block * CHUNKS + chunk) * rows, rows)
                target[pl.ds(row, rows), :] = tile[:, chunk * group_width : (chunk + 1) * group_width]
            return carry

        lax.fori_loop(0, blocks, one, 0)

    unpack(input_ref, inputs)
    unpack(grad_ref, grads)
    spaced_inputs[...] = jnp.zeros_like(spaced_inputs)
    spaced_grads[...] = jnp.zeros_like(spaced_grads)
    input_rows, grad_rows = inputs.shape[0], grads.shape[0]
    halo_rows = (input_rows - grad_rows) // 2

    def place(clip, carry):
        at = pl.multiple_of(half + half * clip, half)
        number = clip.astype(jnp.float32)
        spaced_inputs[pl.ds(at, input_rows), :] += jnp.where(
            input_ids_ref[...] == number, inputs[...].astype(jnp.float32), 0.0
        )
        spaced_grads[pl.ds(at + halo_rows, grad_rows), :] += jnp.where(
            grad_ids_ref[...] == number, grads[...].astype(jnp.float32), 0.0
        )
        return carry

    lax.fori_loop(0, clips, place, 0)
    origin = half + halo_rows
    span = input_cols.shape[0]
    spaced = spaced_grads[...]
    for tap in range(TAPS):
        moved = pltpu.roll(spaced, tap, 0) if tap else spaced
        grad_cols[:, tap * group_width : (tap + 1) * group_width] = moved[
            origin : origin + span
        ].astype(jnp.bfloat16)
    for turn in range(KERNEL // TAPS):
        begin = origin - half + turn * TAPS
        input_cols[:, turn * group_width : (turn + 1) * group_width] = spaced_inputs[
            begin : begin + span, :
        ].astype(jnp.bfloat16)
    result = over_rows_dot(input_cols[...], grad_cols[...]).astype(jnp.bfloat16)
    for place_at in range(2 * KERNEL // TAPS):
        turn, side = place_at // 2, place_at % 2
        out_ref[place_at] = result[
            turn * group_width : (turn + 1) * group_width,
            side * CHUNKS * group_width : (side + 1) * CHUNKS * group_width,
        ]


def taps_grad(inputs, grads, input_ids, grad_ids, clips, halo, group_width):
    _, rows, lanes = grads.shape
    half = KERNEL // 2
    grad_rows = grad_ids.shape[0]
    input_rows = input_ids.shape[0]
    long = input_rows + half * clips + KERNEL + (input_rows - grad_rows) // 2
    span = grad_rows + half * clips
    return pl.pallas_call(
        functools.partial(taps_grad_kernel, clips, halo),
        out_shape=jax.ShapeDtypeStruct((2 * KERNEL // TAPS, group_width, lanes), jnp.bfloat16),
        in_specs=[VMEM_WHOLE] * 4,
        out_specs=VMEM_WHOLE,
        scratch_shapes=[
            pltpu.VMEM((input_rows, group_width), jnp.bfloat16),
            pltpu.VMEM((grad_rows, group_width), jnp.bfloat16),
            pltpu.VMEM((long, group_width), jnp.float32),
            pltpu.VMEM((long, group_width), jnp.float32),
            pltpu.VMEM((span, KERNEL // TAPS * group_width), jnp.bfloat16),
            pltpu.VMEM((span, TAPS * group_width), jnp.bfloat16),
        ],
        compiler_params=pltpu.CompilerParams(vmem_limit_bytes=60 << 20),
        name="taps_grad",
    )(inputs, grads, input_ids, grad_ids)

EPS = 1e-05
BF = jnp.bfloat16
SHARE = 384


def norm_parts(values):
    center = values - jnp.mean(values, axis=-1, keepdims=True)
    inverse = lax.rsqrt(jnp.mean(center * center, axis=-1, keepdims=True) + EPS)
    return center * inverse, inverse


def norm_back(unit, inverse, scales, grad):
    scaled = grad * scales
    back = inverse * (
        scaled
        - jnp.mean(scaled, axis=-1, keepdims=True)
        - unit * jnp.mean(scaled * unit, axis=-1, keepdims=True)
    )
    return back, row_sum(grad * unit), row_sum(grad)


def row_sum(values):
    return jnp.sum(values, axis=0, keepdims=True)


def gelu_both(values):
    below = 0.5 + 0.5 * lax.erf(values * 0.7071067811865476)
    bell = jnp.exp(-0.5 * values * values) * 0.3989422804014327
    return values * below, below + values * bell


def call(kernel, outs, scratch, args, name, flops, grid=None, in_specs=None, out_specs=None, limit=56):
    size = sum(a.size * a.dtype.itemsize for a in args)
    size += sum(o.size * o.dtype.itemsize for o in outs)
    extra = {} if grid is None else {"grid": grid}
    return pl.pallas_call(
        kernel,
        out_shape=tuple(outs),
        in_specs=in_specs or [VMEM_WHOLE] * len(args),
        out_specs=out_specs or (VMEM_WHOLE,) * len(outs),
        scratch_shapes=scratch,
        compiler_params=pltpu.CompilerParams(vmem_limit_bytes=limit << 20),
        cost_estimate=pl.CostEstimate(flops=flops, bytes_accessed=size, transcendentals=0),
        name=name,
        **extra,
    )(*args)


def like(shape, dtype=jnp.float32):
    return jax.ShapeDtypeStruct(shape, dtype)


def store_groups(values_b, out_ref):
    rows, width = values_b.shape
    group_width = width // GROUPS
    part = rows // CHUNKS
    for group in range(GROUPS):
        lanes = slice(group * group_width, (group + 1) * group_width)
        out_ref[group] = jnp.concatenate(
            [values_b[part * e : part * (e + 1), lanes] for e in range(CHUNKS)], axis=1
        )


def stem_kernel(
    frames_ref, next_ref, same_ref, weight_ref, gain_ref, bias_ref, proj_ref, gains_ref, biases_ref,
    start_ref, start_b_ref, groups_ref, pre_ref, normed_ref, follow_ref, table_ref,
):
    rows, chans = pre_ref.shape
    table_ref[0:3] = gains_ref[...].T
    table_ref[3:12] = biases_ref[...].T
    moved = pltpu.roll(frames_ref[:, :chans].astype(jnp.float32), rows - 1, 0)
    last = lax.broadcasted_iota(jnp.int32, (rows, 1), 0) == rows - 1
    moved = jnp.where(last, next_ref[...].astype(jnp.float32), moved)
    follow = jnp.where(same_ref[...] > 0.0, moved, 0.0).astype(BF)
    follow_ref[...] = follow
    pre = plain_dot(frames_ref[...], weight_ref[: 2 * chans]) + plain_dot(follow, weight_ref[2 * chans :])
    pre_ref[...] = pre
    unit, _ = norm_parts(gelu_both(pre)[0])
    normed = (unit * gain_ref[...] + bias_ref[...]).astype(BF)
    normed_ref[...] = normed
    start = plain_dot(normed, proj_ref[...]) + table_ref[3:4]
    start_ref[...] = start
    start_b = start.astype(BF)
    start_b_ref[...] = start_b
    store_groups(start_b, groups_ref)


def stem(frames, next_row, same_next, weight, gain, bias, proj, gains, biases):
    rows = frames.shape[0]
    chans, width = proj.shape
    part = rows // CHUNKS
    return call(
        stem_kernel,
        [
            like((rows, width)), like((rows, width), BF),
            like((GROUPS, part, CHUNKS * width // GROUPS), BF),
            like((rows, chans)), like((rows, chans), BF), like((rows, chans), BF), like((12, width)),
        ],
        [],
        (frames, next_row, same_next, weight, gain, bias, proj, gains, biases),
        "stem",
        6 * 10**9,
    )


def project_kernel(conv_ref, start_ref, table_ref, weight_ref, hidden_ref, packed_ref):
    rows, width = start_ref.shape
    half = rows // 2
    mixed = start_ref[...] + gelu_both(conv_ref[...] + table_ref[4:5])[0]
    unit, _ = norm_parts(mixed)
    hidden = unit * table_ref[0:1] + table_ref[5:6]
    hidden_ref[...] = hidden
    hidden_b = hidden.astype(BF)
    shifts = (table_ref[6:7], jnp.zeros((1, width), jnp.float32), table_ref[7:8])
    parts = [
        (plain_dot(hidden_b, weight_ref[:, at * width : (at + 1) * width]) + shift).astype(BF)
        for at, shift in enumerate(shifts)
    ]
    heads = width // HEAD_DIM
    for head in range(heads):
        lanes = slice(head * HEAD_DIM, (head + 1) * HEAD_DIM)
        packed_ref[head] = jnp.concatenate(
            [part[:half, lanes] for part in parts] + [part[half:, lanes] for part in parts], axis=1
        )
    for head in range(heads, RING):
        packed_ref[head] = jnp.zeros_like(packed_ref[head])


def project_heads(conv_sum, start, table, weight):
    rows, width = start.shape
    return call(
        project_kernel,
        [like((rows, width)), like((RING, rows // 2, 6 * HEAD_DIM), BF)],
        [],
        (conv_sum, start, table, weight),
        "project_heads",
        6 * 10**9,
    )


def middle_kernel(
    heads_ref, hidden_ref, table_ref, out_weight_ref, in_ref, in_bias_ref, back_ref, out_grad_ref,
    layer_ref, grad_heads_ref, grad_second_ref, out_part_ref, sums_ref, in_bias_grad_ref, joined_ref,
    attended, before, second, second_b, second_t, inner_b, slope, total, grad_last, grad_last_b,
    joined, sems,
):
    step = pl.program_id(0)
    rows, width = hidden_ref.shape
    half = rows // 2
    chunk = in_ref.shape[1]
    chunks = pl.num_programs(0) // 2
    heads = width // HEAD_DIM
    shares = joined_ref.shape[0]
    in_rows = width // shares
    back_rows = chunk * chunks // shares
    owners = chunk // back_rows

    def in_copy(at):
        place = (slice(None), pl.ds(pl.multiple_of(at * in_rows, 16), in_rows))
        return pltpu.make_async_copy(joined.at[place], joined_ref.at[place], sems.at[0, at])

    def back_copy(at):
        place = (pl.ds(at * owners, owners), pl.ds(in_rows * chunks, joined_ref.shape[1] - in_rows * chunks))
        return pltpu.make_async_copy(joined.at[place], joined_ref.at[place], sems.at[1, at])

    @pl.when(step == 0)
    def _():
        for head in range(heads):
            lanes = slice(head * HEAD_DIM, (head + 1) * HEAD_DIM)
            attended[:half, lanes] = heads_ref[head, :, :HEAD_DIM]
            attended[half:, lanes] = heads_ref[head, :, HEAD_DIM:]
        value = hidden_ref[...] + plain_dot(attended[...], out_weight_ref[...]) + table_ref[8:9]
        before[...] = value
        unit, _ = norm_parts(value)
        value = unit * table_ref[1:2] + table_ref[9:10]
        second[...] = value
        second_b[...] = value.astype(BF)
        second_t[...] = value.T.astype(BF)
        total[...] = jnp.zeros_like(total)

    @pl.when(step < chunks)
    def _():
        at = pl.multiple_of(step * chunk, chunk)
        value, back = gelu_both(plain_dot(second_b[...], in_ref[...]) + in_bias_ref[:, pl.ds(at, chunk)])
        value_b = value.astype(BF)
        inner_b[step] = value_b
        slope[step] = back
        total[...] += plain_dot(value_b, back_ref[...])

    @pl.when(step == chunks - 1)
    def _():
        unit, inverse = norm_parts(second[...] + total[...] + table_ref[10:11])
        layer_ref[...] = (unit * table_ref[2:3] + table_ref[11:12]).astype(BF)
        back, gain, bias = norm_back(unit, inverse, table_ref[2:3], out_grad_ref[...].astype(jnp.float32))
        grad_last[...] = back
        grad_last_b[...] = back.astype(BF)
        total[...] = back
        sums_ref[0:1] = gain
        sums_ref[1:2] = bias
        sums_ref[2:3] = row_sum(back)

    @pl.when(step >= chunks)
    def _():
        turn = step - chunks
        at = pl.multiple_of(turn * chunk, chunk)
        grad = row_dot(grad_last_b[...], back_ref[...]) * slope[turn]
        in_bias_grad_ref[:, pl.ds(at, chunk)] = row_sum(grad)
        grad_b = grad.astype(BF)
        total[...] += row_dot(grad_b, in_ref[...])
        product = plain_dot(second_t[...], grad_b).astype(BF)
        for share in range(shares):
            joined[share, pl.ds(pl.multiple_of(turn * in_rows, 16), in_rows), :] = product[
                share * in_rows : (share + 1) * in_rows
            ]
        in_copy(turn).start()
        product = over_rows_dot(inner_b[turn], grad_last_b[...]).astype(BF)
        for owner in range(owners):
            for place in range(width // SHARE):
                begin = in_rows * chunks + place * back_rows
                joined[turn * owners + owner, begin : begin + back_rows, :] = product[
                    owner * back_rows : (owner + 1) * back_rows, place * SHARE : (place + 1) * SHARE
                ]
        back_copy(turn).start()

    @pl.when(step == 2 * chunks - 1)
    def _():
        unit, inverse = norm_parts(before[...])
        back, gain, bias = norm_back(unit, inverse, table_ref[1:2], total[...])
        grad_second_ref[...] = back
        sums_ref[3:4] = row_sum(back)
        sums_ref[4:5] = gain
        sums_ref[5:6] = bias
        sums_ref[6:8] = jnp.zeros((2, width), jnp.float32)
        back_b = back.astype(BF)
        grads = row_dot(back_b, out_weight_ref[...]).astype(BF)
        for head in range(heads):
            lanes = slice(head * HEAD_DIM, (head + 1) * HEAD_DIM)
            grad_heads_ref[head] = jnp.concatenate([grads[:half, lanes], grads[half:, lanes]], axis=1)
        for head in range(heads, RING):
            grad_heads_ref[head] = jnp.zeros_like(grad_heads_ref[head])
        product = over_rows_dot(attended[...], back_b).astype(BF)
        for share in range(shares):
            for place in range(width // SHARE):
                out_part_ref[share, place * in_rows : (place + 1) * in_rows, :] = product[
                    share * in_rows : (share + 1) * in_rows, place * SHARE : (place + 1) * SHARE
                ]

        def finish(at, carry):
            in_copy(at).wait()
            back_copy(at).wait()
            return carry

        lax.fori_loop(0, chunks, finish, 0)


def middle(heads, hidden, table, out_weight, ffn_in, in_bias, ffn_out, out_grad, count):
    rows, width = hidden.shape
    inner = ffn_in.shape[1]
    chunk = SHARE
    chunks = inner // chunk
    own = lambda shape: pl.BlockSpec(shape, lambda step: (0,) * len(shape))
    outs = [
        like((rows, width), BF),
        like((RING, rows // 2, 2 * HEAD_DIM), BF),
        like((rows, width)),
        like((count, width // count * width // SHARE, SHARE), BF),
        like((8, width)),
        like((1, inner)),
        like((count, 2 * width // count * inner // SHARE, SHARE), BF),
    ]
    args = (heads, hidden, table, out_weight, ffn_in, in_bias, ffn_out, out_grad)
    in_specs = [own(a.shape) for a in args]
    in_specs[4] = pl.BlockSpec((width, chunk), lambda step: (0, step % chunks))
    in_specs[6] = pl.BlockSpec((chunk, width), lambda step: (step % chunks, 0))
    out_specs = [own(o.shape) for o in outs]
    out_specs[6] = pl.BlockSpec(memory_space=pl.ANY)
    scratch = [
        pltpu.VMEM((rows, width), BF),
        pltpu.VMEM((rows, width), jnp.float32),
        pltpu.VMEM((rows, width), jnp.float32),
        pltpu.VMEM((rows, width), BF),
        pltpu.VMEM((width, rows), BF),
        pltpu.VMEM((chunks, rows, chunk), BF),
        pltpu.VMEM((chunks, rows, chunk), jnp.float32),
        pltpu.VMEM((rows, width), jnp.float32),
        pltpu.VMEM((rows, width), jnp.float32),
        pltpu.VMEM((rows, width), BF),
        pltpu.VMEM(outs[6].shape, BF),
        pltpu.SemaphoreType.DMA((2, chunks)),
    ]
    return call(
        middle_kernel, outs, scratch, args, "middle", 2 * 10**10, (2 * chunks,), in_specs, tuple(out_specs)
    )


def after_heads_kernel(
    packed_ref, grad_second_ref, hidden_ref, conv_ref, start_ref, table_ref, weight_ref, out_part_ref,
    mixed_ref, conv_b_ref, groups_ref, joined_ref, sums_ref, grads,
):
    rows, width = hidden_ref.shape
    half = rows // 2
    heads = width // HEAD_DIM
    shares = joined_ref.shape[0]
    own_rows = width // shares
    for head in range(heads):
        tile = packed_ref[head]
        for part in range(3):
            lanes = slice(part * width + head * HEAD_DIM, part * width + (head + 1) * HEAD_DIM)
            grads[:half, lanes] = tile[:, part * HEAD_DIM : (part + 1) * HEAD_DIM]
            grads[half:, lanes] = tile[:, (part + 3) * HEAD_DIM : (part + 4) * HEAD_DIM]
    hidden_t = hidden_ref[...].T.astype(BF)
    blocks = 3 * width // SHARE
    for place in range(blocks):
        lanes = slice(place * SHARE, (place + 1) * SHARE)
        product = plain_dot(hidden_t, grads[:, lanes]).astype(BF)
        for share in range(shares):
            joined_ref[share, place * own_rows : (place + 1) * own_rows, :] = product[
                share * own_rows : (share + 1) * own_rows
            ]
    for share in range(shares):
        joined_ref[share, blocks * own_rows :, :] = out_part_ref[share]
    back = grad_second_ref[...] + row_dot(grads[...], weight_ref[...])
    value, slope = gelu_both(conv_ref[...] + table_ref[4:5])
    unit, inverse = norm_parts(start_ref[...] + value)
    mixed, gain, bias = norm_back(unit, inverse, table_ref[0:1], back)
    mixed_ref[...] = mixed
    conv = mixed * slope
    conv_b = conv.astype(BF)
    conv_b_ref[...] = conv_b
    store_groups(conv_b, groups_ref)
    sums_ref[0:1] = gain
    sums_ref[1:2] = bias
    sums_ref[2:3] = row_sum(conv)
    sums_ref[3:4] = row_sum(grads[:, :width].astype(jnp.float32))
    sums_ref[4:5] = row_sum(grads[:, 2 * width :].astype(jnp.float32))
    sums_ref[5:8] = jnp.zeros((3, width), jnp.float32)


def after_heads(packed, grad_second, hidden, conv_sum, start, table, weight, out_part):
    rows, width = hidden.shape
    shares = out_part.shape[0]
    return call(
        after_heads_kernel,
        [
            like((rows, width)), like((rows, width), BF),
            like((GROUPS, rows // CHUNKS, CHUNKS * width // GROUPS), BF),
            like((shares, out_part.shape[1] + width // shares * 3 * width // SHARE, SHARE), BF),
            like((8, width)),
        ],
        [pltpu.VMEM((rows, 3 * width), BF)],
        (packed, grad_second, hidden, conv_sum, start, table, weight, out_part),
        "after_heads",
        6 * 10**9,
    )


PIECE = 128


def stem_back_kernel(
    input_ref, mixed_ref, normed_ref, pre_ref, frames_ref, follow_ref, same_ref, weight_ref, gain_ref,
    proj_ref, middle_sums_ref, inner_sums_ref, after_sums_ref,
    samples_ref, carried_ref, joined_ref, table, spread, woven,
):
    rows, chans = pre_ref.shape
    width = input_ref.shape[1]
    shares = joined_ref.shape[0]
    start = mixed_ref[...] + input_ref[...]
    start_b = start.astype(BF)

    def share_out(product, begin):
        own, columns = product.shape[0] // shares, product.shape[1]
        for share in range(shares):
            for place in range(columns // PIECE):
                at = begin + place * own
                joined_ref[share, at : at + own, :] = product[
                    share * own : (share + 1) * own, place * PIECE : (place + 1) * PIECE
                ]
        return begin + own * columns // PIECE

    at = share_out(over_rows_dot(normed_ref[...], start_b).astype(BF), 0)
    value, slope = gelu_both(pre_ref[...])
    unit, inverse = norm_parts(value)
    feature, gain_sum, bias_sum = norm_back(
        unit, inverse, gain_ref[...], row_dot(start_b, proj_ref[...])
    )
    pre_b = (feature * slope).astype(BF)
    taps_t = jnp.concatenate(
        [
            over_rows_dot(frames_ref[:, :chans], pre_b),
            over_rows_dot(frames_ref[:, chans:], pre_b),
            over_rows_dot(follow_ref[...], pre_b),
        ],
        axis=0,
    ).astype(BF)
    at = share_out(taps_t, at)
    first = row_dot(pre_b, weight_ref[:chans])
    follow = jnp.where(same_ref[...] > 0.0, row_dot(pre_b, weight_ref[2 * chans :]), 0.0)
    carried_ref[...] = follow[rows - 1 :]
    moved = pltpu.roll(follow, 1, 0)
    top = lax.broadcasted_iota(jnp.int32, (rows, 1), 0) == 0
    even = first + jnp.where(top, 0.0, moved)
    odd = row_dot(pre_b, weight_ref[chans : 2 * chans])
    for lane in range(0, chans, PIECE):
        woven[pl.ds(0, rows, stride=2), :] = even[:, lane : lane + PIECE]
        woven[pl.ds(1, rows, stride=2), :] = odd[:, lane : lane + PIECE]
        samples_ref[:, lane : lane + PIECE] = woven[...]
    table[0:1] = after_sums_ref[0:1]
    table[1:2] = middle_sums_ref[4:5]
    table[2:3] = middle_sums_ref[0:1]
    table[3:4] = row_sum(start)
    table[4:5] = after_sums_ref[2:3]
    table[5:6] = after_sums_ref[1:2]
    table[6:7] = after_sums_ref[3:4]
    table[7:8] = after_sums_ref[4:5]
    table[8:9] = middle_sums_ref[3:4]
    table[9:10] = middle_sums_ref[5:6]
    table[10:11] = middle_sums_ref[2:3]
    table[11:12] = middle_sums_ref[1:2]
    spread[...] = jnp.zeros_like(spread)
    own, own_chans = width // shares, chans // shares
    own_inner = inner_sums_ref.shape[1] // shares
    for share in range(shares):
        spread[share, 0:12, 0:own] = table[:, share * own : (share + 1) * own]
        for place in range(-(-own_inner // PIECE)):
            length = min(PIECE, own_inner - place * PIECE)
            begin = share * own_inner + place * PIECE
            spread[share, 12 + place : 13 + place, 0:length] = inner_sums_ref[:, begin : begin + length]
        lanes = slice(share * own_chans, (share + 1) * own_chans)
        spread[share, 14:15, 0:own_chans] = gain_sum[:, lanes]
        spread[share, 15:16, 0:own_chans] = bias_sum[:, lanes]
        joined_ref[share, at:, :] = spread[share].astype(BF)


def stem_back(input_grad, mixed, normed, pre, frames, follow, same_next, weight, gain, proj, sums, shares):
    rows, chans = pre.shape
    width = input_grad.shape[1]
    pieces = (chans // shares * width + 3 * chans // shares * chans) // PIECE + 16
    return call(
        stem_back_kernel,
        [like((2 * rows, chans)), like((1, chans)), like((shares, pieces, PIECE), BF)],
        [pltpu.VMEM((12, width), jnp.float32), pltpu.VMEM((shares, 16, PIECE), jnp.float32),
         pltpu.VMEM((2 * rows, PIECE), jnp.float32)],
        (input_grad, mixed, normed, pre, frames, follow, same_next, weight, gain, proj) + sums,
        "stem_back",
        6 * 10**9,
    )


def from_behind(value, axis, steps):
    count = lax.axis_size(axis)
    initial, last = (max(0, -steps), min(count, count - steps))
    return lax.ppermute(value, axis, [(source, source + steps) for source in range(initial, last)])


def padded_2(value, width):
    length = value.shape[0]
    before = from_behind(value[length - width :], "seq", 1)
    after = from_behind(value[:width], "seq", -1)
    return jnp.concatenate([before, value, after], axis=0)


def clip_span(ends, begin, count, total):
    places = begin + jnp.arange(count, dtype=jnp.int32)
    found = jnp.sum((places[:, None] >= ends[None, :]).astype(jnp.int32), axis=1)
    inside = jnp.logical_and(places >= 0, places < total)
    return jnp.where(inside, found, -1)


def near_groups():
    size = lax.axis_size("seq")
    return [[base + i for i in range(RING)] for base in range(0, size, RING)]


def swap(value):
    groups = None if lax.axis_size("seq") == RING else near_groups()
    return lax.all_to_all(value, "seq", 0, 0, axis_index_groups=groups)


def with_far_blocks(value, count):
    if lax.axis_size("seq") == RING or count == 0:
        return value
    before = from_behind(value[value.shape[0] - count :], "seq", RING)
    after = from_behind(value[:count], "seq", -RING)
    return jnp.concatenate([before, value, after], axis=0)


def fold_far_blocks(value, count):
    if lax.axis_size("seq") == RING or count == 0:
        return value
    own = value[count : value.shape[0] - count]
    to_before = from_behind(value[:count], "seq", -RING)
    to_after = from_behind(value[value.shape[0] - count :], "seq", RING)
    wide = own.astype(jnp.float32)
    wide = wide.at[wide.shape[0] - count :].add(to_before.astype(jnp.float32))
    wide = wide.at[:count].add(to_after.astype(jnp.float32))
    return wide.astype(value.dtype)


def sum_pair(share):
    count = lax.axis_size("rep")
    if count == 2:
        other = lax.ppermute(share, "rep", [(0, 1), (1, 0)])
        return share.astype(jnp.float32) + other.astype(jnp.float32)
    return lax.psum(share, "rep").astype(jnp.float32)


def spread_out(total, sizes, lanes):
    out, at = [], 0
    for rows, columns in sizes:
        parts = []
        for _ in range(columns // lanes):
            parts.append(total[at : at + rows])
            at += rows
        out.append(jnp.concatenate(parts, axis=1))
    return out


def regroup(joined, blocks):
    count = lax.axis_size("seq")
    if count == RING:
        return joined
    parts = count // RING
    lanes = joined.shape[2]
    out, at = [], 0
    for number, rows in blocks:
        piece = joined[:, at : at + number * rows]
        at += number * rows
        piece = piece.reshape(RING, number, parts, rows // parts, lanes).transpose(0, 2, 1, 3, 4)
        out.append(piece.reshape(count, number * rows // parts, lanes))
    return jnp.concatenate(out, axis=1)


def regroup_small(small, widths):
    count = lax.axis_size("seq")
    if count == RING:
        return small
    parts = count // RING
    own, own_inner, own_chans = widths
    lanes = small.shape[2]
    table = small[:, :12, : own * parts].reshape(RING, 12, parts, own).transpose(0, 2, 1, 3)
    table = jnp.pad(table.reshape(count, 12, own), ((0, 0), (0, 0), (0, lanes - own)))
    wide = small[:, 12:14].reshape(RING, 2 * lanes)[:, : own_inner * parts].reshape(count, own_inner)
    wide = jnp.pad(wide, ((0, 0), (0, 2 * lanes - own_inner))).reshape(count, 2, lanes)
    stems = small[:, 14:16, : own_chans * parts].reshape(RING, 2, parts, own_chans).transpose(0, 2, 1, 3)
    stems = jnp.pad(stems.reshape(count, 2, own_chans), ((0, 0), (0, 0), (0, lanes - own_chans)))
    return jnp.concatenate([table, wide, stems], axis=1)


def over_seq(joined):
    return lax.psum_scatter(joined, "seq", scatter_dimension=0, tiled=False).astype(jnp.bfloat16)


def local(
    samples,
    clip_lengths,
    stem_weight,
    stem_gain,
    stem_bias,
    proj_weight,
    pos_weight,
    norm_gains,
    biases,
    attn_in,
    attn_out,
    ffn_in,
    ffn_in_bias,
    ffn_out,
    out_grad,
):
    rows_dev = out_grad.shape[1]
    width = attn_out.shape[0]
    chans = stem_weight.shape[1]
    inner = ffn_in.shape[1]
    group_width = width // GROUPS
    count = lax.axis_size("seq")
    place = lax.axis_index("seq")
    total = rows_dev * count
    begin = place * rows_dev
    ends = jnp.cumsum(clip_lengths[0])
    clips = ends.shape[0]
    half = KERNEL // 2
    padded_ids = clip_span(ends, begin - half, rows_dev + 2 * half, total)
    own_ids = padded_ids[half : half + rows_dev]
    same_next = (padded_ids[half + 1 : half + 1 + rows_dev] == own_ids).astype(jnp.float32)[:, None]
    frames = samples[0].reshape(rows_dev, 2 * chans)
    next_row = from_behind(samples[0, :1], "seq", -1)
    fore_weights = conv_weights(False, pos_weight)
    next_row, fore_weights = lax.optimization_barrier((next_row, fore_weights))
    start_x, start_b, start_packed, stem_pre, normed_b, follow, table = stem(
        frames, next_row, same_next, stem_weight, stem_gain[None], stem_bias[None], proj_weight,
        norm_gains, biases,
    )
    padded = padded_2(start_b, half)
    start_groups = swap(start_packed)
    conv_sum = conv_rows(False, padded, padded_ids[None], fore_weights, clips)
    conv_sum, start_groups = lax.optimization_barrier((conv_sum, start_groups))
    hidden, packed = project_heads(conv_sum, start_x, table, attn_in)

    segment = RING * rows_dev
    far = 0 if count == RING else -(-MAXLEN // rows_dev)
    segment_begin = (place // RING) * segment
    key_begin = segment_begin - far * rows_dev
    query_ids = clip_span(ends, segment_begin, segment, total)
    key_ids = clip_span(ends, key_begin, segment + 2 * far * rows_dev, total)
    firsts = segment_begin + Q_TILE * jnp.arange(segment // Q_TILE, dtype=jnp.int32)
    lasts = firsts + (Q_TILE - 1)
    low = jnp.max(jnp.where(ends[None] <= firsts[:, None], ends[None], 0), axis=1)
    high = jnp.min(jnp.where(ends[None] > lasts[:, None], ends[None], total), axis=1)
    low = (low - key_begin) // K_TILE
    high = (high - key_begin + (K_TILE - 1)) // K_TILE
    high = jnp.where(place % RING < HEADS, high, low)
    packed = with_far_blocks(swap(packed), far)
    back_weights = conv_weights(True, pos_weight)
    packed, back_weights = lax.optimization_barrier((packed, back_weights))
    attended_heads, wide, log_total = attend(
        low, high, packed, query_ids[:, None], key_ids[None, :], far
    )
    layer_out, grad_heads, grad_pre_second, out_part, middle_sums, inner_sums, ffn_joined = middle(
        swap(attended_heads), hidden, table, attn_out, ffn_in, ffn_in_bias[None], ffn_out, out_grad[0],
        RING,
    )
    near_rows, near_chans, near_inner = width // RING, chans // RING, inner // RING
    grad_heads = swap(grad_heads)
    ffn_share = over_seq(
        regroup(ffn_joined, [(inner // SHARE, near_rows), (width // SHARE, near_inner)])
    )
    packed_grad = attend_back(
        low, high, packed, grad_heads, wide, log_total, query_ids[:, None], key_ids[None, :], far
    )
    grad_mixed, grad_conv_b, grad_packed, attn_joined, after_sums = after_heads(
        swap(fold_far_blocks(packed_grad, far)), grad_pre_second, hidden, conv_sum, start_x, table,
        attn_in, out_part,
    )
    padded_grad = padded_2(grad_conv_b, half)
    grad_groups = swap(grad_packed)
    input_grad = conv_rows(True, padded_grad, padded_ids[None], back_weights, clips)
    input_grad, grad_groups, ffn_share = lax.optimization_barrier((input_grad, grad_groups, ffn_share))
    attn_share = over_seq(regroup(attn_joined, [(4 * width // SHARE, near_rows)]))
    sample_grad, carried, stem_joined = stem_back(
        input_grad, grad_mixed, normed_b, stem_pre, frames, follow, same_next, stem_weight,
        stem_gain[None], proj_weight, (middle_sums, inner_sums, after_sums), RING,
    )
    carried = from_behind(carried, "seq", 1)
    stem_joined, grad_groups = lax.optimization_barrier((stem_joined, grad_groups))

    near = 0 if count == RING else 1
    first_clip = query_ids[0]
    input_ids = clip_span(ends, segment_begin - near * rows_dev, segment + 2 * near * rows_dev, total)
    taps = taps_grad(
        with_far_blocks(start_groups, near),
        grad_groups,
        (input_ids - first_clip).astype(jnp.float32)[:, None],
        (query_ids - first_clip).astype(jnp.float32)[:, None],
        clips,
        near,
        group_width,
    )
    own_taps = KERNEL // count
    if count == RING:
        pos_pieces = swap(taps)
    else:
        segments = count // RING
        by_tap = taps.reshape(2 * KERNEL // TAPS, group_width, CHUNKS, group_width)
        by_tap = by_tap.transpose(0, 2, 1, 3).reshape(segments, -1, LANES)
        across = [[low_at + RING * j for j in range(segments)] for low_at in range(RING)]
        by_tap = lax.all_to_all(by_tap, "seq", 0, 0, axis_index_groups=across)
        by_tap = jnp.sum(by_tap.astype(jnp.float32), axis=0).astype(jnp.bfloat16)
        by_tap = by_tap.reshape(RING, own_taps, group_width, group_width).transpose(0, 2, 1, 3)
        pos_pieces = swap(by_tap.reshape(RING, group_width, own_taps * group_width))
    pos_total = sum_pair(pos_pieces).reshape(GROUPS, group_width, own_taps, group_width)
    pos_grad = pos_total.transpose(2, 1, 0, 3).reshape(own_taps * group_width, width)

    own = width // count
    own_chans = chans // count
    if count != RING:
        stem_joined = jnp.concatenate(
            [
                regroup(
                    stem_joined[:, :-16],
                    [(width // PIECE, near_chans), (chans // PIECE, 3 * near_chans)],
                ),
                regroup_small(stem_joined[:, -16:], (own, inner // count, own_chans)),
            ],
            axis=1,
        )
    received = lax.all_to_all(stem_joined, "seq", 0, 0)
    stem_total = sum_pair(jnp.sum(received.astype(jnp.float32), axis=0).astype(jnp.bfloat16))
    grad_proj, grad_stem = spread_out(
        stem_total[:-16], [(own_chans, width), (3 * own_chans, chans)], PIECE
    )
    small = stem_total[-16:]
    grad_ffn_in, grad_ffn_out = spread_out(
        sum_pair(ffn_share), [(own, inner), (inner // count, width)], SHARE
    )
    grad_attn_in, grad_attn_out = spread_out(
        sum_pair(attn_share), [(own, 3 * width), (own, width)], SHARE
    )
    sample_grad = sample_grad.at[:1].add(carried)
    return (
        layer_out[None],
        sample_grad[None],
        grad_stem,
        small[14, :own_chans],
        small[15, :own_chans],
        grad_proj,
        pos_grad,
        small[:3, :own].T,
        small[3:12, :own].T,
        grad_attn_in,
        grad_attn_out,
        grad_ffn_in,
        small[12:14].reshape(-1)[: inner // count],
        grad_ffn_out,
    )


def solution(mesh):
    streams = P("rep", "seq", None)
    rows = P("seq", None)
    return jax.shard_map(
        local,
        mesh=mesh,
        in_specs=(streams, P("rep", None)) + (P(),) * 12 + (streams,),
        out_specs=(streams, streams, rows, P("seq"), P("seq"))
        + (rows,) * 7
        + (P("seq"), rows),
        check_vma=False,
    )
```

```python
import functools

import jax
import jax.numpy as jnp
from jax import lax
from jax.experimental import pallas as pl
from jax.experimental.pallas import tpu as pltpu
from jax.sharding import PartitionSpec as P

HEADS = 12
KERNEL = 128
GROUPS = 16
MAXLEN = 1536
RING = 16
HEAD_DIM = 64
EPS = 1e-05
BF = jnp.bfloat16
VMEM_WHOLE = pl.BlockSpec(memory_space=pltpu.VMEM)
SMEM_WHOLE = pl.BlockSpec(memory_space=pltpu.SMEM)
TOTAL, BEGIN, SEGMENT, KEYS, ACTIVE, CORE = range(6)


def row_dot(left, right):
    return lax.dot_general(left, right, (((1,), (1,)), ((), ())), preferred_element_type=jnp.float32)


def plain_dot(left, right):
    return lax.dot_general(left, right, (((1,), (0,)), ((), ())), preferred_element_type=jnp.float32)


def over_rows_dot(left, right):
    return lax.dot_general(left, right, (((0,), (0,)), ((), ())), preferred_element_type=jnp.float32)


def pair_slot(shape, share, marks, clips):
    if shape[0] == 1:
        return 0, share
    return (marks[clips + CORE] if share % 2 == 0 else 1 - marks[clips + CORE]), share // 2


def over_clips(clips, step, state):
    if clips <= 8:
        for clip in range(clips):
            state = step(clip, state)
        return state
    return lax.fori_loop(0, clips, step, state)


def clip_bounds(marks, clips, places):
    def step(clip, state):
        first, end = state
        mark = marks[clip]
        return (
            jnp.maximum(first, jnp.where(mark <= places, mark, 0)),
            jnp.minimum(end, jnp.where(mark > places, mark, marks[clips + TOTAL])),
        )

    return over_clips(clips, step, (jnp.zeros_like(places), jnp.zeros_like(places) + marks[clips + TOTAL]))


def like(shape, dtype=jnp.float32):
    return jax.ShapeDtypeStruct(shape, dtype)


def call(kernel, outs, scratch, args, name, flops, grid=None, in_specs=None, out_specs=None, limit=56):
    size = sum(a.size * a.dtype.itemsize for a in args)
    size += sum(o.size * o.dtype.itemsize for o in outs)
    extra = {} if grid is None else {"grid": grid}
    return pl.pallas_call(
        kernel,
        out_shape=tuple(outs),
        in_specs=in_specs or [SMEM_WHOLE if a.dtype == jnp.int32 else VMEM_WHOLE for a in args],
        out_specs=out_specs or (VMEM_WHOLE,) * len(outs),
        scratch_shapes=scratch,
        compiler_params=pltpu.CompilerParams(vmem_limit_bytes=limit << 20),
        cost_estimate=pl.CostEstimate(flops=flops, bytes_accessed=size, transcendentals=0),
        name=name,
        **extra,
    )(*args)


Q_TILE = 512
K_TILE = 512
LOW = -1e30
LOG2E = 1.4426950408889634


def unpack_heads(packed_ref, targets):
    blocks, half, lanes = packed_ref.shape
    share = lanes // 2

    def one(block, carry):
        tile = packed_ref[block]
        turned = tile.T
        for side in range(2):
            row = pl.multiple_of(block * 2 * half + side * half, half)
            for place, (rows, columns) in enumerate(targets):
                begin = side * share + place * HEAD_DIM
                if rows is not None:
                    rows[pl.ds(row, half), :] = tile[:, begin : begin + HEAD_DIM]
                if columns is not None:
                    columns[0:HEAD_DIM, pl.ds(row, half)] = turned[begin : begin + HEAD_DIM]
        return carry

    lax.fori_loop(0, blocks, one, 0)


def tile_spans(marks, clips, index):
    first = marks[clips + SEGMENT] + index * Q_TILE
    begin = marks[clips + KEYS]
    low, low_end = clip_bounds(marks, clips, first)
    high_start, high = clip_bounds(marks, clips, first + Q_TILE - 1)
    low, low_end, high_start, high = (v - begin for v in (low, low_end, high_start, high))
    up = K_TILE - 1
    start = lax.div(low, K_TILE)
    stop = jnp.where(marks[clips + ACTIVE] > 0, lax.div(high + up, K_TILE), start)
    inner = lax.div(high_start + up, K_TILE)
    outer = lax.div(high, K_TILE)
    whole = (low == high_start) & (inner < outer) & (stop > start)
    inner = jnp.where(whole, inner, stop)
    outer = jnp.where(whole, outer, stop)
    places = first + lax.broadcasted_iota(jnp.int32, (1, Q_TILE), 1)
    starts, ends = clip_bounds(marks, clips, places)
    return (start, inner, outer, stop), starts - begin, ends - begin


def allowed(column, starts, ends):
    places = column + lax.broadcasted_iota(jnp.int32, (K_TILE, 1), 0)
    return (places >= starts) & (places < ends)


def over_spans(spans, step, state):
    for at in range(3):
        state = lax.fori_loop(spans[at], spans[at + 1], functools.partial(step, at != 1), state)
    return state


def attend_kernel(clips, halo, marks, packed_ref, out_ref, wide_ref, log_ref, query_t, keys, value_t):
    rows = wide_ref.shape[1]
    half = packed_ref.shape[1]
    block = 2 * half
    more = value_t.shape[0] - HEAD_DIM
    value_t[HEAD_DIM:] = jnp.where(
        lax.broadcasted_iota(jnp.int32, (more, value_t.shape[1]), 0) == 0, 1.0, 0.0
    ).astype(BF)
    unpack_heads(packed_ref, ((None, query_t), (keys, None), (None, value_t)))
    factor = HEAD_DIM ** (-0.5) * LOG2E

    def query_tile(index, carry):
        first = pl.multiple_of(index * Q_TILE, Q_TILE)
        q = query_t[:, pl.ds(halo * block + first, Q_TILE)]
        spans, starts, ends = tile_spans(marks, clips, index)

        def key_tile(masked, at, state):
            top, total = state
            column = pl.multiple_of(at * K_TILE, K_TILE)
            scores = plain_dot(keys[pl.ds(column, K_TILE), :], q) * factor
            if masked:
                scores = jnp.where(allowed(column, starts, ends), scores, LOW)
            new_top = jnp.maximum(top, jnp.max(scores, axis=0, keepdims=True))
            weight = jnp.exp2(scores - new_top).astype(BF)
            total = total * jnp.exp2(top - new_top) + plain_dot(
                value_t[:, pl.ds(column, K_TILE)], weight
            )
            return new_top, total

        top, total = over_spans(
            spans,
            key_tile,
            (
                jnp.full((1, Q_TILE), 0.5 * LOW, jnp.float32),
                jnp.zeros((HEAD_DIM + more, Q_TILE), jnp.float32),
            ),
        )
        mass = jnp.maximum(total[HEAD_DIM : HEAD_DIM + 1], 1e-37)
        attended = total[:HEAD_DIM] / mass
        wide_ref[:, pl.ds(first, Q_TILE)] = attended
        log_ref[:, pl.ds(first, Q_TILE)] = top + jnp.log2(mass)
        narrow = attended.T.astype(BF)
        for inner in range(Q_TILE // block):
            out_ref[index * (Q_TILE // block) + inner] = jnp.concatenate(
                [
                    narrow[inner * block : inner * block + half],
                    narrow[inner * block + half : (inner + 1) * block],
                ],
                axis=1,
            )
        return carry

    lax.fori_loop(0, rows // Q_TILE, query_tile, 0)


def attend(marks, packed, clips, halo):
    blocks, half, _ = packed.shape
    rows = (blocks - 2 * halo) * 2 * half
    key_rows = blocks * 2 * half
    return call(
        functools.partial(attend_kernel, clips, halo),
        [
            like((blocks - 2 * halo, half, 2 * HEAD_DIM), BF),
            like((HEAD_DIM, rows)),
            like((1, rows)),
        ],
        [
            pltpu.VMEM((HEAD_DIM, key_rows), BF),
            pltpu.VMEM((key_rows, HEAD_DIM), BF),
            pltpu.VMEM((HEAD_DIM + 16, key_rows), BF),
        ],
        (marks, packed),
        "attend",
        25 * 10**9,
    )


def attend_back_kernel(
    clips, halo, marks, packed_ref, grad_ref, wide_ref, log_ref, out_ref,
    query, query_t, keys, key_t, values, grads, grad_t, key_grads, value_grads,
):
    unpack_heads(packed_ref, ((query, query_t), (keys, key_t), (values, None)))
    unpack_heads(grad_ref, ((grads, grad_t),))
    blocks, half, _ = packed_ref.shape
    rows = wide_ref.shape[1]
    block = 2 * half
    scale = HEAD_DIM ** (-0.5)
    key_grads[...] = jnp.zeros_like(key_grads)
    value_grads[...] = jnp.zeros_like(value_grads)
    if halo:
        out_ref[...] = jnp.zeros_like(out_ref)

    def query_tile(index, carry):
        first = pl.multiple_of(index * Q_TILE, Q_TILE)
        own = pl.ds(halo * block + first, Q_TILE)
        q, q_t = query[own, :], query_t[:, own]
        g, g_t = grads[pl.ds(first, Q_TILE), :], grad_t[:, pl.ds(first, Q_TILE)]
        log_total = log_ref[:, pl.ds(first, Q_TILE)]
        delta = jnp.sum(
            g_t.astype(jnp.float32) * wide_ref[:, pl.ds(first, Q_TILE)], axis=0, keepdims=True
        )
        spans, starts, ends = tile_spans(marks, clips, index)

        def key_tile(masked, at, running):
            column = pl.multiple_of(at * K_TILE, K_TILE)
            here = pl.ds(column, K_TILE)
            probs = jnp.exp2(plain_dot(keys[here, :], q_t) * (scale * LOG2E) - log_total)
            if masked:
                probs = jnp.where(allowed(column, starts, ends), probs, 0.0)
            prob_grad = plain_dot(values[here, :], g_t)
            score_grad = (probs * (prob_grad - delta)).astype(BF)
            value_grads[here, :] += plain_dot(probs.astype(BF), g)
            key_grads[here, :] += plain_dot(score_grad, q)
            return running + plain_dot(key_t[:, here], score_grad)

        query_grad = over_spans(spans, key_tile, jnp.zeros((HEAD_DIM, Q_TILE), jnp.float32))
        query_grad = (query_grad.T * scale).astype(BF)
        for inner in range(Q_TILE // block):
            spot = halo + index * (Q_TILE // block) + inner
            out_ref[spot, :, 0:HEAD_DIM] = query_grad[inner * block : inner * block + half]
            out_ref[spot, :, 3 * HEAD_DIM : 4 * HEAD_DIM] = query_grad[
                inner * block + half : (inner + 1) * block
            ]
        return carry

    lax.fori_loop(0, rows // Q_TILE, query_tile, 0)

    def finish(spot, carry):
        for side in range(2):
            row = pl.multiple_of(spot * block + side * half, half)
            begin = (3 * side + 1) * HEAD_DIM
            out_ref[spot, :, begin : begin + 2 * HEAD_DIM] = jnp.concatenate(
                [key_grads[pl.ds(row, half), :] * scale, value_grads[pl.ds(row, half), :]], axis=1
            ).astype(BF)
        return carry

    lax.fori_loop(0, blocks, finish, 0)


def attend_back(marks, packed, grad, wide, log_total, clips, halo):
    blocks, half, lanes = packed.shape
    rows = wide.shape[1]
    key_rows = blocks * 2 * half
    return call(
        functools.partial(attend_back_kernel, clips, halo),
        [like((blocks, half, lanes), BF)],
        [
            pltpu.VMEM((key_rows, HEAD_DIM), BF),
            pltpu.VMEM((HEAD_DIM, key_rows), BF),
            pltpu.VMEM((key_rows, HEAD_DIM), BF),
            pltpu.VMEM((HEAD_DIM, key_rows), BF),
            pltpu.VMEM((key_rows, HEAD_DIM), BF),
            pltpu.VMEM((rows, HEAD_DIM), BF),
            pltpu.VMEM((HEAD_DIM, rows), BF),
            pltpu.VMEM((key_rows, HEAD_DIM), jnp.float32),
            pltpu.VMEM((key_rows, HEAD_DIM), jnp.float32),
        ],
        (marks, packed, grad, wide, log_total),
        "attend_back",
        35 * 10**9,
        limit=60,
    )[0]


TAPS = 16
SHOT = 384
TURNS = KERNEL // TAPS


def conv_weights_kernel(back, weight_ref, out_ref):
    group_width = out_ref.shape[1]
    if back:
        for group in range(GROUPS):
            lanes = slice(group_width * group, group_width * (group + 1))
            out_ref[group] = jnp.concatenate(
                [weight_ref[group_width * tap : group_width * (tap + 1), lanes] for tap in range(TAPS)],
                axis=1,
            )
    else:
        turned = weight_ref[...].T
        for group in range(GROUPS):
            out_ref[group] = turned[group_width * group : group_width * (group + 1)]


def conv_weights(back, weight, first, turns):
    width = weight.shape[1]
    group_width = width // GROUPS
    return call(
        functools.partial(conv_weights_kernel, back),
        [like((GROUPS, turns * group_width, TAPS * group_width), weight.dtype)],
        [],
        (weight,),
        "conv_weights_back" if back else "conv_weights",
        0,
        (turns,),
        [pl.BlockSpec((TAPS * group_width, width), lambda turn: (turn + first, 0))],
        (pl.BlockSpec((GROUPS, group_width, TAPS * group_width), lambda turn: (0, turn, 0)),),
    )[0]


def conv_kernel(back, clips, parts, marks, before_ref, rows_ref, after_ref, *refs):
    weight_refs, (out_ref, spaced, total) = refs[:parts], refs[parts:]
    group = pl.program_id(0)
    rows, width = rows_ref.shape
    half = KERNEL // 2
    long = rows + 2 * half
    group_width = width // GROUPS
    room = spaced.shape[1]
    places = marks[clips + BEGIN] - half + lax.broadcasted_iota(jnp.int32, (1, long), 1)
    ids = over_clips(
        clips,
        lambda clip, found: found + jnp.where(places >= marks[clip], 1, 0),
        jnp.zeros((1, long), jnp.int32),
    )
    ids = jnp.where((places >= 0) & (places < marks[clips + TOTAL]), ids, -1)

    def number_of(place):
        step = lambda clip, found: found + jnp.where(place >= marks[clip], 1, 0)
        return over_clips(clips, step, jnp.int32(0))

    first = number_of(marks[clips + BEGIN])
    count = number_of(marks[clips + BEGIN] + rows - 1) - first + 1

    @pl.when(group == 0)
    def _():
        turned = jnp.concatenate(
            [before_ref[...], rows_ref[...], after_ref[...]], axis=0
        ).astype(jnp.float32).T
        rest = jnp.zeros((width, room - long), jnp.float32)

        def of_clip(clip):
            return jnp.concatenate([jnp.where(ids == first + clip, turned, 0.0), rest], axis=1)

        spaced[...] = of_clip(0).astype(BF)

        def place(clip, carry):
            spaced[...] += pltpu.roll(of_clip(clip), clip * half, 1).astype(BF)
            return carry

        lax.fori_loop(1, count, place, 0)

    row = pl.multiple_of(group * group_width, group_width)
    shots = lax.div(rows + half * (count - 1) + SHOT - 1, SHOT)

    def shot(index, carry):
        base = pl.multiple_of(index * SHOT, 128)
        tile = spaced[pl.ds(row, group_width), pl.ds(base, SHOT + 2 * KERNEL)]
        moved = []
        for tap in range(TAPS):
            begin = TAPS - tap if back else tap
            moved.append(tile[:, begin : begin + SHOT + KERNEL])
        moved = jnp.concatenate(moved, axis=0)
        result = None
        turn = 0
        for weight_ref in weight_refs:
            product = plain_dot(weight_ref[0], moved)
            for inner in range(product.shape[0] // group_width):
                begin = (TURNS - 1 - turn if back else turn) * TAPS
                piece = product[inner * group_width : (inner + 1) * group_width, begin : begin + SHOT]
                result = piece if result is None else result + piece
                turn += 1
        total[pl.ds(row, group_width), pl.ds(base, SHOT)] = result
        return carry

    lax.fori_loop(0, shots, shot, 0)

    @pl.when(group == GROUPS - 1)
    def _():
        wide = total.shape[1]
        own = ids[:, half : half + rows]

        def collect(clip, carry):
            moved = pltpu.roll(total[...], lax.rem(wide - clip * half, wide), 1)[:, :rows]
            total[:, :rows] = jnp.where(own == first + clip, moved, total[:, :rows])
            return carry

        lax.fori_loop(1, count, collect, 0)
        out_ref[...] = total[:, :rows].T


def conv_rows(back, marks, before, value, after, weights, clips):
    rows, width = value.shape
    shots = -(-(rows + KERNEL // 2 * (clips - 1)) // SHOT)
    whole = lambda a: pl.BlockSpec(a.shape, lambda group: (0, 0))
    return call(
        functools.partial(conv_kernel, back, clips, len(weights)),
        [like((rows, width))],
        [
            pltpu.VMEM((width, SHOT * shots + 2 * KERNEL), BF),
            pltpu.VMEM((width, SHOT * shots), jnp.float32),
        ],
        (marks, before, value, after) + tuple(weights),
        "conv_back" if back else "conv",
        15 * 10**9,
        (GROUPS,),
        [SMEM_WHOLE, whole(before), whole(value), whole(after)]
        + [pl.BlockSpec((1,) + weight.shape[1:], lambda group: (group, 0, 0)) for weight in weights],
        (pl.BlockSpec((rows, width), lambda group: (0, 0)),),
        limit=48,
    )[0]


def taps_grad_kernel(
    clips, marks, both_ref, out_ref, inputs, spaced, input_cols, grad_cols
):
    half = KERNEL // 2
    group_width = inputs.shape[0]
    long = inputs.shape[1]
    blocks, _, block = both_ref.shape
    halo = (blocks - RING) // 2
    halo_rows = halo * block
    first = over_clips(
        clips,
        lambda clip, found: found + jnp.where(marks[clips + SEGMENT] >= marks[clip], 1, 0),
        jnp.int32(0),
    )
    origin = half + halo_rows
    span = input_cols.shape[1]

    def lay(first_row, begin_block, number, target, reach):
        for at in range(number):
            target[:, at * block : (at + 1) * block] = both_ref[
                begin_block + at, first_row : first_row + group_width
            ].astype(jnp.float32)
        target[:, number * block :] = jnp.zeros((group_width, long - number * block), jnp.float32)
        lanes = lax.broadcasted_iota(jnp.int32, (1, long), 1)
        places = marks[clips + SEGMENT] - reach + lanes
        held = lanes < number * block
        spaced[...] = jnp.zeros_like(spaced)

        def place(clip, carry):
            begin = jnp.where(clip > 0, marks[jnp.maximum(clip - 1, 0)], 0)
            keep = (places >= begin) & (places < marks[clip]) & held
            spaced[...] += pltpu.roll(
                jnp.where(keep, target[...], 0.0), origin - reach + half * (clip - first), 1
            )
            return carry

        lax.fori_loop(first, clips, place, 0)
        return spaced[...]

    laid = lay(0, 0, blocks, inputs, halo_rows)
    for turn in range(TURNS):
        begin = origin - half + turn * TAPS
        input_cols[turn * group_width : (turn + 1) * group_width, :] = laid[
            :, begin : begin + span
        ].astype(BF)
    laid = lay(group_width, halo, RING, inputs, 0)
    for tap in range(TAPS):
        grad_cols[tap * group_width : (tap + 1) * group_width, :] = laid[
            :, origin - tap : origin - tap + span
        ].astype(BF)
    result = row_dot(input_cols[...], grad_cols[...]).astype(BF)
    side_lanes = TAPS * group_width // 2
    for place_at in range(2 * TURNS):
        turn, side = place_at // 2, place_at % 2
        for piece in range(side_lanes // 128):
            begin = side * side_lanes + piece * 128
            row, column = pair_slot(out_ref.shape, place_at, marks, clips)
            out_ref[row, column, piece * group_width : (piece + 1) * group_width] = result[
                turn * group_width : (turn + 1) * group_width, begin : begin + 128
            ]


def taps_grad(marks, both, shape, clips):
    blocks, two, block = both.shape
    group_width = two // 2
    half = KERNEL // 2
    halo_rows = (blocks - RING) // 2 * block
    span = -(-(RING * block + half * clips) // 128) * 128
    long = span + 2 * halo_rows + half + 2 * KERNEL
    long = -(-long // 128) * 128
    more = TAPS * group_width // 2 // 128 * group_width
    return call(
        functools.partial(taps_grad_kernel, clips),
        [like(shape + (more, 128), BF)],
        [
            pltpu.VMEM((group_width, long), jnp.float32),
            pltpu.VMEM((group_width, long), jnp.float32),
            pltpu.VMEM((TURNS * group_width, span), BF),
            pltpu.VMEM((TAPS * group_width, span), BF),
        ],
        (marks, both),
        "taps_grad",
        10**10,
        limit=60,
    )[0]


def weave_taps_kernel(own_ref, other_ref, out_ref):
    group_width = out_ref.shape[1] // GROUPS
    taps = out_ref.shape[0] // group_width
    pieces = own_ref.shape[1] // group_width
    both = []
    for group in range(GROUPS):
        rows = own_ref[group].astype(jnp.float32) + other_ref[group].astype(jnp.float32)
        both.append(
            jnp.concatenate([rows[at * group_width : (at + 1) * group_width] for at in range(pieces)], axis=1)
        )
    for tap in range(taps):
        lanes = slice(tap * group_width, (tap + 1) * group_width)
        out_ref[tap * group_width : (tap + 1) * group_width, :] = jnp.concatenate(
            [value[:, lanes] for value in both], axis=1
        )


def weave_taps(own, other, taps, group_width):
    return call(
        weave_taps_kernel, [like((taps * group_width, GROUPS * group_width))], [], (own, other), "weave_taps", 0
    )[0]


def join_pair_kernel(clips, marks, sums_ref, other_sums_ref, taps_ref, other_taps_ref, out_ref):
    below, rows = sums_ref.shape[2], taps_ref.shape[2]
    out_ref[:, :below] = (
        sums_ref[0].astype(jnp.float32) + other_sums_ref[...].astype(jnp.float32)
    ).astype(BF)
    first = marks[clips + CORE] == 0
    out_ref[:, below : below + rows] = jnp.where(first, taps_ref[0], other_taps_ref[...])
    out_ref[:, below + rows :] = jnp.where(first, other_taps_ref[...], taps_ref[0])


def join_pair(marks, sums, other_sums, taps, other_taps, clips):
    _, chips, below, lanes = sums.shape
    return call(
        functools.partial(join_pair_kernel, clips),
        [like((chips, below + 2 * taps.shape[2], lanes), BF)],
        [],
        (marks, sums, other_sums, taps, other_taps),
        "join_pair",
        0,
    )[0]


SHARE = 384
PIECE = 128


def norm_parts(values):
    center = values - jnp.mean(values, axis=-1, keepdims=True)
    inverse = lax.rsqrt(jnp.mean(center * center, axis=-1, keepdims=True) + EPS)
    return center * inverse, inverse


def norm_back(unit, inverse, scales, grad):
    scaled = grad * scales
    back = inverse * (
        scaled
        - jnp.mean(scaled, axis=-1, keepdims=True)
        - unit * jnp.mean(scaled * unit, axis=-1, keepdims=True)
    )
    return back, row_sum(grad * unit), row_sum(grad)


def row_sum(values):
    return jnp.sum(values, axis=0, keepdims=True)


def gelu_both(values):
    below = 0.5 + 0.5 * lax.erf(values * 0.7071067811865476)
    bell = jnp.exp(-0.5 * values * values) * 0.3989422804014327
    return values * below, below + values * bell


def store_turned(values_b, out_ref, first):
    group_width = values_b.shape[1] // GROUPS
    turned = values_b.T
    for group in range(GROUPS):
        out_ref[group, first : first + group_width] = turned[group * group_width : (group + 1) * group_width]


def same_clip_next(marks, clips, rows):
    following = marks[clips + BEGIN] + 1 + lax.broadcasted_iota(jnp.int32, (rows, 1), 0)
    step = lambda clip, other: jnp.maximum(other, jnp.where(following == marks[clip], 1, 0))
    return over_clips(clips, step, jnp.zeros((rows, 1), jnp.int32)) == 0


def stem_kernel(
    clips, marks, samples_ref, next_ref, weight_ref, gain_ref, bias_ref, proj_ref, gains_ref, biases_ref,
    start_ref, start_b_ref, pre_ref, normed_ref, unfold_ref, table_ref, wide,
):
    rows, chans = pre_ref.shape
    table_ref[0:3] = gains_ref[...]
    table_ref[3:12] = biases_ref[...]
    last = lax.broadcasted_iota(jnp.int32, (rows, 1), 0) == rows - 1
    same = same_clip_next(marks, clips, rows)
    for lane in range(0, chans, PIECE):
        lanes = slice(lane, lane + PIECE)
        wide[...] = samples_ref[:, lanes].astype(jnp.float32)
        even = wide[pl.ds(0, rows, stride=2), :]
        unfold_ref[:, lanes] = even.astype(BF)
        unfold_ref[:, chans + lane : chans + lane + PIECE] = wide[pl.ds(1, rows, stride=2), :].astype(BF)
        moved = jnp.where(last, next_ref[:, lanes].astype(jnp.float32), pltpu.roll(even, rows - 1, 0))
        unfold_ref[:, 2 * chans + lane : 2 * chans + lane + PIECE] = jnp.where(same, moved, 0.0).astype(BF)
    pre = plain_dot(unfold_ref[...], weight_ref[...])
    pre_ref[...] = pre
    unit, _ = norm_parts(gelu_both(pre)[0])
    normed = (unit * gain_ref[...] + bias_ref[...]).astype(BF)
    normed_ref[...] = normed
    start = plain_dot(normed, proj_ref[...]) + table_ref[3:4]
    start_ref[...] = start
    start_b_ref[...] = start.astype(BF)


def stem(marks, samples, next_row, weight, gain, bias, proj, gains, biases, clips):
    rows = samples.shape[0] // 2
    chans, width = proj.shape
    return call(
        functools.partial(stem_kernel, clips),
        [
            like((rows, width)), like((rows, width), BF),
            like((rows, chans)), like((rows, chans), BF), like((rows, 3 * chans), BF), like((12, width)),
        ],
        [pltpu.VMEM((2 * rows, PIECE), jnp.float32)],
        (marks, samples, next_row, weight, gain, bias, proj, gains, biases),
        "stem",
        6 * 10**9,
    )


def project_kernel(conv_ref, start_ref, table_ref, weight_ref, hidden_ref, packed_ref):
    rows, width = start_ref.shape
    half = rows // 2
    mixed = start_ref[...] + gelu_both(conv_ref[...] + table_ref[4:5])[0]
    unit, _ = norm_parts(mixed)
    hidden = unit * table_ref[0:1] + table_ref[5:6]
    hidden_ref[...] = hidden
    hidden_b = hidden.astype(BF)
    shifts = (table_ref[6:7], jnp.zeros((1, width), jnp.float32), table_ref[7:8])
    parts = [
        (plain_dot(hidden_b, weight_ref[:, at * width : (at + 1) * width]) + shift).astype(BF)
        for at, shift in enumerate(shifts)
    ]
    heads = width // HEAD_DIM
    for head in range(heads):
        lanes = slice(head * HEAD_DIM, (head + 1) * HEAD_DIM)
        packed_ref[head] = jnp.concatenate(
            [part[:half, lanes] for part in parts] + [part[half:, lanes] for part in parts], axis=1
        )
    for head in range(heads, RING):
        packed_ref[head] = jnp.zeros_like(packed_ref[head])


def project_heads(conv_sum, start, table, weight):
    rows, width = start.shape
    return call(
        project_kernel,
        [like((rows, width)), like((RING, rows // 2, 6 * HEAD_DIM), BF)],
        [],
        (conv_sum, start, table, weight),
        "project_heads",
        6 * 10**9,
    )


def middle_kernel(
    heads_ref, hidden_ref, table_ref, out_weight_ref, in_ref, in_bias_ref, back_ref, out_grad_ref,
    layer_ref, grad_heads_ref, grad_second_ref, out_part_ref, sums_ref, in_bias_grad_ref, joined_ref,
    attended, before, second, second_b, second_t, inner_b, slope, total, grad_last, grad_last_b,
    joined, sems,
):
    step = pl.program_id(0)
    rows, width = hidden_ref.shape
    half = rows // 2
    chunk = in_ref.shape[1]
    chunks = pl.num_programs(0) // 2
    heads = width // HEAD_DIM
    shares = joined_ref.shape[0]
    in_rows = width // shares
    back_rows = chunk * chunks // shares
    owners = chunk // back_rows

    def in_copy(at):
        place = (slice(None), pl.ds(pl.multiple_of(at * in_rows, 16), in_rows))
        return pltpu.make_async_copy(joined.at[place], joined_ref.at[place], sems.at[0, at])

    def back_copy(at):
        place = (pl.ds(at * owners, owners), pl.ds(in_rows * chunks, joined_ref.shape[1] - in_rows * chunks))
        return pltpu.make_async_copy(joined.at[place], joined_ref.at[place], sems.at[1, at])

    @pl.when(step == 0)
    def _():
        for head in range(heads):
            lanes = slice(head * HEAD_DIM, (head + 1) * HEAD_DIM)
            attended[:half, lanes] = heads_ref[head, :, :HEAD_DIM]
            attended[half:, lanes] = heads_ref[head, :, HEAD_DIM:]
        value = hidden_ref[...] + plain_dot(attended[...], out_weight_ref[...]) + table_ref[8:9]
        before[...] = value
        unit, _ = norm_parts(value)
        value = unit * table_ref[1:2] + table_ref[9:10]
        second[...] = value
        second_b[...] = value.astype(BF)
        second_t[...] = value.T.astype(BF)
        total[...] = jnp.zeros_like(total)

    @pl.when(step < chunks)
    def _():
        at = pl.multiple_of(step * chunk, chunk)
        value, back = gelu_both(plain_dot(second_b[...], in_ref[...]) + in_bias_ref[:, pl.ds(at, chunk)])
        value_b = value.astype(BF)
        inner_b[step] = value_b
        slope[step] = back
        total[...] += plain_dot(value_b, back_ref[...])

    @pl.when(step == chunks - 1)
    def _():
        unit, inverse = norm_parts(second[...] + total[...] + table_ref[10:11])
        layer_ref[...] = (unit * table_ref[2:3] + table_ref[11:12]).astype(BF)
        back, gain, bias = norm_back(unit, inverse, table_ref[2:3], out_grad_ref[...].astype(jnp.float32))
        grad_last[...] = back
        grad_last_b[...] = back.astype(BF)
        total[...] = back
        sums_ref[0:1] = gain
        sums_ref[1:2] = bias
        sums_ref[2:3] = row_sum(back)

    @pl.when(step >= chunks)
    def _():
        turn = step - chunks
        at = pl.multiple_of(turn * chunk, chunk)
        grad = row_dot(grad_last_b[...], back_ref[...]) * slope[turn]
        in_bias_grad_ref[:, pl.ds(at, chunk)] = row_sum(grad)
        grad_b = grad.astype(BF)
        total[...] += row_dot(grad_b, in_ref[...])
        product = plain_dot(second_t[...], grad_b).astype(BF)
        for share in range(shares):
            joined[share, pl.ds(pl.multiple_of(turn * in_rows, 16), in_rows), :] = product[
                share * in_rows : (share + 1) * in_rows
            ]
        in_copy(turn).start()
        product = over_rows_dot(inner_b[turn], grad_last_b[...]).astype(BF)
        for owner in range(owners):
            for place in range(width // SHARE):
                begin = in_rows * chunks + place * back_rows
                joined[turn * owners + owner, begin : begin + back_rows, :] = product[
                    owner * back_rows : (owner + 1) * back_rows, place * SHARE : (place + 1) * SHARE
                ]
        back_copy(turn).start()

    @pl.when(step == 2 * chunks - 1)
    def _():
        unit, inverse = norm_parts(before[...])
        back, gain, bias = norm_back(unit, inverse, table_ref[1:2], total[...])
        grad_second_ref[...] = back
        sums_ref[3:4] = row_sum(back)
        sums_ref[4:5] = gain
        sums_ref[5:6] = bias
        sums_ref[6:8] = jnp.zeros((2, width), jnp.float32)
        back_b = back.astype(BF)
        grads = row_dot(back_b, out_weight_ref[...]).astype(BF)
        for head in range(heads):
            lanes = slice(head * HEAD_DIM, (head + 1) * HEAD_DIM)
            grad_heads_ref[head] = jnp.concatenate([grads[:half, lanes], grads[half:, lanes]], axis=1)
        for head in range(heads, RING):
            grad_heads_ref[head] = jnp.zeros_like(grad_heads_ref[head])
        product = over_rows_dot(attended[...], back_b).astype(BF)
        for share in range(shares):
            for place in range(width // SHARE):
                out_part_ref[share, place * in_rows : (place + 1) * in_rows, :] = product[
                    share * in_rows : (share + 1) * in_rows, place * SHARE : (place + 1) * SHARE
                ]

        def finish(at, carry):
            in_copy(at).wait()
            back_copy(at).wait()
            return carry

        lax.fori_loop(0, chunks, finish, 0)


def middle(heads, hidden, table, out_weight, ffn_in, in_bias, ffn_out, out_grad, count):
    rows, width = hidden.shape
    inner = ffn_in.shape[1]
    chunk = SHARE
    chunks = inner // chunk
    own = lambda shape: pl.BlockSpec(shape, lambda step: (0,) * len(shape))
    outs = [
        like((rows, width), BF),
        like((RING, rows // 2, 2 * HEAD_DIM), BF),
        like((rows, width)),
        like((count, width // count * width // SHARE, SHARE), BF),
        like((8, width)),
        like((1, inner)),
        like((count, 2 * width // count * inner // SHARE, SHARE), BF),
    ]
    args = (heads, hidden, table, out_weight, ffn_in, in_bias, ffn_out, out_grad)
    in_specs = [own(a.shape) for a in args]
    in_specs[4] = pl.BlockSpec((width, chunk), lambda step: (0, step % chunks))
    in_specs[6] = pl.BlockSpec((chunk, width), lambda step: (step % chunks, 0))
    out_specs = [own(o.shape) for o in outs]
    out_specs[6] = pl.BlockSpec(memory_space=pl.ANY)
    scratch = [
        pltpu.VMEM((rows, width), BF),
        pltpu.VMEM((rows, width), jnp.float32),
        pltpu.VMEM((rows, width), jnp.float32),
        pltpu.VMEM((rows, width), BF),
        pltpu.VMEM((width, rows), BF),
        pltpu.VMEM((chunks, rows, chunk), BF),
        pltpu.VMEM((chunks, rows, chunk), jnp.float32),
        pltpu.VMEM((rows, width), jnp.float32),
        pltpu.VMEM((rows, width), jnp.float32),
        pltpu.VMEM((rows, width), BF),
        pltpu.VMEM(outs[6].shape, BF),
        pltpu.SemaphoreType.DMA((2, chunks)),
    ]
    return call(
        middle_kernel, outs, scratch, args, "middle", 2 * 10**10, (2 * chunks,), in_specs, tuple(out_specs)
    )


def after_heads_kernel(
    packed_ref, grad_second_ref, hidden_ref, conv_ref, start_ref, table_ref, weight_ref, out_part_ref,
    mixed_ref, conv_b_ref, groups_ref, joined_ref, sums_ref, grads,
):
    rows, width = hidden_ref.shape
    half = rows // 2
    heads = width // HEAD_DIM
    shares = joined_ref.shape[0]
    own_rows = width // shares
    for head in range(heads):
        tile = packed_ref[head]
        for part in range(3):
            lanes = slice(part * width + head * HEAD_DIM, part * width + (head + 1) * HEAD_DIM)
            grads[:half, lanes] = tile[:, part * HEAD_DIM : (part + 1) * HEAD_DIM]
            grads[half:, lanes] = tile[:, (part + 3) * HEAD_DIM : (part + 4) * HEAD_DIM]
    hidden_t = hidden_ref[...].T.astype(BF)
    blocks = 3 * width // SHARE
    for place in range(blocks):
        lanes = slice(place * SHARE, (place + 1) * SHARE)
        product = plain_dot(hidden_t, grads[:, lanes]).astype(BF)
        for share in range(shares):
            joined_ref[share, place * own_rows : (place + 1) * own_rows, :] = product[
                share * own_rows : (share + 1) * own_rows
            ]
    for share in range(shares):
        joined_ref[share, blocks * own_rows :, :] = out_part_ref[share]
    back = grad_second_ref[...] + row_dot(grads[...], weight_ref[...])
    value, slope = gelu_both(conv_ref[...] + table_ref[4:5])
    unit, inverse = norm_parts(start_ref[...] + value)
    mixed, gain, bias = norm_back(unit, inverse, table_ref[0:1], back)
    mixed_ref[...] = mixed
    conv = mixed * slope
    conv_b = conv.astype(BF)
    conv_b_ref[...] = conv_b
    store_turned(start_ref[...].astype(BF), groups_ref, 0)
    store_turned(conv_b, groups_ref, width // GROUPS)
    sums_ref[0:1] = gain
    sums_ref[1:2] = bias
    sums_ref[2:3] = row_sum(conv)
    sums_ref[3:4] = row_sum(grads[:, :width].astype(jnp.float32))
    sums_ref[4:5] = row_sum(grads[:, 2 * width :].astype(jnp.float32))
    sums_ref[5:8] = jnp.zeros((3, width), jnp.float32)


def after_heads(packed, grad_second, hidden, conv_sum, start, table, weight, out_part):
    rows, width = hidden.shape
    shares = out_part.shape[0]
    return call(
        after_heads_kernel,
        [
            like((rows, width)), like((rows, width), BF),
            like((GROUPS, 2 * width // GROUPS, rows), BF),
            like((shares, out_part.shape[1] + width // shares * 3 * width // SHARE, SHARE), BF),
            like((8, width)),
        ],
        [pltpu.VMEM((rows, 3 * width), BF)],
        (packed, grad_second, hidden, conv_sum, start, table, weight, out_part),
        "after_heads",
        6 * 10**9,
    )


def stem_back_kernel(
    clips, marks, input_ref, mixed_ref, normed_ref, pre_ref, unfold_ref, weight_ref, gain_ref, proj_ref,
    middle_sums_ref, inner_sums_ref, after_sums_ref,
    samples_ref, carried_ref, joined_ref, table, spread, woven,
):
    rows, chans = pre_ref.shape
    width = input_ref.shape[1]
    shares = joined_ref.shape[0] * joined_ref.shape[1]
    start = mixed_ref[...] + input_ref[...]
    start_b = start.astype(BF)

    def share_out(product, begin):
        own, columns = product.shape[0] // shares, product.shape[1]
        for share in range(shares):
            for place in range(columns // PIECE):
                at = begin + place * own
                row, column = pair_slot(joined_ref.shape, share, marks, clips)
                joined_ref[row, column, at : at + own, :] = product[
                    share * own : (share + 1) * own, place * PIECE : (place + 1) * PIECE
                ]
        return begin + own * columns // PIECE

    at = share_out(over_rows_dot(normed_ref[...], start_b).astype(BF), 0)
    value, slope = gelu_both(pre_ref[...])
    unit, inverse = norm_parts(value)
    feature, gain_sum, bias_sum = norm_back(
        unit, inverse, gain_ref[...], row_dot(start_b, proj_ref[...])
    )
    pre_b = (feature * slope).astype(BF)
    taps_t = over_rows_dot(unfold_ref[...], pre_b).astype(BF)
    at = share_out(taps_t, at)
    first = row_dot(pre_b, weight_ref[:chans])
    same = same_clip_next(marks, clips, rows)
    follow = jnp.where(same, row_dot(pre_b, weight_ref[2 * chans :]), 0.0)
    carried_ref[...] = follow[rows - 1 :]
    moved = pltpu.roll(follow, 1, 0)
    top = lax.broadcasted_iota(jnp.int32, (rows, 1), 0) == 0
    even = first + jnp.where(top, 0.0, moved)
    odd = row_dot(pre_b, weight_ref[chans : 2 * chans])
    for lane in range(0, chans, PIECE):
        woven[pl.ds(0, rows, stride=2), :] = even[:, lane : lane + PIECE]
        woven[pl.ds(1, rows, stride=2), :] = odd[:, lane : lane + PIECE]
        samples_ref[:, lane : lane + PIECE] = woven[...]
    table[0:1] = after_sums_ref[0:1]
    table[1:2] = middle_sums_ref[4:5]
    table[2:3] = middle_sums_ref[0:1]
    table[3:4] = row_sum(start)
    table[4:5] = after_sums_ref[2:3]
    table[5:6] = after_sums_ref[1:2]
    table[6:7] = after_sums_ref[3:4]
    table[7:8] = after_sums_ref[4:5]
    table[8:9] = middle_sums_ref[3:4]
    table[9:10] = middle_sums_ref[5:6]
    table[10:11] = middle_sums_ref[2:3]
    table[11:12] = middle_sums_ref[1:2]
    spread[...] = jnp.zeros_like(spread)
    own, own_chans = width // shares, chans // shares
    own_inner = inner_sums_ref.shape[1] // shares
    for share in range(shares):
        spread[share, 0:12, 0:own] = table[:, share * own : (share + 1) * own]
        for place in range(-(-own_inner // PIECE)):
            length = min(PIECE, own_inner - place * PIECE)
            begin = share * own_inner + place * PIECE
            spread[share, 12 + place : 13 + place, 0:length] = inner_sums_ref[:, begin : begin + length]
        lanes = slice(share * own_chans, (share + 1) * own_chans)
        spread[share, 14:15, 0:own_chans] = gain_sum[:, lanes]
        spread[share, 15:16, 0:own_chans] = bias_sum[:, lanes]
        row, column = pair_slot(joined_ref.shape, share, marks, clips)
        joined_ref[row, column, at:, :] = spread[share].astype(BF)


def stem_back(marks, input_grad, mixed, normed, pre, unfold, weight, gain, proj, sums, shares, clips):
    rows, chans = pre.shape
    width = input_grad.shape[1]
    pieces = (chans // RING * width + 3 * chans // RING * chans) // PIECE + 16
    return call(
        functools.partial(stem_back_kernel, clips),
        [like((2 * rows, chans)), like((1, chans)), like(shares + (pieces, PIECE), BF)],
        [pltpu.VMEM((12, width), jnp.float32), pltpu.VMEM((RING, 16, PIECE), jnp.float32),
         pltpu.VMEM((2 * rows, PIECE), jnp.float32)],
        (marks, input_grad, mixed, normed, pre, unfold, weight, gain, proj) + sums,
        "stem_back",
        6 * 10**9,
    )


def from_behind(value, axis, steps):
    count = lax.axis_size(axis)
    initial, last = (max(0, -steps), min(count, count - steps))
    return lax.ppermute(value, axis, [(source, source + steps) for source in range(initial, last)])


def edges(value, width):
    length = value.shape[0]
    return from_behind(value[length - width :], "seq", 1), from_behind(value[:width], "seq", -1)


def near_groups():
    size = lax.axis_size("seq")
    return [[base + i for i in range(RING)] for base in range(0, size, RING)]


def swap(value):
    groups = None if lax.axis_size("seq") == RING else near_groups()
    return lax.all_to_all(value, "seq", 0, 0, axis_index_groups=groups)


def with_far_blocks(value, count):
    if lax.axis_size("seq") == RING or count == 0:
        return value
    before = from_behind(value[value.shape[0] - count :], "seq", RING)
    after = from_behind(value[:count], "seq", -RING)
    return jnp.concatenate([before, value, after], axis=0)


def fold_far_blocks(value, count):
    if lax.axis_size("seq") == RING or count == 0:
        return value
    own = value[count : value.shape[0] - count]
    to_before = from_behind(value[:count], "seq", -RING)
    to_after = from_behind(value[value.shape[0] - count :], "seq", RING)
    wide = own.astype(jnp.float32)
    wide = wide.at[wide.shape[0] - count :].add(to_before.astype(jnp.float32))
    wide = wide.at[:count].add(to_after.astype(jnp.float32))
    return wide.astype(value.dtype)


def other_stream(share):
    return lax.ppermute(share, "rep", [(0, 1), (1, 0)])


def sum_pair(share):
    return share.astype(jnp.float32) + other_stream(share).astype(jnp.float32)


def spread_out(total, sizes, lanes):
    out, at = [], 0
    for rows, columns in sizes:
        parts = []
        for _ in range(columns // lanes):
            parts.append(total[at : at + rows])
            at += rows
        out.append(jnp.concatenate(parts, axis=1))
    return out


def regroup(joined, blocks):
    count = lax.axis_size("seq")
    if count == RING:
        return joined
    parts = count // RING
    lanes = joined.shape[2]
    out, at = [], 0
    for number, rows in blocks:
        piece = joined[:, at : at + number * rows]
        at += number * rows
        piece = piece.reshape(RING, number, parts, rows // parts, lanes).transpose(0, 2, 1, 3, 4)
        out.append(piece.reshape(count, number * rows // parts, lanes))
    return jnp.concatenate(out, axis=1)


def regroup_small(small, widths):
    count = lax.axis_size("seq")
    if count == RING:
        return small
    parts = count // RING
    own, own_inner, own_chans = widths
    lanes = small.shape[2]
    table = small[:, :12, : own * parts].reshape(RING, 12, parts, own).transpose(0, 2, 1, 3)
    table = jnp.pad(table.reshape(count, 12, own), ((0, 0), (0, 0), (0, lanes - own)))
    wide = small[:, 12:14].reshape(RING, 2 * lanes)[:, : own_inner * parts].reshape(count, own_inner)
    wide = jnp.pad(wide, ((0, 0), (0, 2 * lanes - own_inner))).reshape(count, 2, lanes)
    stems = small[:, 14:16, : own_chans * parts].reshape(RING, 2, parts, own_chans).transpose(0, 2, 1, 3)
    stems = jnp.pad(stems.reshape(count, 2, own_chans), ((0, 0), (0, 0), (0, lanes - own_chans)))
    return jnp.concatenate([table, wide, stems], axis=1)


def over_seq(joined):
    return lax.psum_scatter(joined, "seq", scatter_dimension=0, tiled=False).astype(jnp.bfloat16)


def local(
    samples,
    clip_lengths,
    stem_weight,
    stem_gain,
    stem_bias,
    proj_weight,
    pos_weight,
    norm_gains,
    biases,
    attn_in,
    attn_out,
    ffn_in,
    ffn_in_bias,
    ffn_out,
    out_grad,
):
    rows_dev = out_grad.shape[1]
    width = attn_out.shape[0]
    chans = stem_weight.shape[1]
    inner = ffn_in.shape[1]
    group_width = width // GROUPS
    count = lax.axis_size("seq")
    place = lax.axis_index("seq")
    total = rows_dev * count
    begin = place * rows_dev
    ends = jnp.cumsum(clip_lengths[0])
    clips = ends.shape[0]
    half = KERNEL // 2
    far = 0 if count == RING else -(-MAXLEN // rows_dev)
    segment_begin = (place // RING) * RING * rows_dev
    active = jnp.where(place % RING < HEADS, 1, 0)
    marks = jnp.concatenate(
        [ends, jnp.stack([jnp.int32(total), begin, segment_begin, segment_begin - far * rows_dev, active, place % 2])]
    ).astype(jnp.int32)
    next_row = from_behind(samples[0, :1], "seq", -1)
    one_weights = conv_weights(False, pos_weight, 0, TURNS // 2)
    next_row, one_weights = lax.optimization_barrier((next_row, one_weights))
    start_x, start_b, stem_pre, normed_b, unfold, table = stem(
        marks, samples[0], next_row, stem_weight, stem_gain[None], stem_bias[None], proj_weight,
        norm_gains.T, biases.T, clips,
    )
    before, after = edges(start_b, half)
    rest_source, _ = lax.optimization_barrier((pos_weight, table))
    rest_weights = conv_weights(False, rest_source, TURNS // 2, TURNS // 2)
    before, after, rest_weights = lax.optimization_barrier((before, after, rest_weights))
    conv_sum = conv_rows(False, marks, before, start_b, after, (one_weights, rest_weights), clips)
    hidden, packed = project_heads(conv_sum, start_x, table, attn_in)
    back_source, _ = lax.optimization_barrier((pos_weight, hidden))
    packed = with_far_blocks(swap(packed), far)
    back_weights = conv_weights(True, back_source, 0, TURNS)
    packed, back_weights = lax.optimization_barrier((packed, back_weights))
    attended_heads, wide, log_total = attend(marks, packed, clips, far)
    layer_out, grad_heads, grad_pre_second, out_part, middle_sums, inner_sums, ffn_joined = middle(
        swap(attended_heads), hidden, table, attn_out, ffn_in, ffn_in_bias[None], ffn_out, out_grad[0],
        RING,
    )
    near_rows, near_chans, near_inner = width // RING, chans // RING, inner // RING
    grad_heads = swap(grad_heads)
    ffn_share = over_seq(
        regroup(ffn_joined, [(inner // SHARE, near_rows), (width // SHARE, near_inner)])
    )
    packed_grad = attend_back(marks, packed, grad_heads, wide, log_total, clips, far)
    grad_mixed, grad_conv_b, grad_packed, attn_joined, after_sums = after_heads(
        swap(fold_far_blocks(packed_grad, far)), grad_pre_second, hidden, conv_sum, start_x, table,
        attn_in, out_part,
    )
    before, after = edges(grad_conv_b, half)
    before, after, grad_packed = lax.optimization_barrier((before, after, grad_packed))
    grad_groups = swap(grad_packed)
    input_grad = conv_rows(True, marks, before, grad_conv_b, after, (back_weights,), clips)
    input_grad, grad_groups, ffn_share = lax.optimization_barrier((input_grad, grad_groups, ffn_share))
    attn_share = over_seq(regroup(attn_joined, [(4 * width // SHARE, near_rows)]))
    shape = (2, RING // 2) if count == RING else (1, RING)
    sample_grad, carried, stem_joined = stem_back(
        marks, input_grad, grad_mixed, normed_b, stem_pre, unfold, stem_weight, stem_gain[None],
        proj_weight, (middle_sums, inner_sums, after_sums), shape, clips,
    )
    carried = from_behind(carried, "seq", 1)
    own = width // count
    own_chans = chans // count
    own_taps = KERNEL // count
    below = stem_joined.shape[2]
    grad_ffn = spread_out(sum_pair(ffn_share), [(own, inner), (inner // count, width)], SHARE)
    stem_joined, grad_ffn, grad_groups = lax.optimization_barrier((stem_joined, grad_ffn, grad_groups))
    taps = taps_grad(marks, with_far_blocks(grad_groups, 0 if count == RING else 1), shape, clips)
    if count == RING:
        pairs = [(i, i ^ 1) for i in range(count)]
        joined = join_pair(
            marks,
            stem_joined,
            lax.ppermute(stem_joined[1], "seq", pairs),
            taps,
            lax.ppermute(taps[1], "seq", pairs),
            clips,
        )
        alike = [list(range(core, count, 2)) for core in range(2)]
        received = lax.all_to_all(joined, "seq", 0, 0, axis_index_groups=alike)
        pos_pieces = received[:, below:].reshape(GROUPS, -1, PIECE)
    else:
        stem_joined = stem_joined[0]
        stem_joined = jnp.concatenate(
            [
                regroup(
                    stem_joined[:, :-16],
                    [(width // PIECE, near_chans), (chans // PIECE, 3 * near_chans)],
                ),
                regroup_small(stem_joined[:, -16:], (own, inner // count, own_chans)),
            ],
            axis=1,
        )
        received = lax.all_to_all(stem_joined, "seq", 0, 0)
        below = stem_joined.shape[1]
        segments = count // RING
        by_tap = taps.reshape(2 * TURNS, 3, group_width, PIECE).transpose(0, 2, 1, 3)
        by_tap = by_tap.reshape(2 * TURNS, group_width, TAPS // 2, group_width)
        by_tap = by_tap.transpose(0, 2, 1, 3).reshape(segments, -1, 2 * PIECE)
        across = [[low_at + RING * j for j in range(segments)] for low_at in range(RING)]
        by_tap = lax.all_to_all(by_tap, "seq", 0, 0, axis_index_groups=across)
        by_tap = jnp.sum(by_tap.astype(jnp.float32), axis=0).astype(jnp.bfloat16)
        by_tap = by_tap.reshape(RING, own_taps, group_width, group_width).transpose(0, 2, 1, 3)
        pos_pieces = swap(by_tap.reshape(RING, group_width, own_taps * group_width))
    pos_grad = weave_taps(pos_pieces, other_stream(pos_pieces), own_taps, group_width)
    stem_total = sum_pair(jnp.sum(received[:, :below].astype(jnp.float32), axis=0).astype(jnp.bfloat16))
    grad_proj, grad_stem = spread_out(
        stem_total[:-16], [(own_chans, width), (3 * own_chans, chans)], PIECE
    )
    small = stem_total[-16:]
    grad_ffn_in, grad_ffn_out = grad_ffn
    grad_attn_in, grad_attn_out = spread_out(
        sum_pair(attn_share), [(own, 3 * width), (own, width)], SHARE
    )
    sample_grad = sample_grad.at[:1].add(carried)
    return (
        layer_out[None],
        sample_grad[None],
        grad_stem,
        small[14, :own_chans],
        small[15, :own_chans],
        grad_proj,
        pos_grad,
        small[:3, :own].T,
        small[3:12, :own].T,
        grad_attn_in,
        grad_attn_out,
        grad_ffn_in,
        small[12:14].reshape(-1)[: inner // count],
        grad_ffn_out,
    )


def solution(mesh):
    streams = P("rep", "seq", None)
    rows = P("seq", None)
    return jax.shard_map(
        local,
        mesh=mesh,
        in_specs=(streams, P("rep", None)) + (P(),) * 12 + (streams,),
        out_specs=(streams, streams, rows, P("seq"), P("seq"))
        + (rows,) * 7
        + (P("seq"), rows),
        check_vma=False,
    )
```

```python
import functools

import jax
import jax.numpy as jnp
from jax import lax
from jax.experimental import pallas as pl
from jax.experimental.pallas import tpu as pltpu
from jax.sharding import PartitionSpec as P

HEADS = 12
KERNEL = 128
GROUPS = 16
MAXLEN = 1536
RING = 16
HEAD_DIM = 64
EPS = 1e-05
BF = jnp.bfloat16
VMEM_WHOLE = pl.BlockSpec(memory_space=pltpu.VMEM)
SMEM_WHOLE = pl.BlockSpec(memory_space=pltpu.SMEM)
TOTAL, BEGIN, SEGMENT, KEYS, ACTIVE, CORE = range(6)


def row_dot(left, right):
    return lax.dot_general(left, right, (((1,), (1,)), ((), ())), preferred_element_type=jnp.float32)


def plain_dot(left, right):
    return lax.dot_general(left, right, (((1,), (0,)), ((), ())), preferred_element_type=jnp.float32)


def over_rows_dot(left, right):
    return lax.dot_general(left, right, (((0,), (0,)), ((), ())), preferred_element_type=jnp.float32)


def store_pairs(refs, even, rows, values):
    if len(refs) == 1:
        for share, value in enumerate(values):
            refs[0][share, rows, :] = value
        return
    kept, sent = refs
    for at in range(len(values) // 2):
        first, second = values[2 * at], values[2 * at + 1]
        kept[at, rows, :] = jnp.where(even, first, second)
        sent[at, rows, :] = jnp.where(even, second, first)


def over_clips(clips, step, state):
    if clips <= 8:
        for clip in range(clips):
            state = step(clip, state)
        return state
    return lax.fori_loop(0, clips, step, state)


def clip_bounds(marks, clips, places):
    def step(clip, state):
        first, end = state
        mark = marks[clip]
        return (
            jnp.maximum(first, jnp.where(mark <= places, mark, 0)),
            jnp.minimum(end, jnp.where(mark > places, mark, marks[clips + TOTAL])),
        )

    return over_clips(clips, step, (jnp.zeros_like(places), jnp.zeros_like(places) + marks[clips + TOTAL]))


def like(shape, dtype=jnp.float32):
    return jax.ShapeDtypeStruct(shape, dtype)


def call(kernel, outs, scratch, args, name, flops, grid=None, in_specs=None, out_specs=None, limit=56):
    size = sum(a.size * a.dtype.itemsize for a in args)
    size += sum(o.size * o.dtype.itemsize for o in outs)
    extra = {} if grid is None else {"grid": grid}
    return pl.pallas_call(
        kernel,
        out_shape=tuple(outs),
        in_specs=in_specs or [SMEM_WHOLE if a.dtype == jnp.int32 else VMEM_WHOLE for a in args],
        out_specs=out_specs or (VMEM_WHOLE,) * len(outs),
        scratch_shapes=scratch,
        compiler_params=pltpu.CompilerParams(vmem_limit_bytes=limit << 20),
        cost_estimate=pl.CostEstimate(flops=flops, bytes_accessed=size, transcendentals=0),
        name=name,
        **extra,
    )(*args)


Q_TILE = 512
K_TILE = 512
LOW = -1e30
LOG2E = 1.4426950408889634


def unpack_heads(packed_ref, targets):
    blocks, half, lanes = packed_ref.shape
    share = lanes // 2

    def one(block, carry):
        tile = packed_ref[block]
        turned = tile.T
        for side in range(2):
            row = pl.multiple_of(block * 2 * half + side * half, half)
            for place, (rows, columns) in enumerate(targets):
                begin = side * share + place * HEAD_DIM
                if rows is not None:
                    rows[pl.ds(row, half), :] = tile[:, begin : begin + HEAD_DIM]
                if columns is not None:
                    columns[0:HEAD_DIM, pl.ds(row, half)] = turned[begin : begin + HEAD_DIM]
        return carry

    lax.fori_loop(0, blocks, one, 0)


def tile_spans(marks, clips, index):
    first = marks[clips + SEGMENT] + index * Q_TILE
    begin = marks[clips + KEYS]
    low, low_end = clip_bounds(marks, clips, first)
    high_start, high = clip_bounds(marks, clips, first + Q_TILE - 1)
    low, low_end, high_start, high = (v - begin for v in (low, low_end, high_start, high))
    up = K_TILE - 1
    start = lax.div(low, K_TILE)
    stop = jnp.where(marks[clips + ACTIVE] > 0, lax.div(high + up, K_TILE), start)
    inner = lax.div(high_start + up, K_TILE)
    outer = lax.div(high, K_TILE)
    whole = (low == high_start) & (inner < outer) & (stop > start)
    inner = jnp.where(whole, inner, stop)
    outer = jnp.where(whole, outer, stop)
    places = first + lax.broadcasted_iota(jnp.int32, (1, Q_TILE), 1)
    starts, ends = clip_bounds(marks, clips, places)
    return (start, inner, outer, stop), starts - begin, ends - begin


def allowed(column, starts, ends):
    places = column + lax.broadcasted_iota(jnp.int32, (K_TILE, 1), 0)
    return (places >= starts) & (places < ends)


def over_spans(spans, step, state):
    for at in range(3):
        state = lax.fori_loop(spans[at], spans[at + 1], functools.partial(step, at != 1), state)
    return state


def attend_kernel(clips, halo, marks, packed_ref, out_ref, wide_ref, log_ref, query_t, keys, value_t):
    rows = wide_ref.shape[1]
    half = packed_ref.shape[1]
    block = 2 * half
    more = value_t.shape[0] - HEAD_DIM
    value_t[HEAD_DIM:] = jnp.where(
        lax.broadcasted_iota(jnp.int32, (more, value_t.shape[1]), 0) == 0, 1.0, 0.0
    ).astype(BF)
    unpack_heads(packed_ref, ((None, query_t), (keys, None), (None, value_t)))
    factor = HEAD_DIM ** (-0.5) * LOG2E

    def query_tile(index, carry):
        first = pl.multiple_of(index * Q_TILE, Q_TILE)
        q = query_t[:, pl.ds(halo * block + first, Q_TILE)]
        spans, starts, ends = tile_spans(marks, clips, index)

        def key_tile(masked, at, state):
            top, total = state
            column = pl.multiple_of(at * K_TILE, K_TILE)
            scores = plain_dot(keys[pl.ds(column, K_TILE), :], q) * factor
            if masked:
                scores = jnp.where(allowed(column, starts, ends), scores, LOW)
            new_top = jnp.maximum(top, jnp.max(scores, axis=0, keepdims=True))
            weight = jnp.exp2(scores - new_top).astype(BF)
            total = total * jnp.exp2(top - new_top) + plain_dot(
                value_t[:, pl.ds(column, K_TILE)], weight
            )
            return new_top, total

        top, total = over_spans(
            spans,
            key_tile,
            (
                jnp.full((1, Q_TILE), 0.5 * LOW, jnp.float32),
                jnp.zeros((HEAD_DIM + more, Q_TILE), jnp.float32),
            ),
        )
        mass = jnp.maximum(total[HEAD_DIM : HEAD_DIM + 1], 1e-37)
        attended = total[:HEAD_DIM] / mass
        wide_ref[:, pl.ds(first, Q_TILE)] = attended
        log_ref[:, pl.ds(first, Q_TILE)] = top + jnp.log2(mass)
        narrow = attended.T.astype(BF)
        for inner in range(Q_TILE // block):
            out_ref[index * (Q_TILE // block) + inner] = jnp.concatenate(
                [
                    narrow[inner * block : inner * block + half],
                    narrow[inner * block + half : (inner + 1) * block],
                ],
                axis=1,
            )
        return carry

    lax.fori_loop(0, rows // Q_TILE, query_tile, 0)


def attend(marks, packed, clips, halo):
    blocks, half, _ = packed.shape
    rows = (blocks - 2 * halo) * 2 * half
    key_rows = blocks * 2 * half
    return call(
        functools.partial(attend_kernel, clips, halo),
        [
            like((blocks - 2 * halo, half, 2 * HEAD_DIM), BF),
            like((HEAD_DIM, rows)),
            like((1, rows)),
        ],
        [
            pltpu.VMEM((HEAD_DIM, key_rows), BF),
            pltpu.VMEM((key_rows, HEAD_DIM), BF),
            pltpu.VMEM((HEAD_DIM + 16, key_rows), BF),
        ],
        (marks, packed),
        "attend",
        25 * 10**9,
    )


def attend_back_kernel(
    clips, halo, marks, packed_ref, grad_ref, wide_ref, log_ref, out_ref,
    query, query_t, keys, key_t, values, grads, grad_t, key_grads, value_grads,
):
    unpack_heads(packed_ref, ((query, query_t), (keys, key_t), (values, None)))
    unpack_heads(grad_ref, ((grads, grad_t),))
    blocks, half, _ = packed_ref.shape
    rows = wide_ref.shape[1]
    block = 2 * half
    scale = HEAD_DIM ** (-0.5)
    key_grads[...] = jnp.zeros_like(key_grads)
    value_grads[...] = jnp.zeros_like(value_grads)
    if halo:
        out_ref[...] = jnp.zeros_like(out_ref)

    def query_tile(index, carry):
        first = pl.multiple_of(index * Q_TILE, Q_TILE)
        own = pl.ds(halo * block + first, Q_TILE)
        q, q_t = query[own, :], query_t[:, own]
        g, g_t = grads[pl.ds(first, Q_TILE), :], grad_t[:, pl.ds(first, Q_TILE)]
        log_total = log_ref[:, pl.ds(first, Q_TILE)]
        delta = jnp.sum(
            g_t.astype(jnp.float32) * wide_ref[:, pl.ds(first, Q_TILE)], axis=0, keepdims=True
        )
        spans, starts, ends = tile_spans(marks, clips, index)

        def key_tile(masked, at, running):
            column = pl.multiple_of(at * K_TILE, K_TILE)
            here = pl.ds(column, K_TILE)
            probs = jnp.exp2(plain_dot(keys[here, :], q_t) * (scale * LOG2E) - log_total)
            if masked:
                probs = jnp.where(allowed(column, starts, ends), probs, 0.0)
            prob_grad = plain_dot(values[here, :], g_t)
            score_grad = (probs * (prob_grad - delta)).astype(BF)
            value_grads[here, :] += plain_dot(probs.astype(BF), g)
            key_grads[here, :] += plain_dot(score_grad, q)
            return running + plain_dot(key_t[:, here], score_grad)

        query_grad = over_spans(spans, key_tile, jnp.zeros((HEAD_DIM, Q_TILE), jnp.float32))
        query_grad = (query_grad.T * scale).astype(BF)
        for inner in range(Q_TILE // block):
            spot = halo + index * (Q_TILE // block) + inner
            out_ref[spot, :, 0:HEAD_DIM] = query_grad[inner * block : inner * block + half]
            out_ref[spot, :, 3 * HEAD_DIM : 4 * HEAD_DIM] = query_grad[
                inner * block + half : (inner + 1) * block
            ]
        return carry

    lax.fori_loop(0, rows // Q_TILE, query_tile, 0)

    def finish(spot, carry):
        for side in range(2):
            row = pl.multiple_of(spot * block + side * half, half)
            begin = (3 * side + 1) * HEAD_DIM
            out_ref[spot, :, begin : begin + 2 * HEAD_DIM] = jnp.concatenate(
                [key_grads[pl.ds(row, half), :] * scale, value_grads[pl.ds(row, half), :]], axis=1
            ).astype(BF)
        return carry

    lax.fori_loop(0, blocks, finish, 0)


def attend_back(marks, packed, grad, wide, log_total, clips, halo):
    blocks, half, lanes = packed.shape
    rows = wide.shape[1]
    key_rows = blocks * 2 * half
    return call(
        functools.partial(attend_back_kernel, clips, halo),
        [like((blocks, half, lanes), BF)],
        [
            pltpu.VMEM((key_rows, HEAD_DIM), BF),
            pltpu.VMEM((HEAD_DIM, key_rows), BF),
            pltpu.VMEM((key_rows, HEAD_DIM), BF),
            pltpu.VMEM((HEAD_DIM, key_rows), BF),
            pltpu.VMEM((key_rows, HEAD_DIM), BF),
            pltpu.VMEM((rows, HEAD_DIM), BF),
            pltpu.VMEM((HEAD_DIM, rows), BF),
            pltpu.VMEM((key_rows, HEAD_DIM), jnp.float32),
            pltpu.VMEM((key_rows, HEAD_DIM), jnp.float32),
        ],
        (marks, packed, grad, wide, log_total),
        "attend_back",
        35 * 10**9,
        limit=60,
    )[0]


TAPS = 16
SHOT = 384
TURNS = KERNEL // TAPS


def conv_weights_kernel(back, weight_ref, out_ref):
    group_width = out_ref.shape[1]
    if back:
        for group in range(GROUPS):
            lanes = slice(group_width * group, group_width * (group + 1))
            out_ref[group] = jnp.concatenate(
                [weight_ref[group_width * tap : group_width * (tap + 1), lanes] for tap in range(TAPS)],
                axis=1,
            )
    else:
        turned = weight_ref[...].T
        for group in range(GROUPS):
            out_ref[group] = turned[group_width * group : group_width * (group + 1)]


def conv_weights(back, weight, first, turns):
    width = weight.shape[1]
    group_width = width // GROUPS
    return call(
        functools.partial(conv_weights_kernel, back),
        [like((GROUPS, turns * group_width, TAPS * group_width), weight.dtype)],
        [],
        (weight,),
        "conv_weights_back" if back else "conv_weights",
        0,
        (turns,),
        [pl.BlockSpec((TAPS * group_width, width), lambda turn: (turn + first, 0))],
        (pl.BlockSpec((GROUPS, group_width, TAPS * group_width), lambda turn: (0, turn, 0)),),
    )[0]


def conv_kernel(back, clips, parts, marks, before_ref, rows_ref, after_ref, *refs):
    weight_refs, (out_ref, spaced, total) = refs[:parts], refs[parts:]
    group = pl.program_id(0)
    rows, width = rows_ref.shape
    half = KERNEL // 2
    long = rows + 2 * half
    group_width = width // GROUPS
    room = spaced.shape[1]
    places = marks[clips + BEGIN] - half + lax.broadcasted_iota(jnp.int32, (1, long), 1)
    ids = over_clips(
        clips,
        lambda clip, found: found + jnp.where(places >= marks[clip], 1, 0),
        jnp.zeros((1, long), jnp.int32),
    )
    ids = jnp.where((places >= 0) & (places < marks[clips + TOTAL]), ids, -1)

    def number_of(place):
        step = lambda clip, found: found + jnp.where(place >= marks[clip], 1, 0)
        return over_clips(clips, step, jnp.int32(0))

    first = number_of(marks[clips + BEGIN])
    count = number_of(marks[clips + BEGIN] + rows - 1) - first + 1

    @pl.when(group == 0)
    def _():
        turned = jnp.concatenate(
            [before_ref[...], rows_ref[...], after_ref[...]], axis=0
        ).astype(jnp.float32).T
        rest = jnp.zeros((width, room - long), jnp.float32)

        def of_clip(clip):
            return jnp.concatenate([jnp.where(ids == first + clip, turned, 0.0), rest], axis=1)

        spaced[...] = of_clip(0).astype(BF)

        def place(clip, carry):
            spaced[...] += pltpu.roll(of_clip(clip), clip * half, 1).astype(BF)
            return carry

        lax.fori_loop(1, count, place, 0)

    row = pl.multiple_of(group * group_width, group_width)
    shots = lax.div(rows + half * (count - 1) + SHOT - 1, SHOT)

    def shot(index, carry):
        base = pl.multiple_of(index * SHOT, 128)
        tile = spaced[pl.ds(row, group_width), pl.ds(base, SHOT + 2 * KERNEL)]
        moved = []
        for tap in range(TAPS):
            begin = TAPS - tap if back else tap
            moved.append(tile[:, begin : begin + SHOT + KERNEL])
        moved = jnp.concatenate(moved, axis=0)
        result = None
        turn = 0
        for weight_ref in weight_refs:
            product = plain_dot(weight_ref[0], moved)
            for inner in range(product.shape[0] // group_width):
                begin = (TURNS - 1 - turn if back else turn) * TAPS
                piece = product[inner * group_width : (inner + 1) * group_width, begin : begin + SHOT]
                result = piece if result is None else result + piece
                turn += 1
        total[pl.ds(row, group_width), pl.ds(base, SHOT)] = result
        return carry

    lax.fori_loop(0, shots, shot, 0)

    @pl.when(group == GROUPS - 1)
    def _():
        wide = total.shape[1]
        own = ids[:, half : half + rows]

        def collect(clip, carry):
            moved = pltpu.roll(total[...], lax.rem(wide - clip * half, wide), 1)[:, :rows]
            total[:, :rows] = jnp.where(own == first + clip, moved, total[:, :rows])
            return carry

        lax.fori_loop(1, count, collect, 0)
        out_ref[...] = total[:, :rows].T


def conv_rows(back, marks, before, value, after, weights, clips):
    rows, width = value.shape
    shots = -(-(rows + KERNEL // 2 * (clips - 1)) // SHOT)
    whole = lambda a: pl.BlockSpec(a.shape, lambda group: (0, 0))
    return call(
        functools.partial(conv_kernel, back, clips, len(weights)),
        [like((rows, width))],
        [
            pltpu.VMEM((width, SHOT * shots + 2 * KERNEL), BF),
            pltpu.VMEM((width, SHOT * shots), jnp.float32),
        ],
        (marks, before, value, after) + tuple(weights),
        "conv_back" if back else "conv",
        15 * 10**9,
        (GROUPS,),
        [SMEM_WHOLE, whole(before), whole(value), whole(after)]
        + [pl.BlockSpec((1,) + weight.shape[1:], lambda group: (group, 0, 0)) for weight in weights],
        (pl.BlockSpec((rows, width), lambda group: (0, 0)),),
        limit=48,
    )[0]


def taps_grad_kernel(
    clips, marks, both_ref, *refs
):
    half = KERNEL // 2
    out_refs, (inputs, spaced, input_cols, grad_cols) = refs[:-4], refs[-4:]
    group_width = inputs.shape[0]
    long = inputs.shape[1]
    blocks, _, block = both_ref.shape
    halo = (blocks - RING) // 2
    halo_rows = halo * block
    first = over_clips(
        clips,
        lambda clip, found: found + jnp.where(marks[clips + SEGMENT] >= marks[clip], 1, 0),
        jnp.int32(0),
    )
    origin = half + halo_rows
    span = input_cols.shape[1]

    def lay(first_row, begin_block, number, target, reach):
        for at in range(number):
            target[:, at * block : (at + 1) * block] = both_ref[
                begin_block + at, first_row : first_row + group_width
            ].astype(jnp.float32)
        target[:, number * block :] = jnp.zeros((group_width, long - number * block), jnp.float32)
        lanes = lax.broadcasted_iota(jnp.int32, (1, long), 1)
        places = marks[clips + SEGMENT] - reach + lanes
        held = lanes < number * block
        spaced[...] = jnp.zeros_like(spaced)

        def place(clip, carry):
            begin = jnp.where(clip > 0, marks[jnp.maximum(clip - 1, 0)], 0)
            keep = (places >= begin) & (places < marks[clip]) & held
            spaced[...] += pltpu.roll(
                jnp.where(keep, target[...], 0.0), origin - reach + half * (clip - first), 1
            )
            return carry

        lax.fori_loop(first, clips, place, 0)
        return spaced[...]

    laid = lay(0, 0, blocks, inputs, halo_rows)
    for turn in range(TURNS):
        begin = origin - half + turn * TAPS
        input_cols[turn * group_width : (turn + 1) * group_width, :] = laid[
            :, begin : begin + span
        ].astype(BF)
    laid = lay(group_width, halo, RING, inputs, 0)
    for tap in range(TAPS):
        grad_cols[tap * group_width : (tap + 1) * group_width, :] = laid[
            :, origin - tap : origin - tap + span
        ].astype(BF)
    result = row_dot(input_cols[...], grad_cols[...]).astype(BF)
    side_lanes = TAPS * group_width // 2
    even_core = marks[clips + CORE] == 0
    for piece in range(side_lanes // 128):
        values = []
        for place_at in range(2 * TURNS):
            turn, begin = place_at // 2, place_at % 2 * side_lanes + piece * 128
            values.append(result[turn * group_width : (turn + 1) * group_width, begin : begin + 128])
        store_pairs(out_refs, even_core, slice(piece * group_width, (piece + 1) * group_width), values)


def taps_grad(marks, both, shape, clips):
    blocks, two, block = both.shape
    group_width = two // 2
    half = KERNEL // 2
    halo_rows = (blocks - RING) // 2 * block
    span = -(-(RING * block + half * clips) // 128) * 128
    long = span + 2 * halo_rows + half + 2 * KERNEL
    long = -(-long // 128) * 128
    more = TAPS * group_width // 2 // 128 * group_width
    return call(
        functools.partial(taps_grad_kernel, clips),
        [like((n, more, 128), BF) for n in shape],
        [
            pltpu.VMEM((group_width, long), jnp.float32),
            pltpu.VMEM((group_width, long), jnp.float32),
            pltpu.VMEM((TURNS * group_width, span), BF),
            pltpu.VMEM((TAPS * group_width, span), BF),
        ],
        (marks, both),
        "taps_grad",
        10**10,
        limit=60,
    )


def weave_taps_kernel(own_ref, out_ref):
    group_width = out_ref.shape[1] // GROUPS
    taps = out_ref.shape[0] // group_width
    pieces = own_ref.shape[1] // group_width
    both = []
    for group in range(GROUPS):
        rows = own_ref[group].astype(jnp.float32)
        both.append(
            jnp.concatenate([rows[at * group_width : (at + 1) * group_width] for at in range(pieces)], axis=1)
        )
    for tap in range(taps):
        lanes = slice(tap * group_width, (tap + 1) * group_width)
        out_ref[tap * group_width : (tap + 1) * group_width, :] = jnp.concatenate(
            [value[:, lanes] for value in both], axis=1
        )


def weave_taps(own, taps, group_width):
    return call(
        weave_taps_kernel, [like((taps * group_width, GROUPS * group_width))], [], (own,), "weave_taps", 0
    )[0]


def add_shares_kernel(own_ref, other_ref, out_ref):
    out_ref[...] = (own_ref[...].astype(jnp.float32) + other_ref[...].astype(jnp.float32)).astype(BF)


def add_shares(own, other):
    return call(add_shares_kernel, [like(other.shape, BF)], [], (own, other), "add_shares", 0)[0]


def join_pair_kernel(clips, marks, taps_ref, other_ref, out_ref):
    rows = taps_ref.shape[1]
    first = marks[clips + CORE] == 0
    out_ref[:, :rows] = jnp.where(first, taps_ref[...], other_ref[...])
    out_ref[:, rows:] = jnp.where(first, other_ref[...], taps_ref[...])


def join_pair(marks, taps, other, clips):
    chips, rows, lanes = taps.shape
    return call(
        functools.partial(join_pair_kernel, clips),
        [like((chips, 2 * rows, lanes), BF)],
        [],
        (marks, taps, other),
        "join_pair",
        0,
    )[0]


SHARE = 384
PIECE = 128


def norm_parts(values):
    center = values - jnp.mean(values, axis=-1, keepdims=True)
    inverse = lax.rsqrt(jnp.mean(center * center, axis=-1, keepdims=True) + EPS)
    return center * inverse, inverse


def norm_back(unit, inverse, scales, grad):
    scaled = grad * scales
    back = inverse * (
        scaled
        - jnp.mean(scaled, axis=-1, keepdims=True)
        - unit * jnp.mean(scaled * unit, axis=-1, keepdims=True)
    )
    return back, row_sum(grad * unit), row_sum(grad)


def row_sum(values):
    return jnp.sum(values, axis=0, keepdims=True)


def gelu_both(values):
    below = 0.5 + 0.5 * lax.erf(values * 0.7071067811865476)
    bell = jnp.exp(-0.5 * values * values) * 0.3989422804014327
    return values * below, below + values * bell


def store_turned(values_b, out_ref, first):
    group_width = values_b.shape[1] // GROUPS
    turned = values_b.T
    for group in range(GROUPS):
        out_ref[group, first : first + group_width] = turned[group * group_width : (group + 1) * group_width]


def same_clip_next(marks, clips, rows):
    following = marks[clips + BEGIN] + 1 + lax.broadcasted_iota(jnp.int32, (rows, 1), 0)
    step = lambda clip, other: jnp.maximum(other, jnp.where(following == marks[clip], 1, 0))
    return over_clips(clips, step, jnp.zeros((rows, 1), jnp.int32)) == 0


def stem_kernel(
    clips, marks, samples_ref, next_ref, weight_ref, gain_ref, bias_ref, proj_ref, gains_ref, biases_ref,
    start_ref, start_b_ref, pre_ref, normed_ref, unfold_ref, table_ref, wide,
):
    rows, chans = pre_ref.shape
    table_ref[0:3] = gains_ref[...]
    table_ref[3:12] = biases_ref[...]
    last = lax.broadcasted_iota(jnp.int32, (rows, 1), 0) == rows - 1
    same = same_clip_next(marks, clips, rows)
    for lane in range(0, chans, PIECE):
        lanes = slice(lane, lane + PIECE)
        wide[...] = samples_ref[:, lanes].astype(jnp.float32)
        even = wide[pl.ds(0, rows, stride=2), :]
        unfold_ref[:, lanes] = even.astype(BF)
        unfold_ref[:, chans + lane : chans + lane + PIECE] = wide[pl.ds(1, rows, stride=2), :].astype(BF)
        moved = jnp.where(last, next_ref[:, lanes].astype(jnp.float32), pltpu.roll(even, rows - 1, 0))
        unfold_ref[:, 2 * chans + lane : 2 * chans + lane + PIECE] = jnp.where(same, moved, 0.0).astype(BF)
    pre = plain_dot(unfold_ref[...], weight_ref[...])
    pre_ref[...] = pre
    unit, _ = norm_parts(gelu_both(pre)[0])
    normed = (unit * gain_ref[...] + bias_ref[...]).astype(BF)
    normed_ref[...] = normed
    start = plain_dot(normed, proj_ref[...]) + table_ref[3:4]
    start_ref[...] = start
    start_b_ref[...] = start.astype(BF)


def stem(marks, samples, next_row, weight, gain, bias, proj, gains, biases, clips):
    rows = samples.shape[0] // 2
    chans, width = proj.shape
    return call(
        functools.partial(stem_kernel, clips),
        [
            like((rows, width)), like((rows, width), BF),
            like((rows, chans)), like((rows, chans), BF), like((rows, 3 * chans), BF), like((12, width)),
        ],
        [pltpu.VMEM((2 * rows, PIECE), jnp.float32)],
        (marks, samples, next_row, weight, gain, bias, proj, gains, biases),
        "stem",
        6 * 10**9,
    )


def project_kernel(conv_ref, start_ref, table_ref, weight_ref, hidden_ref, packed_ref):
    rows, width = start_ref.shape
    half = rows // 2
    mixed = start_ref[...] + gelu_both(conv_ref[...] + table_ref[4:5])[0]
    unit, _ = norm_parts(mixed)
    hidden = unit * table_ref[0:1] + table_ref[5:6]
    hidden_ref[...] = hidden
    hidden_b = hidden.astype(BF)
    shifts = (table_ref[6:7], jnp.zeros((1, width), jnp.float32), table_ref[7:8])
    parts = [
        (plain_dot(hidden_b, weight_ref[:, at * width : (at + 1) * width]) + shift).astype(BF)
        for at, shift in enumerate(shifts)
    ]
    heads = width // HEAD_DIM
    for head in range(heads):
        lanes = slice(head * HEAD_DIM, (head + 1) * HEAD_DIM)
        packed_ref[head] = jnp.concatenate(
            [part[:half, lanes] for part in parts] + [part[half:, lanes] for part in parts], axis=1
        )
    for head in range(heads, RING):
        packed_ref[head] = jnp.zeros_like(packed_ref[head])


def project_heads(conv_sum, start, table, weight):
    rows, width = start.shape
    return call(
        project_kernel,
        [like((rows, width)), like((RING, rows // 2, 6 * HEAD_DIM), BF)],
        [],
        (conv_sum, start, table, weight),
        "project_heads",
        6 * 10**9,
    )


def middle_kernel(
    heads_ref, hidden_ref, table_ref, out_weight_ref, in_ref, in_bias_ref, back_ref, out_grad_ref,
    layer_ref, grad_heads_ref, grad_second_ref, out_part_ref, sums_ref, in_bias_grad_ref, joined_ref,
    attended, before, second, second_b, second_t, inner_b, slope, total, grad_last, grad_last_b,
    joined, sems,
):
    step = pl.program_id(0)
    rows, width = hidden_ref.shape
    half = rows // 2
    chunk = in_ref.shape[1]
    chunks = pl.num_programs(0) // 2
    heads = width // HEAD_DIM
    shares = joined_ref.shape[0]
    in_rows = width // shares
    back_rows = chunk * chunks // shares
    owners = chunk // back_rows

    def in_copy(at):
        place = (slice(None), pl.ds(pl.multiple_of(at * in_rows, 16), in_rows))
        return pltpu.make_async_copy(joined.at[place], joined_ref.at[place], sems.at[0, at])

    def back_copy(at):
        place = (pl.ds(at * owners, owners), pl.ds(in_rows * chunks, joined_ref.shape[1] - in_rows * chunks))
        return pltpu.make_async_copy(joined.at[place], joined_ref.at[place], sems.at[1, at])

    @pl.when(step == 0)
    def _():
        for head in range(heads):
            lanes = slice(head * HEAD_DIM, (head + 1) * HEAD_DIM)
            attended[:half, lanes] = heads_ref[head, :, :HEAD_DIM]
            attended[half:, lanes] = heads_ref[head, :, HEAD_DIM:]
        value = hidden_ref[...] + plain_dot(attended[...], out_weight_ref[...]) + table_ref[8:9]
        before[...] = value
        unit, _ = norm_parts(value)
        value = unit * table_ref[1:2] + table_ref[9:10]
        second[...] = value
        second_b[...] = value.astype(BF)
        second_t[...] = value.T.astype(BF)
        total[...] = jnp.zeros_like(total)

    @pl.when(step < chunks)
    def _():
        at = pl.multiple_of(step * chunk, chunk)
        value, back = gelu_both(plain_dot(second_b[...], in_ref[...]) + in_bias_ref[:, pl.ds(at, chunk)])
        value_b = value.astype(BF)
        inner_b[step] = value_b
        slope[step] = back
        total[...] += plain_dot(value_b, back_ref[...])

    @pl.when(step == chunks - 1)
    def _():
        unit, inverse = norm_parts(second[...] + total[...] + table_ref[10:11])
        layer_ref[...] = (unit * table_ref[2:3] + table_ref[11:12]).astype(BF)
        back, gain, bias = norm_back(unit, inverse, table_ref[2:3], out_grad_ref[...].astype(jnp.float32))
        grad_last[...] = back
        grad_last_b[...] = back.astype(BF)
        total[...] = back
        sums_ref[0:1] = gain
        sums_ref[1:2] = bias
        sums_ref[2:3] = row_sum(back)

    @pl.when(step >= chunks)
    def _():
        turn = step - chunks
        at = pl.multiple_of(turn * chunk, chunk)
        grad = row_dot(grad_last_b[...], back_ref[...]) * slope[turn]
        in_bias_grad_ref[:, pl.ds(at, chunk)] = row_sum(grad)
        grad_b = grad.astype(BF)
        total[...] += row_dot(grad_b, in_ref[...])
        product = plain_dot(second_t[...], grad_b).astype(BF)
        for share in range(shares):
            joined[share, pl.ds(pl.multiple_of(turn * in_rows, 16), in_rows), :] = product[
                share * in_rows : (share + 1) * in_rows
            ]
        in_copy(turn).start()
        product = over_rows_dot(inner_b[turn], grad_last_b[...]).astype(BF)
        for owner in range(owners):
            for place in range(width // SHARE):
                begin = in_rows * chunks + place * back_rows
                joined[turn * owners + owner, begin : begin + back_rows, :] = product[
                    owner * back_rows : (owner + 1) * back_rows, place * SHARE : (place + 1) * SHARE
                ]
        back_copy(turn).start()

    @pl.when(step == 2 * chunks - 1)
    def _():
        unit, inverse = norm_parts(before[...])
        back, gain, bias = norm_back(unit, inverse, table_ref[1:2], total[...])
        grad_second_ref[...] = back
        sums_ref[3:4] = row_sum(back)
        sums_ref[4:5] = gain
        sums_ref[5:6] = bias
        sums_ref[6:8] = jnp.zeros((2, width), jnp.float32)
        back_b = back.astype(BF)
        grads = row_dot(back_b, out_weight_ref[...]).astype(BF)
        for head in range(heads):
            lanes = slice(head * HEAD_DIM, (head + 1) * HEAD_DIM)
            grad_heads_ref[head] = jnp.concatenate([grads[:half, lanes], grads[half:, lanes]], axis=1)
        for head in range(heads, RING):
            grad_heads_ref[head] = jnp.zeros_like(grad_heads_ref[head])
        product = over_rows_dot(attended[...], back_b).astype(BF)
        for share in range(shares):
            for place in range(width // SHARE):
                out_part_ref[share, place * in_rows : (place + 1) * in_rows, :] = product[
                    share * in_rows : (share + 1) * in_rows, place * SHARE : (place + 1) * SHARE
                ]

        def finish(at, carry):
            in_copy(at).wait()
            back_copy(at).wait()
            return carry

        lax.fori_loop(0, chunks, finish, 0)


def middle(heads, hidden, table, out_weight, ffn_in, in_bias, ffn_out, out_grad, count):
    rows, width = hidden.shape
    inner = ffn_in.shape[1]
    chunk = SHARE
    chunks = inner // chunk
    own = lambda shape: pl.BlockSpec(shape, lambda step: (0,) * len(shape))
    outs = [
        like((rows, width), BF),
        like((RING, rows // 2, 2 * HEAD_DIM), BF),
        like((rows, width)),
        like((count, width // count * width // SHARE, SHARE), BF),
        like((8, width)),
        like((1, inner)),
        like((count, 2 * width // count * inner // SHARE, SHARE), BF),
    ]
    args = (heads, hidden, table, out_weight, ffn_in, in_bias, ffn_out, out_grad)
    in_specs = [own(a.shape) for a in args]
    in_specs[4] = pl.BlockSpec((width, chunk), lambda step: (0, step % chunks))
    in_specs[6] = pl.BlockSpec((chunk, width), lambda step: (step % chunks, 0))
    out_specs = [own(o.shape) for o in outs]
    out_specs[6] = pl.BlockSpec(memory_space=pl.ANY)
    scratch = [
        pltpu.VMEM((rows, width), BF),
        pltpu.VMEM((rows, width), jnp.float32),
        pltpu.VMEM((rows, width), jnp.float32),
        pltpu.VMEM((rows, width), BF),
        pltpu.VMEM((width, rows), BF),
        pltpu.VMEM((chunks, rows, chunk), BF),
        pltpu.VMEM((chunks, rows, chunk), jnp.float32),
        pltpu.VMEM((rows, width), jnp.float32),
        pltpu.VMEM((rows, width), jnp.float32),
        pltpu.VMEM((rows, width), BF),
        pltpu.VMEM(outs[6].shape, BF),
        pltpu.SemaphoreType.DMA((2, chunks)),
    ]
    return call(
        middle_kernel, outs, scratch, args, "middle", 2 * 10**10, (2 * chunks,), in_specs, tuple(out_specs)
    )


def after_heads_kernel(
    packed_ref, grad_second_ref, hidden_ref, conv_ref, start_ref, table_ref, weight_ref, out_part_ref,
    mixed_ref, conv_b_ref, groups_ref, joined_ref, sums_ref, grads,
):
    rows, width = hidden_ref.shape
    half = rows // 2
    heads = width // HEAD_DIM
    shares = joined_ref.shape[0]
    own_rows = width // shares
    for head in range(heads):
        tile = packed_ref[head]
        for part in range(3):
            lanes = slice(part * width + head * HEAD_DIM, part * width + (head + 1) * HEAD_DIM)
            grads[:half, lanes] = tile[:, part * HEAD_DIM : (part + 1) * HEAD_DIM]
            grads[half:, lanes] = tile[:, (part + 3) * HEAD_DIM : (part + 4) * HEAD_DIM]
    hidden_t = hidden_ref[...].T.astype(BF)
    blocks = 3 * width // SHARE
    for place in range(blocks):
        lanes = slice(place * SHARE, (place + 1) * SHARE)
        product = plain_dot(hidden_t, grads[:, lanes]).astype(BF)
        for share in range(shares):
            joined_ref[share, place * own_rows : (place + 1) * own_rows, :] = product[
                share * own_rows : (share + 1) * own_rows
            ]
    for share in range(shares):
        joined_ref[share, blocks * own_rows :, :] = out_part_ref[share]
    back = grad_second_ref[...] + row_dot(grads[...], weight_ref[...])
    value, slope = gelu_both(conv_ref[...] + table_ref[4:5])
    unit, inverse = norm_parts(start_ref[...] + value)
    mixed, gain, bias = norm_back(unit, inverse, table_ref[0:1], back)
    mixed_ref[...] = mixed
    conv = mixed * slope
    conv_b = conv.astype(BF)
    conv_b_ref[...] = conv_b
    store_turned(start_ref[...].astype(BF), groups_ref, 0)
    store_turned(conv_b, groups_ref, width // GROUPS)
    sums_ref[0:1] = gain
    sums_ref[1:2] = bias
    sums_ref[2:3] = row_sum(conv)
    sums_ref[3:4] = row_sum(grads[:, :width].astype(jnp.float32))
    sums_ref[4:5] = row_sum(grads[:, 2 * width :].astype(jnp.float32))
    sums_ref[5:8] = jnp.zeros((3, width), jnp.float32)


def after_heads(packed, grad_second, hidden, conv_sum, start, table, weight, out_part):
    rows, width = hidden.shape
    shares = out_part.shape[0]
    return call(
        after_heads_kernel,
        [
            like((rows, width)), like((rows, width), BF),
            like((GROUPS, 2 * width // GROUPS, rows), BF),
            like((shares, out_part.shape[1] + width // shares * 3 * width // SHARE, SHARE), BF),
            like((8, width)),
        ],
        [pltpu.VMEM((rows, 3 * width), BF)],
        (packed, grad_second, hidden, conv_sum, start, table, weight, out_part),
        "after_heads",
        6 * 10**9,
    )


def stem_back_kernel(
    clips, marks, input_ref, mixed_ref, normed_ref, pre_ref, unfold_ref, weight_ref, gain_ref, proj_ref,
    middle_sums_ref, inner_sums_ref, after_sums_ref,
    samples_ref, carried_ref, *refs,
):
    rows, chans = pre_ref.shape
    width = input_ref.shape[1]
    joined_refs, (table, spread, woven) = refs[:-3], refs[-3:]
    shares = RING
    even_core = marks[clips + CORE] == 0
    start = mixed_ref[...] + input_ref[...]
    start_b = start.astype(BF)

    def share_out(product, begin):
        own, columns = product.shape[0] // shares, product.shape[1]
        for place in range(columns // PIECE):
            at = begin + place * own
            store_pairs(
                joined_refs,
                even_core,
                slice(at, at + own),
                [
                    product[share * own : (share + 1) * own, place * PIECE : (place + 1) * PIECE]
                    for share in range(shares)
                ],
            )
        return begin + own * columns // PIECE

    at = share_out(over_rows_dot(normed_ref[...], start_b).astype(BF), 0)
    value, slope = gelu_both(pre_ref[...])
    unit, inverse = norm_parts(value)
    feature, gain_sum, bias_sum = norm_back(
        unit, inverse, gain_ref[...], row_dot(start_b, proj_ref[...])
    )
    pre_b = (feature * slope).astype(BF)
    taps_t = over_rows_dot(unfold_ref[...], pre_b).astype(BF)
    at = share_out(taps_t, at)
    first = row_dot(pre_b, weight_ref[:chans])
    same = same_clip_next(marks, clips, rows)
    follow = jnp.where(same, row_dot(pre_b, weight_ref[2 * chans :]), 0.0)
    carried_ref[...] = follow[rows - 1 :]
    moved = pltpu.roll(follow, 1, 0)
    top = lax.broadcasted_iota(jnp.int32, (rows, 1), 0) == 0
    even = first + jnp.where(top, 0.0, moved)
    odd = row_dot(pre_b, weight_ref[chans : 2 * chans])
    for lane in range(0, chans, PIECE):
        woven[pl.ds(0, rows, stride=2), :] = even[:, lane : lane + PIECE]
        woven[pl.ds(1, rows, stride=2), :] = odd[:, lane : lane + PIECE]
        samples_ref[:, lane : lane + PIECE] = woven[...]
    table[0:1] = after_sums_ref[0:1]
    table[1:2] = middle_sums_ref[4:5]
    table[2:3] = middle_sums_ref[0:1]
    table[3:4] = row_sum(start)
    table[4:5] = after_sums_ref[2:3]
    table[5:6] = after_sums_ref[1:2]
    table[6:7] = after_sums_ref[3:4]
    table[7:8] = after_sums_ref[4:5]
    table[8:9] = middle_sums_ref[3:4]
    table[9:10] = middle_sums_ref[5:6]
    table[10:11] = middle_sums_ref[2:3]
    table[11:12] = middle_sums_ref[1:2]
    spread[...] = jnp.zeros_like(spread)
    own, own_chans = width // shares, chans // shares
    own_inner = inner_sums_ref.shape[1] // shares
    for share in range(shares):
        spread[share, 0:12, 0:own] = table[:, share * own : (share + 1) * own]
        for place in range(-(-own_inner // PIECE)):
            length = min(PIECE, own_inner - place * PIECE)
            begin = share * own_inner + place * PIECE
            spread[share, 12 + place : 13 + place, 0:length] = inner_sums_ref[:, begin : begin + length]
        lanes = slice(share * own_chans, (share + 1) * own_chans)
        spread[share, 14:15, 0:own_chans] = gain_sum[:, lanes]
        spread[share, 15:16, 0:own_chans] = bias_sum[:, lanes]
    store_pairs(
        joined_refs, even_core, slice(at, at + 16), [spread[share].astype(BF) for share in range(shares)]
    )


def stem_back(marks, input_grad, mixed, normed, pre, unfold, weight, gain, proj, sums, shares, clips):
    rows, chans = pre.shape
    width = input_grad.shape[1]
    pieces = (chans // RING * width + 3 * chans // RING * chans) // PIECE + 16
    return call(
        functools.partial(stem_back_kernel, clips),
        [like((2 * rows, chans)), like((1, chans))] + [like((n, pieces, PIECE), BF) for n in shares],
        [pltpu.VMEM((12, width), jnp.float32), pltpu.VMEM((RING, 16, PIECE), jnp.float32),
         pltpu.VMEM((2 * rows, PIECE), jnp.float32)],
        (marks, input_grad, mixed, normed, pre, unfold, weight, gain, proj) + sums,
        "stem_back",
        6 * 10**9,
    )


def from_behind(value, axis, steps):
    count = lax.axis_size(axis)
    initial, last = (max(0, -steps), min(count, count - steps))
    return lax.ppermute(value, axis, [(source, source + steps) for source in range(initial, last)])


def edges(value, width):
    length = value.shape[0]
    return from_behind(value[length - width :], "seq", 1), from_behind(value[:width], "seq", -1)


def near_groups():
    size = lax.axis_size("seq")
    return [[base + i for i in range(RING)] for base in range(0, size, RING)]


def swap(value):
    groups = None if lax.axis_size("seq") == RING else near_groups()
    return lax.all_to_all(value, "seq", 0, 0, axis_index_groups=groups)


def with_far_blocks(value, count):
    if lax.axis_size("seq") == RING or count == 0:
        return value
    before = from_behind(value[value.shape[0] - count :], "seq", RING)
    after = from_behind(value[:count], "seq", -RING)
    return jnp.concatenate([before, value, after], axis=0)


def fold_far_blocks(value, count):
    if lax.axis_size("seq") == RING or count == 0:
        return value
    own = value[count : value.shape[0] - count]
    to_before = from_behind(value[:count], "seq", -RING)
    to_after = from_behind(value[value.shape[0] - count :], "seq", RING)
    wide = own.astype(jnp.float32)
    wide = wide.at[wide.shape[0] - count :].add(to_before.astype(jnp.float32))
    wide = wide.at[:count].add(to_after.astype(jnp.float32))
    return wide.astype(value.dtype)


def other_stream(share):
    return lax.ppermute(share, "rep", [(0, 1), (1, 0)])


def sum_pair(share):
    return share.astype(jnp.float32) + other_stream(share).astype(jnp.float32)


def spread_out(total, sizes, lanes):
    out, at = [], 0
    for rows, columns in sizes:
        parts = []
        for _ in range(columns // lanes):
            parts.append(total[at : at + rows])
            at += rows
        out.append(jnp.concatenate(parts, axis=1))
    return out


def regroup(joined, blocks):
    count = lax.axis_size("seq")
    if count == RING:
        return joined
    parts = count // RING
    lanes = joined.shape[2]
    out, at = [], 0
    for number, rows in blocks:
        piece = joined[:, at : at + number * rows]
        at += number * rows
        piece = piece.reshape(RING, number, parts, rows // parts, lanes).transpose(0, 2, 1, 3, 4)
        out.append(piece.reshape(count, number * rows // parts, lanes))
    return jnp.concatenate(out, axis=1)


def regroup_small(small, widths):
    count = lax.axis_size("seq")
    if count == RING:
        return small
    parts = count // RING
    own, own_inner, own_chans = widths
    lanes = small.shape[2]
    table = small[:, :12, : own * parts].reshape(RING, 12, parts, own).transpose(0, 2, 1, 3)
    table = jnp.pad(table.reshape(count, 12, own), ((0, 0), (0, 0), (0, lanes - own)))
    wide = small[:, 12:14].reshape(RING, 2 * lanes)[:, : own_inner * parts].reshape(count, own_inner)
    wide = jnp.pad(wide, ((0, 0), (0, 2 * lanes - own_inner))).reshape(count, 2, lanes)
    stems = small[:, 14:16, : own_chans * parts].reshape(RING, 2, parts, own_chans).transpose(0, 2, 1, 3)
    stems = jnp.pad(stems.reshape(count, 2, own_chans), ((0, 0), (0, 0), (0, lanes - own_chans)))
    return jnp.concatenate([table, wide, stems], axis=1)


def over_seq(joined):
    return lax.psum_scatter(joined, "seq", scatter_dimension=0, tiled=False).astype(jnp.bfloat16)


def local(
    samples,
    clip_lengths,
    stem_weight,
    stem_gain,
    stem_bias,
    proj_weight,
    pos_weight,
    norm_gains,
    biases,
    attn_in,
    attn_out,
    ffn_in,
    ffn_in_bias,
    ffn_out,
    out_grad,
):
    rows_dev = out_grad.shape[1]
    width = attn_out.shape[0]
    chans = stem_weight.shape[1]
    inner = ffn_in.shape[1]
    group_width = width // GROUPS
    count = lax.axis_size("seq")
    place = lax.axis_index("seq")
    total = rows_dev * count
    begin = place * rows_dev
    ends = jnp.cumsum(clip_lengths[0])
    clips = ends.shape[0]
    half = KERNEL // 2
    far = 0 if count == RING else -(-MAXLEN // rows_dev)
    segment_begin = (place // RING) * RING * rows_dev
    active = jnp.where(place % RING < HEADS, 1, 0)
    marks = jnp.concatenate(
        [ends, jnp.stack([jnp.int32(total), begin, segment_begin, segment_begin - far * rows_dev, active, place % 2])]
    ).astype(jnp.int32)
    next_row = from_behind(samples[0, :1], "seq", -1)
    one_weights = conv_weights(False, pos_weight, 0, TURNS // 2)
    next_row, one_weights = lax.optimization_barrier((next_row, one_weights))
    start_x, start_b, stem_pre, normed_b, unfold, table = stem(
        marks, samples[0], next_row, stem_weight, stem_gain[None], stem_bias[None], proj_weight,
        norm_gains.T, biases.T, clips,
    )
    before, after = edges(start_b, half)
    rest_source, _ = lax.optimization_barrier((pos_weight, table))
    rest_weights = conv_weights(False, rest_source, TURNS // 2, TURNS // 2)
    before, after, rest_weights = lax.optimization_barrier((before, after, rest_weights))
    conv_sum = conv_rows(False, marks, before, start_b, after, (one_weights, rest_weights), clips)
    hidden, packed = project_heads(conv_sum, start_x, table, attn_in)
    back_source, _ = lax.optimization_barrier((pos_weight, hidden))
    packed = with_far_blocks(swap(packed), far)
    back_weights = conv_weights(True, back_source, 0, TURNS)
    packed, back_weights = lax.optimization_barrier((packed, back_weights))
    attended_heads, wide, log_total = attend(marks, packed, clips, far)
    layer_out, grad_heads, grad_pre_second, out_part, middle_sums, inner_sums, ffn_joined = middle(
        swap(attended_heads), hidden, table, attn_out, ffn_in, ffn_in_bias[None], ffn_out, out_grad[0],
        RING,
    )
    near_rows, near_chans, near_inner = width // RING, chans // RING, inner // RING
    grad_heads = swap(grad_heads)
    ffn_share = over_seq(
        regroup(ffn_joined, [(inner // SHARE, near_rows), (width // SHARE, near_inner)])
    )
    packed_grad = attend_back(marks, packed, grad_heads, wide, log_total, clips, far)
    grad_mixed, grad_conv_b, grad_packed, attn_joined, after_sums = after_heads(
        swap(fold_far_blocks(packed_grad, far)), grad_pre_second, hidden, conv_sum, start_x, table,
        attn_in, out_part,
    )
    before, after = edges(grad_conv_b, half)
    before, after, grad_packed = lax.optimization_barrier((before, after, grad_packed))
    grad_groups = swap(grad_packed)
    input_grad = conv_rows(True, marks, before, grad_conv_b, after, (back_weights,), clips)
    input_grad, grad_groups, ffn_share = lax.optimization_barrier((input_grad, grad_groups, ffn_share))
    attn_share = over_seq(regroup(attn_joined, [(4 * width // SHARE, near_rows)]))
    shape = (RING // 2,) * 2 if count == RING else (RING,)
    sample_grad, carried, *stem_shares = stem_back(
        marks, input_grad, grad_mixed, normed_b, stem_pre, unfold, stem_weight, stem_gain[None],
        proj_weight, (middle_sums, inner_sums, after_sums), shape, clips,
    )
    carried = from_behind(carried, "seq", 1)
    own = width // count
    own_chans = chans // count
    own_taps = KERNEL // count
    grad_ffn = spread_out(sum_pair(ffn_share), [(own, inner), (inner // count, width)], SHARE)
    if count == RING:
        pairs = [(i, i ^ 1) for i in range(count)]
        alike = [list(range(core, count, 2)) for core in range(2)]
        stem_joined = add_shares(stem_shares[0], lax.ppermute(stem_shares[1], "seq", pairs))
        stem_joined, grad_groups = lax.optimization_barrier((stem_joined, grad_groups))
        received = lax.all_to_all(stem_joined, "seq", 0, 0, axis_index_groups=alike)
        taps, sent_taps = taps_grad(marks, grad_groups, shape, clips)
        taps = join_pair(marks, taps, lax.ppermute(sent_taps, "seq", pairs), clips)
        taps = add_shares(taps, other_stream(taps))
        taps, received, grad_ffn = lax.optimization_barrier((taps, received, grad_ffn))
        pos_pieces = lax.all_to_all(taps, "seq", 0, 0, axis_index_groups=alike)
        pos_pieces = pos_pieces.reshape(GROUPS, -1, PIECE)
    else:
        (taps,) = taps_grad(marks, with_far_blocks(grad_groups, 1), shape, clips)
        taps = add_shares(taps, other_stream(taps))
        stem_joined = stem_shares[0]
        stem_joined = jnp.concatenate(
            [
                regroup(
                    stem_joined[:, :-16],
                    [(width // PIECE, near_chans), (chans // PIECE, 3 * near_chans)],
                ),
                regroup_small(stem_joined[:, -16:], (own, inner // count, own_chans)),
            ],
            axis=1,
        )
        received = lax.all_to_all(stem_joined, "seq", 0, 0)
        segments = count // RING
        by_tap = taps.reshape(2 * TURNS, 3, group_width, PIECE).transpose(0, 2, 1, 3)
        by_tap = by_tap.reshape(2 * TURNS, group_width, TAPS // 2, group_width)
        by_tap = by_tap.transpose(0, 2, 1, 3).reshape(segments, -1, 2 * PIECE)
        across = [[low_at + RING * j for j in range(segments)] for low_at in range(RING)]
        by_tap = lax.all_to_all(by_tap, "seq", 0, 0, axis_index_groups=across)
        by_tap = jnp.sum(by_tap.astype(jnp.float32), axis=0).astype(jnp.bfloat16)
        by_tap = by_tap.reshape(RING, own_taps, group_width, group_width).transpose(0, 2, 1, 3)
        pos_pieces = swap(by_tap.reshape(RING, group_width, own_taps * group_width))
    pos_pieces, attn_share = lax.optimization_barrier((pos_pieces, attn_share))
    pos_grad = weave_taps(pos_pieces, own_taps, group_width)
    stem_total = sum_pair(jnp.sum(received.astype(jnp.float32), axis=0).astype(jnp.bfloat16))
    grad_proj, grad_stem = spread_out(
        stem_total[:-16], [(own_chans, width), (3 * own_chans, chans)], PIECE
    )
    small = stem_total[-16:]
    grad_ffn_in, grad_ffn_out = grad_ffn
    grad_attn_in, grad_attn_out = spread_out(
        sum_pair(attn_share), [(own, 3 * width), (own, width)], SHARE
    )
    sample_grad = sample_grad.at[:1].add(carried)
    return (
        layer_out[None],
        sample_grad[None],
        grad_stem,
        small[14, :own_chans],
        small[15, :own_chans],
        grad_proj,
        pos_grad,
        small[:3, :own].T,
        small[3:12, :own].T,
        grad_attn_in,
        grad_attn_out,
        grad_ffn_in,
        small[12:14].reshape(-1)[: inner // count],
        grad_ffn_out,
    )


def solution(mesh):
    streams = P("rep", "seq", None)
    rows = P("seq", None)
    return jax.shard_map(
        local,
        mesh=mesh,
        in_specs=(streams, P("rep", None)) + (P(),) * 12 + (streams,),
        out_specs=(streams, streams, rows, P("seq"), P("seq"))
        + (rows,) * 7
        + (P("seq"), rows),
        check_vma=False,
    )
```

```python
import functools

import jax
import jax.numpy as jnp
from jax import lax
from jax.experimental import pallas as pl
from jax.experimental.pallas import tpu as pltpu
from jax.sharding import PartitionSpec as P

HEADS = 12
KERNEL = 128
GROUPS = 16
MAXLEN = 1536
RING = 16
HEAD_DIM = 64
EPS = 1e-05
BF = jnp.bfloat16
VMEM_WHOLE = pl.BlockSpec(memory_space=pltpu.VMEM)
SMEM_WHOLE = pl.BlockSpec(memory_space=pltpu.SMEM)
TOTAL, BEGIN, SEGMENT, KEYS, ACTIVE, CORE, REP = range(7)


def row_dot(left, right):
    return lax.dot_general(left, right, (((1,), (1,)), ((), ())), preferred_element_type=jnp.float32)


def plain_dot(left, right):
    return lax.dot_general(left, right, (((1,), (0,)), ((), ())), preferred_element_type=jnp.float32)


def over_rows_dot(left, right):
    return lax.dot_general(left, right, (((0,), (0,)), ((), ())), preferred_element_type=jnp.float32)


def store_pairs(refs, even, rows, values):
    if len(refs) == 1:
        for share, value in enumerate(values):
            refs[0][share, rows, :] = value
        return
    kept, sent = refs
    for at in range(len(values) // 2):
        first, second = values[2 * at], values[2 * at + 1]
        kept[at, rows, :] = jnp.where(even, first, second)
        sent[at, rows, :] = jnp.where(even, second, first)


def over_clips(clips, step, state):
    if clips <= 8:
        for clip in range(clips):
            state = step(clip, state)
        return state
    return lax.fori_loop(0, clips, step, state)


def clip_bounds(marks, clips, places):
    def step(clip, state):
        first, end = state
        mark = marks[clip]
        return (
            jnp.maximum(first, jnp.where(mark <= places, mark, 0)),
            jnp.minimum(end, jnp.where(mark > places, mark, marks[clips + TOTAL])),
        )

    return over_clips(clips, step, (jnp.zeros_like(places), jnp.zeros_like(places) + marks[clips + TOTAL]))


def like(shape, dtype=jnp.float32):
    return jax.ShapeDtypeStruct(shape, dtype)


def call(
    kernel, outs, scratch, args, name, flops, grid=None, in_specs=None, out_specs=None, limit=56, aliases=None
):
    size = sum(a.size * a.dtype.itemsize for a in args)
    size += sum(o.size * o.dtype.itemsize for o in outs)
    extra = {} if grid is None else {"grid": grid}
    return pl.pallas_call(
        kernel,
        out_shape=tuple(outs),
        in_specs=in_specs or [SMEM_WHOLE if a.dtype == jnp.int32 else VMEM_WHOLE for a in args],
        out_specs=out_specs or (VMEM_WHOLE,) * len(outs),
        scratch_shapes=scratch,
        compiler_params=pltpu.CompilerParams(vmem_limit_bytes=limit << 20),
        cost_estimate=pl.CostEstimate(flops=flops, bytes_accessed=size, transcendentals=0),
        name=name,
        input_output_aliases=aliases or {},
        **extra,
    )(*args)


Q_TILE = 512
K_TILE = 512
LOW = -1e30
LOG2E = 1.4426950408889634


def unpack_heads(packed_ref, targets):
    blocks, _, block = packed_ref.shape

    def one(at, carry):
        here = pl.ds(pl.multiple_of(at * block, block), block)
        for place, (rows, columns) in enumerate(targets):
            piece = packed_ref[at, place * HEAD_DIM : (place + 1) * HEAD_DIM]
            if rows is not None:
                rows[here, :] = piece.T
            if columns is not None:
                columns[0:HEAD_DIM, here] = piece
        return carry

    lax.fori_loop(0, blocks, one, 0)


def tile_spans(marks, clips, index):
    first = marks[clips + SEGMENT] + index * Q_TILE
    begin = marks[clips + KEYS]
    low, low_end = clip_bounds(marks, clips, first)
    high_start, high = clip_bounds(marks, clips, first + Q_TILE - 1)
    low, low_end, high_start, high = (v - begin for v in (low, low_end, high_start, high))
    up = K_TILE - 1
    start = lax.div(low, K_TILE)
    stop = jnp.where(marks[clips + ACTIVE] > 0, lax.div(high + up, K_TILE), start)
    inner = lax.div(high_start + up, K_TILE)
    outer = lax.div(high, K_TILE)
    whole = (low == high_start) & (inner < outer) & (stop > start)
    inner = jnp.where(whole, inner, stop)
    outer = jnp.where(whole, outer, stop)
    places = first + lax.broadcasted_iota(jnp.int32, (1, Q_TILE), 1)
    starts, ends = clip_bounds(marks, clips, places)
    return (start, inner, outer, stop), starts - begin, ends - begin


def allowed(column, starts, ends):
    places = column + lax.broadcasted_iota(jnp.int32, (K_TILE, 1), 0)
    return (places >= starts) & (places < ends)


def over_spans(spans, step, state):
    for at in range(3):
        state = lax.fori_loop(spans[at], spans[at + 1], functools.partial(step, at != 1), state)
    return state


def attend_kernel(clips, halo, marks, packed_ref, out_ref, wide_ref, log_ref, query_t, keys, value_t):
    rows = wide_ref.shape[1]
    block = packed_ref.shape[2]
    more = value_t.shape[0] - HEAD_DIM
    value_t[HEAD_DIM:] = jnp.where(
        lax.broadcasted_iota(jnp.int32, (more, value_t.shape[1]), 0) == 0, 1.0, 0.0
    ).astype(BF)
    unpack_heads(packed_ref, ((None, query_t), (keys, None), (None, value_t)))
    factor = HEAD_DIM ** (-0.5) * LOG2E

    def query_tile(index, carry):
        first = pl.multiple_of(index * Q_TILE, Q_TILE)
        q = query_t[:, pl.ds(halo * block + first, Q_TILE)]
        spans, starts, ends = tile_spans(marks, clips, index)

        def key_tile(masked, at, state):
            top, total = state
            column = pl.multiple_of(at * K_TILE, K_TILE)
            scores = plain_dot(keys[pl.ds(column, K_TILE), :], q) * factor
            if masked:
                scores = jnp.where(allowed(column, starts, ends), scores, LOW)
            new_top = jnp.maximum(top, jnp.max(scores, axis=0, keepdims=True))
            weight = jnp.exp2(scores - new_top).astype(BF)
            total = total * jnp.exp2(top - new_top) + plain_dot(
                value_t[:, pl.ds(column, K_TILE)], weight
            )
            return new_top, total

        top, total = over_spans(
            spans,
            key_tile,
            (
                jnp.full((1, Q_TILE), 0.5 * LOW, jnp.float32),
                jnp.zeros((HEAD_DIM + more, Q_TILE), jnp.float32),
            ),
        )
        mass = jnp.maximum(total[HEAD_DIM : HEAD_DIM + 1], 1e-37)
        attended = total[:HEAD_DIM] / mass
        wide_ref[:, pl.ds(first, Q_TILE)] = attended
        log_ref[:, pl.ds(first, Q_TILE)] = top + jnp.log2(mass)
        narrow = attended.astype(BF)
        for inner in range(Q_TILE // block):
            out_ref[index * (Q_TILE // block) + inner] = narrow[:, inner * block : (inner + 1) * block]
        return carry

    lax.fori_loop(0, rows // Q_TILE, query_tile, 0)


def attend(marks, packed, clips, halo):
    blocks, _, block = packed.shape
    rows = (blocks - 2 * halo) * block
    key_rows = blocks * block
    return call(
        functools.partial(attend_kernel, clips, halo),
        [
            like((blocks - 2 * halo, HEAD_DIM, block), BF),
            like((HEAD_DIM, rows)),
            like((1, rows)),
        ],
        [
            pltpu.VMEM((HEAD_DIM, key_rows), BF),
            pltpu.VMEM((key_rows, HEAD_DIM), BF),
            pltpu.VMEM((HEAD_DIM + 16, key_rows), BF),
        ],
        (marks, packed),
        "attend",
        25 * 10**9,
    )


def attend_back_kernel(
    clips, halo, marks, packed_ref, grad_ref, wide_ref, log_ref, out_ref,
    query_t, keys, key_t, values, grad_t, key_grads, value_grads,
):
    unpack_heads(packed_ref, ((None, query_t), (keys, key_t), (values, None)))
    unpack_heads(grad_ref, ((None, grad_t),))
    blocks, _, block = packed_ref.shape
    rows = wide_ref.shape[1]
    scale = HEAD_DIM ** (-0.5)
    key_grads[...] = jnp.zeros_like(key_grads)
    value_grads[...] = jnp.zeros_like(value_grads)
    if halo:
        out_ref[...] = jnp.zeros_like(out_ref)

    def query_tile(index, carry):
        first = pl.multiple_of(index * Q_TILE, Q_TILE)
        own = pl.ds(halo * block + first, Q_TILE)
        q_t, g_t = query_t[:, own], grad_t[:, pl.ds(first, Q_TILE)]
        log_total = log_ref[:, pl.ds(first, Q_TILE)]
        delta = jnp.sum(
            g_t.astype(jnp.float32) * wide_ref[:, pl.ds(first, Q_TILE)], axis=0, keepdims=True
        )
        spans, starts, ends = tile_spans(marks, clips, index)

        def key_tile(masked, at, running):
            column = pl.multiple_of(at * K_TILE, K_TILE)
            here = pl.ds(column, K_TILE)
            probs = jnp.exp2(plain_dot(keys[here, :], q_t) * (scale * LOG2E) - log_total)
            if masked:
                probs = jnp.where(allowed(column, starts, ends), probs, 0.0)
            prob_grad = plain_dot(values[here, :], g_t)
            score_grad = (probs * (prob_grad - delta)).astype(BF)
            value_grads[:, here] += row_dot(g_t, probs.astype(BF))
            key_grads[:, here] += row_dot(q_t, score_grad)
            return running + plain_dot(key_t[:, here], score_grad)

        query_grad = over_spans(spans, key_tile, jnp.zeros((HEAD_DIM, Q_TILE), jnp.float32))
        query_grad = (query_grad * scale).astype(BF)
        for inner in range(Q_TILE // block):
            spot = halo + index * (Q_TILE // block) + inner
            out_ref[spot, 0:HEAD_DIM] = query_grad[:, inner * block : (inner + 1) * block]
        return carry

    lax.fori_loop(0, rows // Q_TILE, query_tile, 0)

    def finish(spot, carry):
        here = pl.ds(pl.multiple_of(spot * block, block), block)
        out_ref[spot, HEAD_DIM : 2 * HEAD_DIM] = (key_grads[:, here] * scale).astype(BF)
        out_ref[spot, 2 * HEAD_DIM :] = value_grads[:, here].astype(BF)
        return carry

    lax.fori_loop(0, blocks, finish, 0)


def attend_back(marks, packed, grad, wide, log_total, clips, halo):
    blocks, lanes, block = packed.shape
    rows = wide.shape[1]
    key_rows = blocks * block
    return call(
        functools.partial(attend_back_kernel, clips, halo),
        [like((blocks, lanes, block), BF)],
        [
            pltpu.VMEM((HEAD_DIM, key_rows), BF),
            pltpu.VMEM((key_rows, HEAD_DIM), BF),
            pltpu.VMEM((HEAD_DIM, key_rows), BF),
            pltpu.VMEM((key_rows, HEAD_DIM), BF),
            pltpu.VMEM((HEAD_DIM, rows), BF),
            pltpu.VMEM((HEAD_DIM, key_rows), jnp.float32),
            pltpu.VMEM((HEAD_DIM, key_rows), jnp.float32),
        ],
        (marks, packed, grad, wide, log_total),
        "attend_back",
        35 * 10**9,
        limit=60,
    )[0]


TAPS = 16
SHOT = 384
TURNS = KERNEL // TAPS


def conv_weights_kernel(back, weight_ref, out_ref):
    group_width = out_ref.shape[1]
    if back:
        for group in range(GROUPS):
            lanes = slice(group_width * group, group_width * (group + 1))
            out_ref[group] = jnp.concatenate(
                [weight_ref[group_width * tap : group_width * (tap + 1), lanes] for tap in range(TAPS)],
                axis=1,
            )
    else:
        turned = weight_ref[...].T
        for group in range(GROUPS):
            out_ref[group] = turned[group_width * group : group_width * (group + 1)]


def conv_weights(back, weight, first, turns):
    width = weight.shape[1]
    group_width = width // GROUPS
    return call(
        functools.partial(conv_weights_kernel, back),
        [like((GROUPS, turns * group_width, TAPS * group_width), weight.dtype)],
        [],
        (weight,),
        "conv_weights_back" if back else "conv_weights",
        0,
        (turns,),
        [pl.BlockSpec((TAPS * group_width, width), lambda turn: (turn + first, 0))],
        (pl.BlockSpec((GROUPS, group_width, TAPS * group_width), lambda turn: (0, turn, 0)),),
    )[0]


def conv_kernel(back, clips, parts, marks, before_ref, rows_ref, after_ref, *refs):
    weight_refs, (out_ref, spaced, total) = refs[:parts], refs[parts:]
    group = pl.program_id(0)
    rows, width = rows_ref.shape
    half = KERNEL // 2
    long = rows + 2 * half
    group_width = width // GROUPS
    room = spaced.shape[1]
    places = marks[clips + BEGIN] - half + lax.broadcasted_iota(jnp.int32, (1, long), 1)
    ids = over_clips(
        clips,
        lambda clip, found: found + jnp.where(places >= marks[clip], 1, 0),
        jnp.zeros((1, long), jnp.int32),
    )
    ids = jnp.where((places >= 0) & (places < marks[clips + TOTAL]), ids, -1)

    def number_of(place):
        step = lambda clip, found: found + jnp.where(place >= marks[clip], 1, 0)
        return over_clips(clips, step, jnp.int32(0))

    first = number_of(marks[clips + BEGIN])
    count = number_of(marks[clips + BEGIN] + rows - 1) - first + 1

    @pl.when(group == 0)
    def _():
        turned = jnp.concatenate(
            [before_ref[...], rows_ref[...], after_ref[...]], axis=0
        ).astype(jnp.float32).T
        rest = jnp.zeros((width, room - long), jnp.float32)

        def of_clip(clip):
            return jnp.concatenate([jnp.where(ids == first + clip, turned, 0.0), rest], axis=1)

        spaced[...] = of_clip(0).astype(BF)

        def place(clip, carry):
            spaced[...] += pltpu.roll(of_clip(clip), clip * half, 1).astype(BF)
            return carry

        lax.fori_loop(1, count, place, 0)

    row = pl.multiple_of(group * group_width, group_width)
    shots = lax.div(rows + half * (count - 1) + SHOT - 1, SHOT)

    def shot(index, carry):
        base = pl.multiple_of(index * SHOT, 128)
        tile = spaced[pl.ds(row, group_width), pl.ds(base, SHOT + 2 * KERNEL)]
        moved = []
        for tap in range(TAPS):
            begin = TAPS - tap if back else tap
            moved.append(tile[:, begin : begin + SHOT + KERNEL])
        moved = jnp.concatenate(moved, axis=0)
        result = None
        turn = 0
        for weight_ref in weight_refs:
            product = plain_dot(weight_ref[0], moved)
            for inner in range(product.shape[0] // group_width):
                begin = (TURNS - 1 - turn if back else turn) * TAPS
                piece = product[inner * group_width : (inner + 1) * group_width, begin : begin + SHOT]
                result = piece if result is None else result + piece
                turn += 1
        total[pl.ds(row, group_width), pl.ds(base, SHOT)] = result
        return carry

    lax.fori_loop(0, shots, shot, 0)

    @pl.when(group == GROUPS - 1)
    def _():
        wide = total.shape[1]
        own = ids[:, half : half + rows]

        def collect(clip, carry):
            moved = pltpu.roll(total[...], lax.rem(wide - clip * half, wide), 1)[:, :rows]
            total[:, :rows] = jnp.where(own == first + clip, moved, total[:, :rows])
            return carry

        lax.fori_loop(1, count, collect, 0)
        out_ref[...] = total[:, :rows].T


def conv_rows(back, marks, before, value, after, weights, clips):
    rows, width = value.shape
    shots = -(-(rows + KERNEL // 2 * (clips - 1)) // SHOT)
    whole = lambda a: pl.BlockSpec(a.shape, lambda group: (0, 0))
    return call(
        functools.partial(conv_kernel, back, clips, len(weights)),
        [like((rows, width))],
        [
            pltpu.VMEM((width, SHOT * shots + 2 * KERNEL), BF),
            pltpu.VMEM((width, SHOT * shots), jnp.float32),
        ],
        (marks, before, value, after) + tuple(weights),
        "conv_back" if back else "conv",
        15 * 10**9,
        (GROUPS,),
        [SMEM_WHOLE, whole(before), whole(value), whole(after)]
        + [pl.BlockSpec((1,) + weight.shape[1:], lambda group: (group, 0, 0)) for weight in weights],
        (pl.BlockSpec((rows, width), lambda group: (0, 0)),),
        limit=48,
    )[0]


def taps_grad_kernel(
    clips, marks, both_ref, *refs
):
    half = KERNEL // 2
    out_refs, (inputs, spaced, input_cols, grad_cols) = refs[:-4], refs[-4:]
    group_width = inputs.shape[0]
    long = inputs.shape[1]
    blocks, _, block = both_ref.shape
    halo = (blocks - RING) // 2
    halo_rows = halo * block
    first = over_clips(
        clips,
        lambda clip, found: found + jnp.where(marks[clips + SEGMENT] >= marks[clip], 1, 0),
        jnp.int32(0),
    )
    origin = half + halo_rows
    span = input_cols.shape[1]

    def lay(first_row, begin_block, number, target, reach):
        for at in range(number):
            target[:, at * block : (at + 1) * block] = both_ref[
                begin_block + at, first_row : first_row + group_width
            ].astype(jnp.float32)
        target[:, number * block :] = jnp.zeros((group_width, long - number * block), jnp.float32)
        lanes = lax.broadcasted_iota(jnp.int32, (1, long), 1)
        places = marks[clips + SEGMENT] - reach + lanes
        held = lanes < number * block
        spaced[...] = jnp.zeros_like(spaced)

        def place(clip, carry):
            begin = jnp.where(clip > 0, marks[jnp.maximum(clip - 1, 0)], 0)
            keep = (places >= begin) & (places < marks[clip]) & held
            spaced[...] += pltpu.roll(
                jnp.where(keep, target[...], 0.0), origin - reach + half * (clip - first), 1
            )
            return carry

        lax.fori_loop(first, clips, place, 0)
        return spaced[...]

    laid = lay(0, 0, blocks, inputs, halo_rows)
    for turn in range(TURNS):
        begin = origin - half + turn * TAPS
        input_cols[turn * group_width : (turn + 1) * group_width, :] = laid[
            :, begin : begin + span
        ].astype(BF)
    laid = lay(group_width, halo, RING, inputs, 0)
    for tap in range(TAPS):
        grad_cols[tap * group_width : (tap + 1) * group_width, :] = laid[
            :, origin - tap : origin - tap + span
        ].astype(BF)
    result = row_dot(input_cols[...], grad_cols[...]).astype(BF)
    side_lanes = TAPS * group_width // 2
    even_core = marks[clips + CORE] == 0
    for piece in range(side_lanes // 128):
        values = []
        for place_at in range(2 * TURNS):
            turn, begin = place_at // 2, place_at % 2 * side_lanes + piece * 128
            values.append(result[turn * group_width : (turn + 1) * group_width, begin : begin + 128])
        store_pairs(out_refs, even_core, slice(piece * group_width, (piece + 1) * group_width), values)


def taps_grad(marks, both, shape, clips, width):
    blocks, _, block = both.shape
    group_width = width // GROUPS
    half = KERNEL // 2
    halo_rows = (blocks - RING) // 2 * block
    span = -(-(RING * block + half * clips) // 128) * 128
    long = span + 2 * halo_rows + half + 2 * KERNEL
    long = -(-long // 128) * 128
    more = TAPS * group_width // 2 // 128 * group_width
    return call(
        functools.partial(taps_grad_kernel, clips),
        [like((n, more, 128), BF) for n in shape],
        [
            pltpu.VMEM((group_width, long), jnp.float32),
            pltpu.VMEM((group_width, long), jnp.float32),
            pltpu.VMEM((TURNS * group_width, span), BF),
            pltpu.VMEM((TAPS * group_width, span), BF),
        ],
        (marks, both),
        "taps_grad",
        10**10,
        limit=60,
    )


def weave_taps_kernel(own_ref, out_ref):
    group_width = out_ref.shape[1] // GROUPS
    taps = out_ref.shape[0] // group_width
    pieces = own_ref.shape[1] // group_width
    both = []
    for group in range(GROUPS):
        rows = own_ref[group].astype(jnp.float32)
        both.append(
            jnp.concatenate([rows[at * group_width : (at + 1) * group_width] for at in range(pieces)], axis=1)
        )
    for tap in range(taps):
        lanes = slice(tap * group_width, (tap + 1) * group_width)
        out_ref[tap * group_width : (tap + 1) * group_width, :] = jnp.concatenate(
            [value[:, lanes] for value in both], axis=1
        )


def weave_taps(own, taps, group_width):
    return call(
        weave_taps_kernel, [like((taps * group_width, GROUPS * group_width))], [], (own,), "weave_taps", 0
    )[0]


def add_shares_kernel(own_ref, other_ref, out_ref):
    out_ref[...] = (own_ref[...].astype(jnp.float32) + other_ref[...].astype(jnp.float32)).astype(BF)


def add_shares(own, other):
    block = pl.BlockSpec((2,) + other.shape[1:], lambda at: (at, 0, 0))
    return call(
        add_shares_kernel,
        [like(other.shape, BF)],
        [],
        (own, other),
        "add_shares",
        0,
        (other.shape[0] // 2,),
        [block] * 2,
        (block,),
    )[0]


def split_shares_kernel(clips, marks, own_ref, other_ref, kept_ref, sent_ref):
    total = (own_ref[...].astype(jnp.float32) + other_ref[...].astype(jnp.float32)).astype(BF)
    rows = kept_ref.shape[1]
    lower = marks[clips + REP] == 0
    kept_ref[...] = jnp.where(lower, total[:, :rows], total[:, rows:])
    sent_ref[...] = jnp.where(lower, total[:, rows:], total[:, :rows])


def split_shares(marks, own, other, clips):
    shares, rows, lanes = own.shape
    return call(
        functools.partial(split_shares_kernel, clips),
        [like((shares, rows // 2, lanes), BF)] * 2,
        [],
        (marks, own, other),
        "split_shares",
        0,
    )


def add_below_kernel(own_ref, other_ref, _, out_ref):
    add_shares_kernel(own_ref, other_ref, out_ref)


def add_below(own, other, straight):
    block = pl.BlockSpec((2,) + own.shape[1:], lambda at: (at, 0, 0))
    return call(
        add_below_kernel,
        [like(straight.shape, BF)],
        [],
        (own, other, straight),
        "add_below",
        0,
        (own.shape[0] // 2,),
        [block, block, pl.BlockSpec(memory_space=pl.ANY)],
        (pl.BlockSpec((2,) + own.shape[1:], lambda at: (at, 1, 0)),),
        aliases={2: 0},
    )[0]


def join_pair_kernel(clips, marks, taps_ref, other_ref, out_ref):
    rows = taps_ref.shape[1]
    first = marks[clips + CORE] == 0
    out_ref[:, :rows] = jnp.where(first, taps_ref[...], other_ref[...])
    out_ref[:, rows:] = jnp.where(first, other_ref[...], taps_ref[...])


def join_pair(marks, taps, other, clips):
    chips, rows, lanes = taps.shape
    return call(
        functools.partial(join_pair_kernel, clips),
        [like((chips, 2 * rows, lanes), BF)],
        [],
        (marks, taps, other),
        "join_pair",
        0,
    )[0]


SHARE = 384
PIECE = 128


def norm_parts(values):
    center = values - jnp.mean(values, axis=-1, keepdims=True)
    inverse = lax.rsqrt(jnp.mean(center * center, axis=-1, keepdims=True) + EPS)
    return center * inverse, inverse


def norm_back(unit, inverse, scales, grad):
    scaled = grad * scales
    back = inverse * (
        scaled
        - jnp.mean(scaled, axis=-1, keepdims=True)
        - unit * jnp.mean(scaled * unit, axis=-1, keepdims=True)
    )
    return back, row_sum(grad * unit), row_sum(grad)


def row_sum(values):
    return jnp.sum(values, axis=0, keepdims=True)


def gelu_both(values):
    below = 0.5 + 0.5 * lax.erf(values * 0.7071067811865476)
    bell = jnp.exp(-0.5 * values * values) * 0.3989422804014327
    return values * below, below + values * bell


def store_turned(values_b, out_ref, first):
    group_width = values_b.shape[1] // GROUPS
    turned = values_b.T
    for group in range(GROUPS):
        out_ref[group, first : first + group_width] = turned[group * group_width : (group + 1) * group_width]


def same_clip_next(marks, clips, rows):
    following = marks[clips + BEGIN] + 1 + lax.broadcasted_iota(jnp.int32, (rows, 1), 0)
    step = lambda clip, other: jnp.maximum(other, jnp.where(following == marks[clip], 1, 0))
    return over_clips(clips, step, jnp.zeros((rows, 1), jnp.int32)) == 0


def stem_kernel(
    clips, marks, samples_ref, next_ref, weight_ref, gain_ref, bias_ref, proj_ref, gains_ref, biases_ref,
    start_ref, start_b_ref, pre_ref, normed_ref, unfold_ref, table_ref, wide,
):
    rows, chans = pre_ref.shape
    table_ref[0:3] = gains_ref[...]
    table_ref[3:12] = biases_ref[...]
    last = lax.broadcasted_iota(jnp.int32, (rows, 1), 0) == rows - 1
    same = same_clip_next(marks, clips, rows)
    for lane in range(0, chans, PIECE):
        lanes = slice(lane, lane + PIECE)
        wide[...] = samples_ref[:, lanes].astype(jnp.float32)
        even = wide[pl.ds(0, rows, stride=2), :]
        unfold_ref[:, lanes] = even.astype(BF)
        unfold_ref[:, chans + lane : chans + lane + PIECE] = wide[pl.ds(1, rows, stride=2), :].astype(BF)
        moved = jnp.where(last, next_ref[:, lanes].astype(jnp.float32), pltpu.roll(even, rows - 1, 0))
        unfold_ref[:, 2 * chans + lane : 2 * chans + lane + PIECE] = jnp.where(same, moved, 0.0).astype(BF)
    pre = plain_dot(unfold_ref[...], weight_ref[...])
    pre_ref[...] = pre
    unit, _ = norm_parts(gelu_both(pre)[0])
    normed = (unit * gain_ref[...] + bias_ref[...]).astype(BF)
    normed_ref[...] = normed
    start = plain_dot(normed, proj_ref[...]) + table_ref[3:4]
    start_ref[...] = start
    start_b_ref[...] = start.astype(BF)


def stem(marks, samples, next_row, weight, gain, bias, proj, gains, biases, clips):
    rows = samples.shape[0] // 2
    chans, width = proj.shape
    return call(
        functools.partial(stem_kernel, clips),
        [
            like((rows, width)), like((rows, width), BF),
            like((rows, chans)), like((rows, chans), BF), like((rows, 3 * chans), BF), like((12, width)),
        ],
        [pltpu.VMEM((2 * rows, PIECE), jnp.float32)],
        (marks, samples, next_row, weight, gain, bias, proj, gains, biases),
        "stem",
        6 * 10**9,
    )


def project_kernel(conv_ref, start_ref, table_ref, weight_ref, hidden_ref, hidden_b_ref, packed_ref):
    rows, width = start_ref.shape
    mixed = start_ref[...] + gelu_both(conv_ref[...] + table_ref[4:5])[0]
    unit, _ = norm_parts(mixed)
    hidden = unit * table_ref[0:1] + table_ref[5:6]
    hidden_ref[...] = hidden
    hidden_b = hidden.astype(BF)
    hidden_b_ref[...] = hidden_b
    shifts = (table_ref[6:7], jnp.zeros((1, width), jnp.float32), table_ref[7:8])
    heads = width // HEAD_DIM
    for at, shift in enumerate(shifts):
        part = plain_dot(hidden_b, weight_ref[:, at * width : (at + 1) * width]) + shift
        turned = part.astype(BF).T
        for head in range(heads):
            packed_ref[head, at * HEAD_DIM : (at + 1) * HEAD_DIM] = turned[
                head * HEAD_DIM : (head + 1) * HEAD_DIM
            ]
    for head in range(heads, RING):
        packed_ref[head] = jnp.zeros_like(packed_ref[head])


def project_heads(conv_sum, start, table, weight):
    rows, width = start.shape
    return call(
        project_kernel,
        [like((rows, width)), like((rows, width), BF), like((RING, 3 * HEAD_DIM, rows), BF)],
        [],
        (conv_sum, start, table, weight),
        "project_heads",
        6 * 10**9,
    )


def middle_kernel(
    clips, marks, heads_ref, hidden_ref, table_ref, out_weight_ref, in_ref, in_bias_ref, back_ref, out_grad_ref,
    layer_ref, grad_heads_ref, grad_second_ref, sums_ref, in_bias_grad_ref, kept_ref, sent_ref, straight_ref,
    attended, before, second, second_b, second_t, inner_b, slope, total, grad_last, grad_last_b,
    joined, sems,
):
    step = pl.program_id(0)
    rows, width = hidden_ref.shape
    chunk = in_ref.shape[1]
    chunks = pl.num_programs(0) // 2
    heads = width // HEAD_DIM
    shares = kept_ref.shape[0]
    lower = marks[clips + REP] == 0
    in_rows = width // shares
    back_rows = chunk * chunks // shares
    owners = chunk // back_rows

    first_blocks = 3 * chunks // 4

    def moves(half, place, sem, act):
        for keeps, target in ((lower, (kept_ref, sent_ref)[half]), (~lower, (sent_ref, kept_ref)[half])):

            @pl.when(keeps)
            def _():
                act(pltpu.make_async_copy(joined.at[half].at[place], target.at[place], sem))

    def in_moves(at, act):
        @pl.when(at < first_blocks)
        def _():
            place = (slice(None), pl.ds(pl.multiple_of(at * in_rows, 16), in_rows))
            moves(0, place, sems.at[0, at], act)

        @pl.when(at >= first_blocks)
        def _():
            place = (slice(None), pl.ds(pl.multiple_of((at - first_blocks) * in_rows, 16), in_rows))
            act(pltpu.make_async_copy(joined.at[2].at[place], straight_ref.at[place], sems.at[0, at]))

    def back_moves(at, act):
        mine = pl.ds(at * owners, owners)
        moves(1, (mine, pl.ds(0, back_rows)), sems.at[1, at], act)
        place = (mine, pl.ds((chunks - first_blocks) * in_rows, back_rows))
        act(pltpu.make_async_copy(joined.at[2].at[place], straight_ref.at[place], sems.at[2, at]))

    def out_moves(act):
        moves(1, (slice(None), pl.ds(back_rows, 2 * in_rows)), sems.at[3, 0], act)

    def go(copy):
        copy.start()

    def wait(copy):
        copy.wait()

    @pl.when(step == 0)
    def _():
        for head in range(heads):
            attended[head * HEAD_DIM : (head + 1) * HEAD_DIM] = heads_ref[head]
        value = hidden_ref[...] + over_rows_dot(attended[...], out_weight_ref[...]) + table_ref[8:9]
        before[...] = value
        unit, _ = norm_parts(value)
        value = unit * table_ref[1:2] + table_ref[9:10]
        second[...] = value
        second_b[...] = value.astype(BF)
        second_t[...] = value.T.astype(BF)
        total[...] = jnp.zeros_like(total)

    @pl.when(step < chunks)
    def _():
        at = pl.multiple_of(step * chunk, chunk)
        value, back = gelu_both(plain_dot(second_b[...], in_ref[...]) + in_bias_ref[:, pl.ds(at, chunk)])
        value_b = value.astype(BF)
        inner_b[step] = value_b
        slope[step] = back
        total[...] += plain_dot(value_b, back_ref[...])

    @pl.when(step == chunks - 1)
    def _():
        unit, inverse = norm_parts(second[...] + total[...] + table_ref[10:11])
        layer_ref[...] = (unit * table_ref[2:3] + table_ref[11:12]).astype(BF)
        back, gain, bias = norm_back(unit, inverse, table_ref[2:3], out_grad_ref[...].astype(jnp.float32))
        grad_last[...] = back
        grad_last_b[...] = back.astype(BF)
        total[...] = back
        sums_ref[0:1] = gain
        sums_ref[1:2] = bias
        sums_ref[2:3] = row_sum(back)

    @pl.when(step >= chunks)
    def _():
        turn = step - chunks
        at = pl.multiple_of(turn * chunk, chunk)
        grad = row_dot(grad_last_b[...], back_ref[...]) * slope[turn]
        in_bias_grad_ref[:, pl.ds(at, chunk)] = row_sum(grad)
        grad_b = grad.astype(BF)
        total[...] += row_dot(grad_b, in_ref[...])
        product = plain_dot(second_t[...], grad_b).astype(BF)
        straight = turn >= first_blocks
        row = pl.multiple_of(jnp.where(straight, turn - first_blocks, turn) * in_rows, 16)
        for share in range(shares):
            joined[jnp.where(straight, 2, 0), share, pl.ds(row, in_rows), :] = product[
                share * in_rows : (share + 1) * in_rows
            ]
        in_moves(turn, go)
        product = over_rows_dot(inner_b[turn], grad_last_b[...]).astype(BF)
        for owner in range(owners):
            for place in range(width // SHARE):
                begin = (chunks - first_blocks) * in_rows if place else 0
                joined[1 + place, turn * owners + owner, begin : begin + back_rows, :] = product[
                    owner * back_rows : (owner + 1) * back_rows, place * SHARE : (place + 1) * SHARE
                ]
        back_moves(turn, go)

    @pl.when(step == 2 * chunks - 1)
    def _():
        unit, inverse = norm_parts(before[...])
        back, gain, bias = norm_back(unit, inverse, table_ref[1:2], total[...])
        grad_second_ref[...] = back
        sums_ref[3:4] = row_sum(back)
        sums_ref[4:5] = gain
        sums_ref[5:6] = bias
        sums_ref[6:8] = jnp.zeros((2, width), jnp.float32)
        back_b = back.astype(BF)
        grads = row_dot(out_weight_ref[...], back_b).astype(BF)
        for head in range(heads):
            grad_heads_ref[head] = grads[head * HEAD_DIM : (head + 1) * HEAD_DIM]
        for head in range(heads, RING):
            grad_heads_ref[head] = jnp.zeros_like(grad_heads_ref[head])
        product = plain_dot(attended[...], back_b).astype(BF)
        for share in range(shares):
            for place in range(width // SHARE):
                begin = back_rows + place * in_rows
                joined[1, share, begin : begin + in_rows, :] = product[
                    share * in_rows : (share + 1) * in_rows, place * SHARE : (place + 1) * SHARE
                ]
        out_moves(go)

        def finish(at, carry):
            in_moves(at, wait)
            back_moves(at, wait)
            return carry

        lax.fori_loop(0, chunks, finish, 0)
        out_moves(wait)


def middle(marks, clips, heads, hidden, table, out_weight, ffn_in, in_bias, ffn_out, out_grad, count):
    rows, width = hidden.shape
    inner = ffn_in.shape[1]
    chunk = SHARE
    chunks = inner // chunk
    own = lambda shape: pl.BlockSpec(shape, lambda step: (0,) * len(shape))
    third = (2 * inner + width) * (width // count) // SHARE // 3
    outs = [
        like((rows, width), BF),
        like((RING, HEAD_DIM, rows), BF),
        like((rows, width)),
        like((8, width)),
        like((1, inner)),
        like((count, third, SHARE), BF),
        like((count, third, SHARE), BF),
        like((count, 2 * third, SHARE), BF),
    ]
    args = (marks, heads, hidden, table, out_weight, ffn_in, in_bias, ffn_out, out_grad)
    in_specs = [SMEM_WHOLE] + [own(a.shape) for a in args[1:]]
    in_specs[5] = pl.BlockSpec((width, chunk), lambda step: (0, step % chunks))
    in_specs[7] = pl.BlockSpec((chunk, width), lambda step: (step % chunks, 0))
    out_specs = [own(o.shape) for o in outs]
    out_specs[5] = out_specs[6] = out_specs[7] = pl.BlockSpec(memory_space=pl.ANY)
    scratch = [
        pltpu.VMEM((width, rows), BF),
        pltpu.VMEM((rows, width), jnp.float32),
        pltpu.VMEM((rows, width), jnp.float32),
        pltpu.VMEM((rows, width), BF),
        pltpu.VMEM((width, rows), BF),
        pltpu.VMEM((chunks, rows, chunk), BF),
        pltpu.VMEM((chunks, rows, chunk), jnp.float32),
        pltpu.VMEM((rows, width), jnp.float32),
        pltpu.VMEM((rows, width), jnp.float32),
        pltpu.VMEM((rows, width), BF),
        pltpu.VMEM((3,) + outs[5].shape, BF),
        pltpu.SemaphoreType.DMA((4, chunks)),
    ]
    return call(
        functools.partial(middle_kernel, clips), outs, scratch, args, "middle", 2 * 10**10, (2 * chunks,), in_specs, tuple(out_specs)
    )


def after_heads_kernel(
    whole, packed_ref, grad_second_ref, hidden_ref, conv_ref, start_ref, table_ref, weight_ref, *refs
):
    rows, width = hidden_ref.shape
    heads = width // HEAD_DIM
    if whole:
        heads_ref, mixed_ref, conv_b_ref, groups_ref, sums_ref, grads = refs
        groups_ref[:, 2 * width // GROUPS :] = heads_ref[...]
    else:
        mixed_ref, conv_b_ref, groups_ref, sums_ref, joined_ref, grads, hidden_t = refs
    for head in range(heads):
        for part in range(3):
            row = part * width + head * HEAD_DIM
            grads[row : row + HEAD_DIM] = packed_ref[head, part * HEAD_DIM : (part + 1) * HEAD_DIM]
    if not whole:
        shares = joined_ref.shape[0]
        own_rows = width // shares
        hidden_t[...] = hidden_ref[...].T.astype(BF)

        def weight_block(place, carry):
            row = pl.multiple_of(place * SHARE, SHARE)
            product = row_dot(hidden_t[...], grads[pl.ds(row, SHARE), :]).astype(BF)
            for share in range(shares):
                joined_ref[share, pl.ds(pl.multiple_of(place * own_rows, 16), own_rows), :] = product[
                    share * own_rows : (share + 1) * own_rows
                ]
            return carry

        lax.fori_loop(0, 3 * width // SHARE, weight_block, 0)
    back = grad_second_ref[...] + plain_dot(weight_ref[...], grads[...]).T
    value, slope = gelu_both(conv_ref[...] + table_ref[4:5])
    unit, inverse = norm_parts(start_ref[...] + value)
    mixed, gain, bias = norm_back(unit, inverse, table_ref[0:1], back)
    mixed_ref[...] = mixed
    conv = mixed * slope
    conv_b = conv.astype(BF)
    conv_b_ref[...] = conv_b
    store_turned(start_ref[...].astype(BF), groups_ref, 0)
    store_turned(conv_b, groups_ref, width // GROUPS)
    sums_ref[0:1] = gain
    sums_ref[1:2] = bias
    sums_ref[2:3] = row_sum(conv)
    ones = jnp.ones((8, rows), BF)
    sums_ref[3:4] = row_dot(ones, grads[:width])[0:1]
    sums_ref[4:5] = row_dot(ones, grads[2 * width :])[0:1]
    sums_ref[5:8] = jnp.zeros((3, width), jnp.float32)


def after_heads(packed, grad_second, hidden, conv_sum, start, table, weight, head_grads):
    rows, width = hidden.shape
    whole = head_grads is not None
    lines = 2 * width // GROUPS + (width // RING if whole else 0)
    outs = [like((rows, width)), like((rows, width), BF), like((GROUPS, lines, rows), BF), like((8, width))]
    scratch = [pltpu.VMEM((3 * width, rows), BF)]
    args = (packed, grad_second, hidden, conv_sum, start, table, weight)
    if whole:
        args += (head_grads,)
    else:
        outs.append(like((RING, width // RING * 3 * width // SHARE, SHARE), BF))
        scratch.append(pltpu.VMEM((width, rows), BF))
    return call(
        functools.partial(after_heads_kernel, whole), outs, scratch, args, "after_heads", 5 * 10**9
    )


def head_grads_kernel(clips, marks, packed_ref, hidden_ref, other_ref, out_ref, turned):
    blocks, lines, block = packed_ref.shape
    core = marks[clips + CORE]
    width = hidden_ref.shape[2]

    def one(at, total):
        total = total + plain_dot(packed_ref[2 * at + core], hidden_ref[at])
        return total + plain_dot(packed_ref[2 * at + 1 - core], other_ref[at])

    total = lax.fori_loop(0, blocks // 2, one, jnp.zeros((lines, width), jnp.float32))
    turned[...] = jnp.concatenate([total, jnp.zeros((block - lines, width), jnp.float32)], axis=0).T.astype(BF)
    own = width // RING
    for share in range(RING):
        out_ref[share] = turned[share * own : (share + 1) * own]


def head_grads(marks, packed, hidden, other, clips):
    block = packed.shape[2]
    width = hidden.shape[2]
    return call(
        functools.partial(head_grads_kernel, clips),
        [like((RING, width // RING, block), BF)],
        [pltpu.VMEM((width, block), BF)],
        (marks, packed, hidden, other),
        "head_grads",
        3 * 10**9,
    )[0]


def weave_heads_kernel(own_ref, other_ref, out_ref):
    heads = own_ref.shape[0]
    for part in range(3):
        lanes = slice(part * HEAD_DIM, (part + 1) * HEAD_DIM)
        out_ref[:, part * heads * HEAD_DIM : (part + 1) * heads * HEAD_DIM] = jnp.concatenate(
            [
                own_ref[head, :, lanes].astype(jnp.float32) + other_ref[head, :, lanes].astype(jnp.float32)
                for head in range(heads)
            ],
            axis=1,
        )


def weave_heads(own, other):
    heads, rows, _ = own.shape
    return call(
        weave_heads_kernel, [like((rows, 3 * heads * HEAD_DIM))], [], (own, other), "weave_heads", 0
    )[0]


def stem_back_kernel(
    clips, marks, input_ref, mixed_ref, normed_ref, pre_ref, unfold_ref, weight_ref, gain_ref, proj_ref,
    middle_sums_ref, inner_sums_ref, after_sums_ref,
    samples_ref, carried_ref, *refs,
):
    rows, chans = pre_ref.shape
    width = input_ref.shape[1]
    joined_refs, (table, spread, woven) = refs[:-3], refs[-3:]
    shares = RING
    even_core = marks[clips + CORE] == 0
    start = mixed_ref[...] + input_ref[...]
    start_b = start.astype(BF)

    def share_out(product, begin):
        own, columns = product.shape[0] // shares, product.shape[1]
        for place in range(columns // PIECE):
            at = begin + place * own
            store_pairs(
                joined_refs,
                even_core,
                slice(at, at + own),
                [
                    product[share * own : (share + 1) * own, place * PIECE : (place + 1) * PIECE]
                    for share in range(shares)
                ],
            )
        return begin + own * columns // PIECE

    at = share_out(over_rows_dot(normed_ref[...], start_b).astype(BF), 0)
    value, slope = gelu_both(pre_ref[...])
    unit, inverse = norm_parts(value)
    feature, gain_sum, bias_sum = norm_back(
        unit, inverse, gain_ref[...], row_dot(start_b, proj_ref[...])
    )
    pre_b = (feature * slope).astype(BF)
    taps_t = over_rows_dot(unfold_ref[...], pre_b).astype(BF)
    at = share_out(taps_t, at)
    first = row_dot(pre_b, weight_ref[:chans])
    same = same_clip_next(marks, clips, rows)
    follow = jnp.where(same, row_dot(pre_b, weight_ref[2 * chans :]), 0.0)
    carried_ref[...] = follow[rows - 1 :]
    moved = pltpu.roll(follow, 1, 0)
    top = lax.broadcasted_iota(jnp.int32, (rows, 1), 0) == 0
    even = first + jnp.where(top, 0.0, moved)
    odd = row_dot(pre_b, weight_ref[chans : 2 * chans])
    for lane in range(0, chans, PIECE):
        woven[pl.ds(0, rows, stride=2), :] = even[:, lane : lane + PIECE]
        woven[pl.ds(1, rows, stride=2), :] = odd[:, lane : lane + PIECE]
        samples_ref[:, lane : lane + PIECE] = woven[...]
    table[0:1] = after_sums_ref[0:1]
    table[1:2] = middle_sums_ref[4:5]
    table[2:3] = middle_sums_ref[0:1]
    table[3:4] = row_sum(start)
    table[4:5] = after_sums_ref[2:3]
    table[5:6] = after_sums_ref[1:2]
    table[6:7] = after_sums_ref[3:4]
    table[7:8] = after_sums_ref[4:5]
    table[8:9] = middle_sums_ref[3:4]
    table[9:10] = middle_sums_ref[5:6]
    table[10:11] = middle_sums_ref[2:3]
    table[11:12] = middle_sums_ref[1:2]
    spread[...] = jnp.zeros_like(spread)
    own, own_chans = width // shares, chans // shares
    own_inner = inner_sums_ref.shape[1] // shares
    for share in range(shares):
        spread[share, 0:12, 0:own] = table[:, share * own : (share + 1) * own]
        for place in range(-(-own_inner // PIECE)):
            length = min(PIECE, own_inner - place * PIECE)
            begin = share * own_inner + place * PIECE
            spread[share, 12 + place : 13 + place, 0:length] = inner_sums_ref[:, begin : begin + length]
        lanes = slice(share * own_chans, (share + 1) * own_chans)
        spread[share, 14:15, 0:own_chans] = gain_sum[:, lanes]
        spread[share, 15:16, 0:own_chans] = bias_sum[:, lanes]
    store_pairs(
        joined_refs, even_core, slice(at, at + 32), [spread[share].astype(BF) for share in range(shares)]
    )


def stem_back(marks, input_grad, mixed, normed, pre, unfold, weight, gain, proj, sums, shares, clips):
    rows, chans = pre.shape
    width = input_grad.shape[1]
    pieces = (chans // RING * width + 3 * chans // RING * chans) // PIECE + 32
    return call(
        functools.partial(stem_back_kernel, clips),
        [like((2 * rows, chans)), like((1, chans))] + [like((n, pieces, PIECE), BF) for n in shares],
        [pltpu.VMEM((12, width), jnp.float32), pltpu.VMEM((RING, 32, PIECE), jnp.float32),
         pltpu.VMEM((2 * rows, PIECE), jnp.float32)],
        (marks, input_grad, mixed, normed, pre, unfold, weight, gain, proj) + sums,
        "stem_back",
        6 * 10**9,
    )


def from_behind(value, axis, steps):
    count = lax.axis_size(axis)
    initial, last = (max(0, -steps), min(count, count - steps))
    return lax.ppermute(value, axis, [(source, source + steps) for source in range(initial, last)])


def edges(value, width):
    length = value.shape[0]
    return from_behind(value[length - width :], "seq", 1), from_behind(value[:width], "seq", -1)


def near_groups():
    size = lax.axis_size("seq")
    return [[base + i for i in range(RING)] for base in range(0, size, RING)]


def swap(value):
    groups = None if lax.axis_size("seq") == RING else near_groups()
    return lax.all_to_all(value, "seq", 0, 0, axis_index_groups=groups)


def with_far_blocks(value, count):
    if lax.axis_size("seq") == RING or count == 0:
        return value
    before = from_behind(value[value.shape[0] - count :], "seq", RING)
    after = from_behind(value[:count], "seq", -RING)
    return jnp.concatenate([before, value, after], axis=0)


def fold_far_blocks(value, count):
    if lax.axis_size("seq") == RING or count == 0:
        return value
    own = value[count : value.shape[0] - count]
    to_before = from_behind(value[:count], "seq", -RING)
    to_after = from_behind(value[value.shape[0] - count :], "seq", RING)
    wide = own.astype(jnp.float32)
    wide = wide.at[wide.shape[0] - count :].add(to_before.astype(jnp.float32))
    wide = wide.at[:count].add(to_after.astype(jnp.float32))
    return wide.astype(value.dtype)


def other_stream(share):
    return lax.ppermute(share, "rep", [(0, 1), (1, 0)])


def sum_pair(share):
    return share.astype(jnp.float32) + other_stream(share).astype(jnp.float32)


def spread_out(total, sizes, lanes):
    out, at = [], 0
    for rows, columns in sizes:
        parts = []
        for _ in range(columns // lanes):
            parts.append(total[at : at + rows])
            at += rows
        out.append(jnp.concatenate(parts, axis=1))
    return out


def regroup(joined, blocks):
    count = lax.axis_size("seq")
    if count == RING:
        return joined
    parts = count // RING
    lanes = joined.shape[2]
    out, at = [], 0
    for number, rows in blocks:
        piece = joined[:, at : at + number * rows]
        at += number * rows
        piece = piece.reshape(RING, number, parts, rows // parts, lanes).transpose(0, 2, 1, 3, 4)
        out.append(piece.reshape(count, number * rows // parts, lanes))
    return jnp.concatenate(out, axis=1)


def regroup_small(small, widths):
    count = lax.axis_size("seq")
    if count == RING:
        return small
    parts = count // RING
    own, own_inner, own_chans = widths
    lanes = small.shape[2]
    table = small[:, :12, : own * parts].reshape(RING, 12, parts, own).transpose(0, 2, 1, 3)
    table = jnp.pad(table.reshape(count, 12, own), ((0, 0), (0, 0), (0, lanes - own)))
    wide = small[:, 12:14].reshape(RING, 2 * lanes)[:, : own_inner * parts].reshape(count, own_inner)
    wide = jnp.pad(wide, ((0, 0), (0, 2 * lanes - own_inner))).reshape(count, 2, lanes)
    stems = small[:, 14:16, : own_chans * parts].reshape(RING, 2, parts, own_chans).transpose(0, 2, 1, 3)
    stems = jnp.pad(stems.reshape(count, 2, own_chans), ((0, 0), (0, 0), (0, lanes - own_chans)))
    return jnp.concatenate([table, wide, stems], axis=1)


def over_seq(joined):
    return lax.psum_scatter(joined, "seq", scatter_dimension=0, tiled=False).astype(jnp.bfloat16)


def local(
    samples,
    clip_lengths,
    stem_weight,
    stem_gain,
    stem_bias,
    proj_weight,
    pos_weight,
    norm_gains,
    biases,
    attn_in,
    attn_out,
    ffn_in,
    ffn_in_bias,
    ffn_out,
    out_grad,
):
    rows_dev = out_grad.shape[1]
    width = attn_out.shape[0]
    chans = stem_weight.shape[1]
    inner = ffn_in.shape[1]
    group_width = width // GROUPS
    count = lax.axis_size("seq")
    place = lax.axis_index("seq")
    total = rows_dev * count
    begin = place * rows_dev
    ends = jnp.cumsum(clip_lengths[0])
    clips = ends.shape[0]
    half = KERNEL // 2
    far = 0 if count == RING else -(-MAXLEN // rows_dev)
    segment_begin = (place // RING) * RING * rows_dev
    active = jnp.where(place % RING < HEADS, 1, 0)
    marks = jnp.concatenate(
        [ends, jnp.stack([jnp.int32(total), begin, segment_begin, segment_begin - far * rows_dev, active, place % 2, lax.axis_index("rep") if count == RING else 0])]
    ).astype(jnp.int32)
    next_row = from_behind(samples[0, :1], "seq", -1)
    one_weights = conv_weights(False, pos_weight, 0, TURNS // 2)
    next_row, one_weights = lax.optimization_barrier((next_row, one_weights))
    start_x, start_b, stem_pre, normed_b, unfold, table = stem(
        marks, samples[0], next_row, stem_weight, stem_gain[None], stem_bias[None], proj_weight,
        norm_gains.T, biases.T, clips,
    )
    before, after = edges(start_b, half)
    rest_source, _ = lax.optimization_barrier((pos_weight, table))
    rest_weights = conv_weights(False, rest_source, TURNS // 2, TURNS // 2)
    before, after, rest_weights = lax.optimization_barrier((before, after, rest_weights))
    conv_sum = conv_rows(False, marks, before, start_b, after, (one_weights, rest_weights), clips)
    hidden, hidden_b, packed = project_heads(conv_sum, start_x, table, attn_in)
    pairs = [(i, i ^ 1) for i in range(count)]
    alike = [list(range(core, count, 2)) for core in range(2)]
    back_source, _ = lax.optimization_barrier((pos_weight, hidden))
    packed = with_far_blocks(swap(packed), far)
    back_weights = conv_weights(True, back_source, 0, TURNS)
    packed, back_weights, hidden_b = lax.optimization_barrier((packed, back_weights, hidden_b))
    if count == RING:
        gathered = lax.all_gather(hidden_b, "seq", axis=0, tiled=False, axis_index_groups=alike)
    attended_heads, wide, log_total = attend(marks, packed, clips, far)
    layer_out, grad_heads, grad_pre_second, middle_sums, inner_sums, ffn_kept, ffn_sent, straight = middle(
        marks, clips, swap(attended_heads), hidden, table, attn_out, ffn_in, ffn_in_bias[None], ffn_out, out_grad[0],
        RING,
    )
    near_rows, near_chans, near_inner = width // RING, chans // RING, inner // RING
    if count == RING:
        grad_heads, gathered = lax.optimization_barrier((grad_heads, gathered))
        other_gathered = lax.ppermute(gathered, "seq", pairs)
        ffn_other = other_stream(ffn_sent)
    grad_heads = swap(grad_heads)
    packed_grad = attend_back(marks, packed, grad_heads, wide, log_total, clips, far)
    own_heads = None
    if count == RING:
        own_heads = head_grads(marks, packed_grad, gathered, other_gathered, clips)
    swapped = swap(fold_far_blocks(packed_grad, far))
    if count == RING:
        ffn_other, own_heads = lax.optimization_barrier((ffn_other, own_heads))
        ffn_joined = add_below(ffn_kept, ffn_other, straight)
        swapped, own_heads, ffn_joined = lax.optimization_barrier((swapped, own_heads, ffn_joined))
    grad_mixed, grad_conv_b, grad_packed, after_sums, *attn_joined = after_heads(
        swapped, grad_pre_second, hidden, conv_sum, start_x, table, attn_in, own_heads
    )
    if count != RING:
        ffn_joined = jnp.concatenate([straight[:, : ffn_kept.shape[1]], ffn_kept, ffn_sent], axis=1)
        first_blocks = 3 * inner // SHARE // 4
        ffn_joined = regroup(
            ffn_joined,
            [
                (inner // SHARE - first_blocks, near_rows),
                (1, near_inner),
                (first_blocks, near_rows),
                (1, near_inner),
                (2, near_rows),
            ],
        )
    ffn_share = over_seq(ffn_joined)
    before, after = edges(grad_conv_b, half)
    before, after, grad_packed = lax.optimization_barrier((before, after, grad_packed))
    grad_groups = swap(grad_packed)
    input_grad = conv_rows(True, marks, before, grad_conv_b, after, (back_weights,), clips)
    shape = (RING // 2,) * 2 if count == RING else (RING,)
    sample_grad, carried, *stem_shares = stem_back(
        marks, input_grad, grad_mixed, normed_b, stem_pre, unfold, stem_weight, stem_gain[None],
        proj_weight, (middle_sums, inner_sums, after_sums), shape, clips,
    )
    carried = from_behind(carried, "seq", 1)
    own = width // count
    own_chans = chans // count
    own_taps = KERNEL // count

    def ffn_parts(share):
        other = other_stream(share)
        if count == RING:
            at = share.shape[0] // 2
            lower = lax.axis_index("rep") == 0
            share = jnp.concatenate(
                [
                    share[:at].astype(jnp.float32) + other[:at].astype(jnp.float32),
                    jnp.where(lower, share[at:], other[at:]).astype(jnp.float32),
                    jnp.where(lower, other[at:], share[at:]).astype(jnp.float32),
                ],
                axis=0,
            )
        else:
            share = share.astype(jnp.float32) + other.astype(jnp.float32)
        most = 3 * inner // 4
        sizes = [(own, inner - most), (inner // count, SHARE), (own, most), (inner // count, SHARE), (own, width)]
        in_end, back_end, in_start, back_start, out = spread_out(share, sizes, SHARE)
        return (
            jnp.concatenate([in_start, in_end], axis=1),
            jnp.concatenate([back_start, back_end], axis=1),
            out,
        )

    if count == RING:
        kept, sent = split_shares(marks, stem_shares[0], lax.ppermute(stem_shares[1], "seq", pairs), clips)
        other_sent = other_stream(sent)
        taps, sent_taps = taps_grad(marks, grad_groups, shape, clips, width)
        other_sent, taps, sent_taps = lax.optimization_barrier((other_sent, taps, sent_taps))
        received = lax.all_to_all(add_shares(kept, other_sent), "seq", 0, 0, axis_index_groups=alike)
        taps = join_pair(marks, taps, lax.ppermute(sent_taps, "seq", pairs), clips)
        taps = add_shares(taps, other_stream(taps))
        taps, received, grad_groups = lax.optimization_barrier((taps, received, grad_groups))
        by_head = grad_groups[:HEADS, 2 * group_width :]
        grad_attn_in = weave_heads(by_head, other_stream(by_head))
        pos_pieces = lax.all_to_all(taps, "seq", 0, 0, axis_index_groups=alike)
        pos_pieces = pos_pieces.reshape(GROUPS, -1, PIECE)
    else:
        attn_share = over_seq(regroup(attn_joined[0], [(3 * width // SHARE, near_rows)]))
        (grad_attn_in,) = spread_out(sum_pair(attn_share), [(own, 3 * width)], SHARE)
        (taps,) = taps_grad(marks, with_far_blocks(grad_groups, 1), shape, clips, width)
        taps = add_shares(taps, other_stream(taps))
        stem_joined = stem_shares[0]
        stem_joined = jnp.concatenate(
            [
                regroup(
                    stem_joined[:, :-32],
                    [(width // PIECE, near_chans), (chans // PIECE, 3 * near_chans)],
                ),
                regroup_small(stem_joined[:, -32:-16], (own, inner // count, own_chans)),
            ],
            axis=1,
        )
        received = lax.all_to_all(stem_joined, "seq", 0, 0)
        segments = count // RING
        by_tap = taps.reshape(2 * TURNS, 3, group_width, PIECE).transpose(0, 2, 1, 3)
        by_tap = by_tap.reshape(2 * TURNS, group_width, TAPS // 2, group_width)
        by_tap = by_tap.transpose(0, 2, 1, 3).reshape(segments, -1, 2 * PIECE)
        across = [[low_at + RING * j for j in range(segments)] for low_at in range(RING)]
        by_tap = lax.all_to_all(by_tap, "seq", 0, 0, axis_index_groups=across)
        by_tap = jnp.sum(by_tap.astype(jnp.float32), axis=0).astype(jnp.bfloat16)
        by_tap = by_tap.reshape(RING, own_taps, group_width, group_width).transpose(0, 2, 1, 3)
        pos_pieces = swap(by_tap.reshape(RING, group_width, own_taps * group_width))
    pos_grad = weave_taps(pos_pieces, own_taps, group_width)
    stem_total = jnp.sum(received.astype(jnp.float32), axis=0).astype(jnp.bfloat16)
    if count == RING:
        other = other_stream(stem_total)
        lower = lax.axis_index("rep") == 0
        stem_total = jnp.concatenate(
            [jnp.where(lower, stem_total, other), jnp.where(lower, other, stem_total)], axis=0
        )[:-16].astype(jnp.float32)
    else:
        stem_total = sum_pair(stem_total)
    grad_proj, grad_stem = spread_out(
        stem_total[:-16], [(own_chans, width), (3 * own_chans, chans)], PIECE
    )
    small = stem_total[-16:]
    grad_ffn_in, grad_ffn_out, grad_attn_out = ffn_parts(ffn_share)
    sample_grad = sample_grad.at[:1].add(carried)
    return (
        layer_out[None],
        sample_grad[None],
        grad_stem,
        small[14, :own_chans],
        small[15, :own_chans],
        grad_proj,
        pos_grad,
        small[:3, :own].T,
        small[3:12, :own].T,
        grad_attn_in,
        grad_attn_out,
        grad_ffn_in,
        small[12:14].reshape(-1)[: inner // count],
        grad_ffn_out,
    )


def solution(mesh):
    streams = P("rep", "seq", None)
    rows = P("seq", None)
    return jax.shard_map(
        local,
        mesh=mesh,
        in_specs=(streams, P("rep", None)) + (P(),) * 12 + (streams,),
        out_specs=(streams, streams, rows, P("seq"), P("seq"))
        + (rows,) * 7
        + (P("seq"), rows),
        check_vma=False,
    )
```

```python
import functools

import jax
import jax.numpy as jnp
from jax import lax
from jax.experimental import pallas as pl
from jax.experimental.pallas import tpu as pltpu
from jax.sharding import PartitionSpec as P

HEADS = 12
KERNEL = 128
GROUPS = 16
MAXLEN = 1536
RING = 16
HEAD_DIM = 64
EPS = 1e-05
BF = jnp.bfloat16
VMEM_WHOLE = pl.BlockSpec(memory_space=pltpu.VMEM)
SMEM_WHOLE = pl.BlockSpec(memory_space=pltpu.SMEM)
TOTAL, BEGIN, SEGMENT, KEYS, ACTIVE, CORE, REP = range(7)


def row_dot(left, right):
    return lax.dot_general(left, right, (((1,), (1,)), ((), ())), preferred_element_type=jnp.float32)


def plain_dot(left, right):
    return lax.dot_general(left, right, (((1,), (0,)), ((), ())), preferred_element_type=jnp.float32)


def over_rows_dot(left, right):
    return lax.dot_general(left, right, (((0,), (0,)), ((), ())), preferred_element_type=jnp.float32)


def store_pairs(refs, even, rows, values):
    if len(refs) == 1:
        for share, value in enumerate(values):
            refs[0][share, rows, :] = value
        return
    kept, sent = refs
    for at in range(len(values) // 2):
        first, second = values[2 * at], values[2 * at + 1]
        kept[at, rows, :] = jnp.where(even, first, second)
        sent[at, rows, :] = jnp.where(even, second, first)


def over_clips(clips, step, state):
    if clips <= 8:
        for clip in range(clips):
            state = step(clip, state)
        return state
    return lax.fori_loop(0, clips, step, state)


def clip_bounds(marks, clips, places):
    def step(clip, state):
        first, end = state
        mark = marks[clip]
        return (
            jnp.maximum(first, jnp.where(mark <= places, mark, 0)),
            jnp.minimum(end, jnp.where(mark > places, mark, marks[clips + TOTAL])),
        )

    return over_clips(clips, step, (jnp.zeros_like(places), jnp.zeros_like(places) + marks[clips + TOTAL]))


def like(shape, dtype=jnp.float32):
    return jax.ShapeDtypeStruct(shape, dtype)


def call(
    kernel, outs, scratch, args, name, flops, grid=None, in_specs=None, out_specs=None, limit=56, aliases=None
):
    size = sum(a.size * a.dtype.itemsize for a in args)
    size += sum(o.size * o.dtype.itemsize for o in outs)
    extra = {} if grid is None else {"grid": grid}
    return pl.pallas_call(
        kernel,
        out_shape=tuple(outs),
        in_specs=in_specs or [SMEM_WHOLE if a.dtype == jnp.int32 else VMEM_WHOLE for a in args],
        out_specs=out_specs or (VMEM_WHOLE,) * len(outs),
        scratch_shapes=scratch,
        compiler_params=pltpu.CompilerParams(vmem_limit_bytes=limit << 20),
        cost_estimate=pl.CostEstimate(flops=flops, bytes_accessed=size, transcendentals=0),
        name=name,
        input_output_aliases=aliases or {},
        **extra,
    )(*args)


Q_TILE = 512
K_TILE = 512
LOW = -1e30
LOG2E = 1.4426950408889634


def unpack_heads(packed_ref, targets):
    blocks, _, block = packed_ref.shape

    def one(at, carry):
        here = pl.ds(pl.multiple_of(at * block, block), block)
        for place, (rows, columns) in enumerate(targets):
            piece = packed_ref[at, place * HEAD_DIM : (place + 1) * HEAD_DIM]
            if rows is not None:
                rows[here, :] = piece.T
            if columns is not None:
                columns[0:HEAD_DIM, here] = piece
        return carry

    lax.fori_loop(0, blocks, one, 0)


def tile_spans(marks, clips, index):
    first = marks[clips + SEGMENT] + index * Q_TILE
    begin = marks[clips + KEYS]
    low, low_end = clip_bounds(marks, clips, first)
    high_start, high = clip_bounds(marks, clips, first + Q_TILE - 1)
    low, low_end, high_start, high = (v - begin for v in (low, low_end, high_start, high))
    up = K_TILE - 1
    start = lax.div(low, K_TILE)
    stop = jnp.where(marks[clips + ACTIVE] > 0, lax.div(high + up, K_TILE), start)
    inner = lax.div(high_start + up, K_TILE)
    outer = lax.div(high, K_TILE)
    whole = (low == high_start) & (inner < outer) & (stop > start)
    inner = jnp.where(whole, inner, stop)
    outer = jnp.where(whole, outer, stop)
    places = first + lax.broadcasted_iota(jnp.int32, (1, Q_TILE), 1)
    starts, ends = clip_bounds(marks, clips, places)
    return (start, inner, outer, stop), starts - begin, ends - begin


def allowed(column, starts, ends):
    places = column + lax.broadcasted_iota(jnp.int32, (K_TILE, 1), 0)
    return (places >= starts) & (places < ends)


def over_spans(spans, step, state):
    for at in range(3):
        state = lax.fori_loop(spans[at], spans[at + 1], functools.partial(step, at != 1), state)
    return state


def attend_kernel(clips, halo, marks, packed_ref, out_ref, wide_ref, log_ref, query_t, keys, value_t):
    rows = wide_ref.shape[1]
    block = packed_ref.shape[2]
    more = value_t.shape[0] - HEAD_DIM
    value_t[HEAD_DIM:] = jnp.where(
        lax.broadcasted_iota(jnp.int32, (more, value_t.shape[1]), 0) == 0, 1.0, 0.0
    ).astype(BF)
    unpack_heads(packed_ref, ((None, query_t), (keys, None), (None, value_t)))
    factor = HEAD_DIM ** (-0.5) * LOG2E

    def query_tile(index, carry):
        first = pl.multiple_of(index * Q_TILE, Q_TILE)
        q = query_t[:, pl.ds(halo * block + first, Q_TILE)]
        spans, starts, ends = tile_spans(marks, clips, index)

        def key_tile(masked, at, state):
            top, total = state
            column = pl.multiple_of(at * K_TILE, K_TILE)
            scores = plain_dot(keys[pl.ds(column, K_TILE), :], q) * factor
            if masked:
                scores = jnp.where(allowed(column, starts, ends), scores, LOW)
            new_top = jnp.maximum(top, jnp.max(scores, axis=0, keepdims=True))
            weight = jnp.exp2(scores - new_top).astype(BF)
            total = total * jnp.exp2(top - new_top) + plain_dot(
                value_t[:, pl.ds(column, K_TILE)], weight
            )
            return new_top, total

        top, total = over_spans(
            spans,
            key_tile,
            (
                jnp.full((1, Q_TILE), 0.5 * LOW, jnp.float32),
                jnp.zeros((HEAD_DIM + more, Q_TILE), jnp.float32),
            ),
        )
        mass = jnp.maximum(total[HEAD_DIM : HEAD_DIM + 1], 1e-37)
        attended = total[:HEAD_DIM] / mass
        wide_ref[:, pl.ds(first, Q_TILE)] = attended
        log_ref[:, pl.ds(first, Q_TILE)] = top + jnp.log2(mass)
        narrow = attended.astype(BF)
        for inner in range(Q_TILE // block):
            out_ref[index * (Q_TILE // block) + inner] = narrow[:, inner * block : (inner + 1) * block]
        return carry

    lax.fori_loop(0, rows // Q_TILE, query_tile, 0)


def attend(marks, packed, clips, halo):
    blocks, _, block = packed.shape
    rows = (blocks - 2 * halo) * block
    key_rows = blocks * block
    return call(
        functools.partial(attend_kernel, clips, halo),
        [
            like((blocks - 2 * halo, HEAD_DIM, block), BF),
            like((HEAD_DIM, rows)),
            like((1, rows)),
        ],
        [
            pltpu.VMEM((HEAD_DIM, key_rows), BF),
            pltpu.VMEM((key_rows, HEAD_DIM), BF),
            pltpu.VMEM((HEAD_DIM + 16, key_rows), BF),
        ],
        (marks, packed),
        "attend",
        25 * 10**9,
    )


def attend_back_kernel(
    clips, halo, marks, packed_ref, grad_ref, wide_ref, log_ref, out_ref,
    query_t, keys, key_t, values, grad_t, key_grads, value_grads,
):
    unpack_heads(packed_ref, ((None, query_t), (keys, key_t), (values, None)))
    unpack_heads(grad_ref, ((None, grad_t),))
    blocks, _, block = packed_ref.shape
    rows = wide_ref.shape[1]
    scale = HEAD_DIM ** (-0.5)
    key_grads[...] = jnp.zeros_like(key_grads)
    value_grads[...] = jnp.zeros_like(value_grads)
    if halo:
        out_ref[...] = jnp.zeros_like(out_ref)

    def query_tile(index, carry):
        first = pl.multiple_of(index * Q_TILE, Q_TILE)
        own = pl.ds(halo * block + first, Q_TILE)
        q_t, g_t = query_t[:, own], grad_t[:, pl.ds(first, Q_TILE)]
        log_total = log_ref[:, pl.ds(first, Q_TILE)]
        delta = jnp.sum(
            g_t.astype(jnp.float32) * wide_ref[:, pl.ds(first, Q_TILE)], axis=0, keepdims=True
        )
        spans, starts, ends = tile_spans(marks, clips, index)

        def key_tile(masked, at, running):
            column = pl.multiple_of(at * K_TILE, K_TILE)
            here = pl.ds(column, K_TILE)
            probs = jnp.exp2(plain_dot(keys[here, :], q_t) * (scale * LOG2E) - log_total)
            if masked:
                probs = jnp.where(allowed(column, starts, ends), probs, 0.0)
            prob_grad = plain_dot(values[here, :], g_t)
            score_grad = (probs * (prob_grad - delta)).astype(BF)
            value_grads[:, here] += row_dot(g_t, probs.astype(BF))
            key_grads[:, here] += row_dot(q_t, score_grad)
            return running + plain_dot(key_t[:, here], score_grad)

        query_grad = over_spans(spans, key_tile, jnp.zeros((HEAD_DIM, Q_TILE), jnp.float32))
        query_grad = (query_grad * scale).astype(BF)
        for inner in range(Q_TILE // block):
            spot = halo + index * (Q_TILE // block) + inner
            out_ref[spot, 0:HEAD_DIM] = query_grad[:, inner * block : (inner + 1) * block]
        return carry

    lax.fori_loop(0, rows // Q_TILE, query_tile, 0)

    def finish(spot, carry):
        here = pl.ds(pl.multiple_of(spot * block, block), block)
        out_ref[spot, HEAD_DIM : 2 * HEAD_DIM] = (key_grads[:, here] * scale).astype(BF)
        out_ref[spot, 2 * HEAD_DIM :] = value_grads[:, here].astype(BF)
        return carry

    lax.fori_loop(0, blocks, finish, 0)


def attend_back(marks, packed, grad, wide, log_total, clips, halo):
    blocks, lanes, block = packed.shape
    rows = wide.shape[1]
    key_rows = blocks * block
    return call(
        functools.partial(attend_back_kernel, clips, halo),
        [like((blocks, lanes, block), BF)],
        [
            pltpu.VMEM((HEAD_DIM, key_rows), BF),
            pltpu.VMEM((key_rows, HEAD_DIM), BF),
            pltpu.VMEM((HEAD_DIM, key_rows), BF),
            pltpu.VMEM((key_rows, HEAD_DIM), BF),
            pltpu.VMEM((HEAD_DIM, rows), BF),
            pltpu.VMEM((HEAD_DIM, key_rows), jnp.float32),
            pltpu.VMEM((HEAD_DIM, key_rows), jnp.float32),
        ],
        (marks, packed, grad, wide, log_total),
        "attend_back",
        35 * 10**9,
        limit=60,
    )[0]


TAPS = 16
SHOT = 384
TURNS = KERNEL // TAPS


def conv_weights_kernel(back, weight_ref, out_ref):
    group_width = out_ref.shape[1]
    if back:
        for group in range(GROUPS):
            lanes = slice(group_width * group, group_width * (group + 1))
            out_ref[group] = jnp.concatenate(
                [weight_ref[group_width * tap : group_width * (tap + 1), lanes] for tap in range(TAPS)],
                axis=1,
            )
    else:
        turned = weight_ref[...].T
        for group in range(GROUPS):
            out_ref[group] = turned[group_width * group : group_width * (group + 1)]


def conv_weights(back, weight, first, turns):
    width = weight.shape[1]
    group_width = width // GROUPS
    return call(
        functools.partial(conv_weights_kernel, back),
        [like((GROUPS, turns * group_width, TAPS * group_width), weight.dtype)],
        [],
        (weight,),
        "conv_weights_back" if back else "conv_weights",
        0,
        (turns,),
        [pl.BlockSpec((TAPS * group_width, width), lambda turn: (turn + first, 0))],
        (pl.BlockSpec((GROUPS, group_width, TAPS * group_width), lambda turn: (0, turn, 0)),),
    )[0]


def conv_kernel(back, clips, parts, marks, before_ref, rows_ref, after_ref, *refs):
    weight_refs, (out_ref, spaced, total) = refs[:parts], refs[parts:]
    group = pl.program_id(0)
    rows, width = rows_ref.shape
    half = KERNEL // 2
    long = rows + 2 * half
    group_width = width // GROUPS
    room = spaced.shape[1]
    places = marks[clips + BEGIN] - half + lax.broadcasted_iota(jnp.int32, (1, long), 1)
    ids = over_clips(
        clips,
        lambda clip, found: found + jnp.where(places >= marks[clip], 1, 0),
        jnp.zeros((1, long), jnp.int32),
    )
    ids = jnp.where((places >= 0) & (places < marks[clips + TOTAL]), ids, -1)

    def number_of(place):
        step = lambda clip, found: found + jnp.where(place >= marks[clip], 1, 0)
        return over_clips(clips, step, jnp.int32(0))

    first = number_of(marks[clips + BEGIN])
    count = number_of(marks[clips + BEGIN] + rows - 1) - first + 1

    @pl.when(group == 0)
    def _():
        turned = jnp.concatenate(
            [before_ref[...], rows_ref[...], after_ref[...]], axis=0
        ).astype(jnp.float32).T
        rest = jnp.zeros((width, room - long), jnp.float32)

        def of_clip(clip):
            return jnp.concatenate([jnp.where(ids == first + clip, turned, 0.0), rest], axis=1)

        spaced[...] = of_clip(0).astype(BF)

        def place(clip, carry):
            spaced[...] += pltpu.roll(of_clip(clip), clip * half, 1).astype(BF)
            return carry

        lax.fori_loop(1, count, place, 0)

    row = pl.multiple_of(group * group_width, group_width)
    shots = lax.div(rows + half * (count - 1) + SHOT - 1, SHOT)

    def shot(index, carry):
        base = pl.multiple_of(index * SHOT, 128)
        tile = spaced[pl.ds(row, group_width), pl.ds(base, SHOT + 2 * KERNEL)]
        moved = []
        for tap in range(TAPS):
            begin = TAPS - tap if back else tap
            moved.append(tile[:, begin : begin + SHOT + KERNEL])
        moved = jnp.concatenate(moved, axis=0)
        result = None
        turn = 0
        for weight_ref in weight_refs:
            product = plain_dot(weight_ref[0], moved)
            for inner in range(product.shape[0] // group_width):
                begin = (TURNS - 1 - turn if back else turn) * TAPS
                piece = product[inner * group_width : (inner + 1) * group_width, begin : begin + SHOT]
                result = piece if result is None else result + piece
                turn += 1
        total[pl.ds(row, group_width), pl.ds(base, SHOT)] = result
        return carry

    lax.fori_loop(0, shots, shot, 0)

    @pl.when(group == GROUPS - 1)
    def _():
        wide = total.shape[1]
        own = ids[:, half : half + rows]

        def collect(clip, carry):
            moved = pltpu.roll(total[...], lax.rem(wide - clip * half, wide), 1)[:, :rows]
            total[:, :rows] = jnp.where(own == first + clip, moved, total[:, :rows])
            return carry

        lax.fori_loop(1, count, collect, 0)
        out_ref[...] = total[:, :rows].T


def conv_rows(back, marks, before, value, after, weights, clips):
    rows, width = value.shape
    shots = -(-(rows + KERNEL // 2 * (clips - 1)) // SHOT)
    whole = lambda a: pl.BlockSpec(a.shape, lambda group: (0, 0))
    return call(
        functools.partial(conv_kernel, back, clips, len(weights)),
        [like((rows, width))],
        [
            pltpu.VMEM((width, SHOT * shots + 2 * KERNEL), BF),
            pltpu.VMEM((width, SHOT * shots), jnp.float32),
        ],
        (marks, before, value, after) + tuple(weights),
        "conv_back" if back else "conv",
        15 * 10**9,
        (GROUPS,),
        [SMEM_WHOLE, whole(before), whole(value), whole(after)]
        + [pl.BlockSpec((1,) + weight.shape[1:], lambda group: (group, 0, 0)) for weight in weights],
        (pl.BlockSpec((rows, width), lambda group: (0, 0)),),
        limit=48,
    )[0]


def taps_grad_kernel(
    clips, marks, both_ref, *refs
):
    half = KERNEL // 2
    out_refs, (inputs, spaced, input_cols, grad_cols) = refs[:-4], refs[-4:]
    group_width = inputs.shape[0]
    long = inputs.shape[1]
    blocks, _, block = both_ref.shape
    halo = (blocks - RING) // 2
    halo_rows = halo * block
    first = over_clips(
        clips,
        lambda clip, found: found + jnp.where(marks[clips + SEGMENT] >= marks[clip], 1, 0),
        jnp.int32(0),
    )
    origin = half + halo_rows
    span = input_cols.shape[1]

    def lay(first_row, begin_block, number, target, reach):
        for at in range(number):
            target[:, at * block : (at + 1) * block] = both_ref[
                begin_block + at, first_row : first_row + group_width
            ].astype(jnp.float32)
        target[:, number * block :] = jnp.zeros((group_width, long - number * block), jnp.float32)
        lanes = lax.broadcasted_iota(jnp.int32, (1, long), 1)
        places = marks[clips + SEGMENT] - reach + lanes
        held = lanes < number * block
        spaced[...] = jnp.zeros_like(spaced)

        def place(clip, carry):
            begin = jnp.where(clip > 0, marks[jnp.maximum(clip - 1, 0)], 0)
            keep = (places >= begin) & (places < marks[clip]) & held
            spaced[...] += pltpu.roll(
                jnp.where(keep, target[...], 0.0), origin - reach + half * (clip - first), 1
            )
            return carry

        lax.fori_loop(first, clips, place, 0)
        return spaced[...]

    laid = lay(0, 0, blocks, inputs, halo_rows)
    for turn in range(TURNS):
        begin = origin - half + turn * TAPS
        input_cols[turn * group_width : (turn + 1) * group_width, :] = laid[
            :, begin : begin + span
        ].astype(BF)
    laid = lay(group_width, halo, RING, inputs, 0)
    for tap in range(TAPS):
        grad_cols[tap * group_width : (tap + 1) * group_width, :] = laid[
            :, origin - tap : origin - tap + span
        ].astype(BF)
    result = row_dot(input_cols[...], grad_cols[...]).astype(BF)
    side_lanes = TAPS * group_width // 2
    even_core = marks[clips + CORE] == 0
    for piece in range(side_lanes // 128):
        values = []
        for place_at in range(2 * TURNS):
            turn, begin = place_at // 2, place_at % 2 * side_lanes + piece * 128
            values.append(result[turn * group_width : (turn + 1) * group_width, begin : begin + 128])
        store_pairs(out_refs, even_core, slice(piece * group_width, (piece + 1) * group_width), values)


def taps_grad(marks, both, shape, clips, width):
    blocks, _, block = both.shape
    group_width = width // GROUPS
    half = KERNEL // 2
    halo_rows = (blocks - RING) // 2 * block
    span = -(-(RING * block + half * clips) // 128) * 128
    long = span + 2 * halo_rows + half + 2 * KERNEL
    long = -(-long // 128) * 128
    more = TAPS * group_width // 2 // 128 * group_width
    return call(
        functools.partial(taps_grad_kernel, clips),
        [like((n, more, 128), BF) for n in shape],
        [
            pltpu.VMEM((group_width, long), jnp.float32),
            pltpu.VMEM((group_width, long), jnp.float32),
            pltpu.VMEM((TURNS * group_width, span), BF),
            pltpu.VMEM((TAPS * group_width, span), BF),
        ],
        (marks, both),
        "taps_grad",
        10**10,
        limit=60,
    )


def weave_taps_kernel(own_ref, out_ref):
    group_width = out_ref.shape[1] // GROUPS
    taps = out_ref.shape[0] // group_width
    pieces = own_ref.shape[1] // group_width
    both = []
    for group in range(GROUPS):
        rows = own_ref[group].astype(jnp.float32)
        both.append(
            jnp.concatenate([rows[at * group_width : (at + 1) * group_width] for at in range(pieces)], axis=1)
        )
    for tap in range(taps):
        lanes = slice(tap * group_width, (tap + 1) * group_width)
        out_ref[tap * group_width : (tap + 1) * group_width, :] = jnp.concatenate(
            [value[:, lanes] for value in both], axis=1
        )


def weave_taps(own, taps, group_width):
    return call(
        weave_taps_kernel, [like((taps * group_width, GROUPS * group_width))], [], (own,), "weave_taps", 0
    )[0]


def add_shares_kernel(own_ref, other_ref, out_ref):
    out_ref[...] = (own_ref[...].astype(jnp.float32) + other_ref[...].astype(jnp.float32)).astype(BF)


def add_shares(own, other):
    block = pl.BlockSpec((2,) + other.shape[1:], lambda at: (at, 0, 0))
    return call(
        add_shares_kernel,
        [like(other.shape, BF)],
        [],
        (own, other),
        "add_shares",
        0,
        (other.shape[0] // 2,),
        [block] * 2,
        (block,),
    )[0]


def split_shares_kernel(clips, marks, own_ref, other_ref, kept_ref, sent_ref):
    total = (own_ref[...].astype(jnp.float32) + other_ref[...].astype(jnp.float32)).astype(BF)
    rows = kept_ref.shape[1]
    lower = marks[clips + REP] == 0
    kept_ref[...] = jnp.where(lower, total[:, :rows], total[:, rows:])
    sent_ref[...] = jnp.where(lower, total[:, rows:], total[:, :rows])


def split_shares(marks, own, other, clips):
    shares, rows, lanes = own.shape
    return call(
        functools.partial(split_shares_kernel, clips),
        [like((shares, rows // 2, lanes), BF)] * 2,
        [],
        (marks, own, other),
        "split_shares",
        0,
    )


def join_stem_kernel(clips, marks, own_ref, other_ref, heads_ref, other_heads_ref, out_ref):
    below, rows = own_ref.shape[1], heads_ref.shape[1]
    out_ref[:, :below] = (own_ref[...].astype(jnp.float32) + other_ref[...].astype(jnp.float32)).astype(BF)
    first = marks[clips + CORE] == 0
    out_ref[:, below : below + rows] = jnp.where(first, heads_ref[...], other_heads_ref[...])
    out_ref[:, below + rows :] = jnp.where(first, other_heads_ref[...], heads_ref[...])


def join_stem(marks, own, other, heads, other_heads, clips):
    chips, below, lanes = own.shape
    return call(
        functools.partial(join_stem_kernel, clips),
        [like((chips, below + 2 * heads.shape[1], lanes), BF)],
        [],
        (marks, own, other, heads, other_heads),
        "join_stem",
        0,
    )[0]


def add_below_kernel(own_ref, other_ref, _, out_ref):
    add_shares_kernel(own_ref, other_ref, out_ref)


def add_below(own, other, straight):
    block = pl.BlockSpec((2,) + own.shape[1:], lambda at: (at, 0, 0))
    return call(
        add_below_kernel,
        [like(straight.shape, BF)],
        [],
        (own, other, straight),
        "add_below",
        0,
        (own.shape[0] // 2,),
        [block, block, pl.BlockSpec(memory_space=pl.ANY)],
        (pl.BlockSpec((2,) + own.shape[1:], lambda at: (at, 1, 0)),),
        aliases={2: 0},
    )[0]


def join_pair_kernel(clips, marks, taps_ref, other_ref, out_ref):
    rows = taps_ref.shape[1]
    first = marks[clips + CORE] == 0
    out_ref[:, :rows] = jnp.where(first, taps_ref[...], other_ref[...])
    out_ref[:, rows:] = jnp.where(first, other_ref[...], taps_ref[...])


def join_pair(marks, taps, other, clips):
    chips, rows, lanes = taps.shape
    return call(
        functools.partial(join_pair_kernel, clips),
        [like((chips, 2 * rows, lanes), BF)],
        [],
        (marks, taps, other),
        "join_pair",
        0,
    )[0]


SHARE = 384
PIECE = 128


def norm_parts(values):
    center = values - jnp.mean(values, axis=-1, keepdims=True)
    inverse = lax.rsqrt(jnp.mean(center * center, axis=-1, keepdims=True) + EPS)
    return center * inverse, inverse


def norm_back(unit, inverse, scales, grad):
    scaled = grad * scales
    back = inverse * (
        scaled
        - jnp.mean(scaled, axis=-1, keepdims=True)
        - unit * jnp.mean(scaled * unit, axis=-1, keepdims=True)
    )
    return back, row_sum(grad * unit), row_sum(grad)


def row_sum(values):
    return jnp.sum(values, axis=0, keepdims=True)


def gelu_both(values):
    below = 0.5 + 0.5 * lax.erf(values * 0.7071067811865476)
    bell = jnp.exp(-0.5 * values * values) * 0.3989422804014327
    return values * below, below + values * bell


def store_turned(values_b, out_ref, first):
    group_width = values_b.shape[1] // GROUPS
    turned = values_b.T
    for group in range(GROUPS):
        out_ref[group, first : first + group_width] = turned[group * group_width : (group + 1) * group_width]


def same_clip_next(marks, clips, rows):
    following = marks[clips + BEGIN] + 1 + lax.broadcasted_iota(jnp.int32, (rows, 1), 0)
    step = lambda clip, other: jnp.maximum(other, jnp.where(following == marks[clip], 1, 0))
    return over_clips(clips, step, jnp.zeros((rows, 1), jnp.int32)) == 0


def stem_kernel(
    clips, marks, samples_ref, next_ref, weight_ref, gain_ref, bias_ref, proj_ref, gains_ref, biases_ref,
    start_ref, start_b_ref, pre_ref, normed_ref, unfold_ref, table_ref, wide,
):
    rows, chans = pre_ref.shape
    table_ref[0:3] = gains_ref[...]
    table_ref[3:12] = biases_ref[...]
    last = lax.broadcasted_iota(jnp.int32, (rows, 1), 0) == rows - 1
    same = same_clip_next(marks, clips, rows)
    for lane in range(0, chans, PIECE):
        lanes = slice(lane, lane + PIECE)
        wide[...] = samples_ref[:, lanes].astype(jnp.float32)
        even = wide[pl.ds(0, rows, stride=2), :]
        unfold_ref[:, lanes] = even.astype(BF)
        unfold_ref[:, chans + lane : chans + lane + PIECE] = wide[pl.ds(1, rows, stride=2), :].astype(BF)
        moved = jnp.where(last, next_ref[:, lanes].astype(jnp.float32), pltpu.roll(even, rows - 1, 0))
        unfold_ref[:, 2 * chans + lane : 2 * chans + lane + PIECE] = jnp.where(same, moved, 0.0).astype(BF)
    pre = plain_dot(unfold_ref[...], weight_ref[...])
    pre_ref[...] = pre
    unit, _ = norm_parts(gelu_both(pre)[0])
    normed = (unit * gain_ref[...] + bias_ref[...]).astype(BF)
    normed_ref[...] = normed
    start = plain_dot(normed, proj_ref[...]) + table_ref[3:4]
    start_ref[...] = start
    start_b_ref[...] = start.astype(BF)


def stem(marks, samples, next_row, weight, gain, bias, proj, gains, biases, clips):
    rows = samples.shape[0] // 2
    chans, width = proj.shape
    return call(
        functools.partial(stem_kernel, clips),
        [
            like((rows, width)), like((rows, width), BF),
            like((rows, chans)), like((rows, chans), BF), like((rows, 3 * chans), BF), like((12, width)),
        ],
        [pltpu.VMEM((2 * rows, PIECE), jnp.float32)],
        (marks, samples, next_row, weight, gain, bias, proj, gains, biases),
        "stem",
        6 * 10**9,
    )


def project_kernel(conv_ref, start_ref, table_ref, weight_ref, hidden_ref, hidden_b_ref, packed_ref):
    rows, width = start_ref.shape
    mixed = start_ref[...] + gelu_both(conv_ref[...] + table_ref[4:5])[0]
    unit, _ = norm_parts(mixed)
    hidden = unit * table_ref[0:1] + table_ref[5:6]
    hidden_ref[...] = hidden
    hidden_b = hidden.astype(BF)
    hidden_b_ref[...] = hidden_b
    shifts = (table_ref[6:7], jnp.zeros((1, width), jnp.float32), table_ref[7:8])
    heads = width // HEAD_DIM
    for at, shift in enumerate(shifts):
        part = plain_dot(hidden_b, weight_ref[:, at * width : (at + 1) * width]) + shift
        turned = part.astype(BF).T
        for head in range(heads):
            packed_ref[head, at * HEAD_DIM : (at + 1) * HEAD_DIM] = turned[
                head * HEAD_DIM : (head + 1) * HEAD_DIM
            ]
    for head in range(heads, RING):
        packed_ref[head] = jnp.zeros_like(packed_ref[head])


def project_heads(conv_sum, start, table, weight):
    rows, width = start.shape
    return call(
        project_kernel,
        [like((rows, width)), like((rows, width), BF), like((RING, 3 * HEAD_DIM, rows), BF)],
        [],
        (conv_sum, start, table, weight),
        "project_heads",
        6 * 10**9,
    )


def middle_kernel(
    clips, marks, heads_ref, hidden_ref, table_ref, out_weight_ref, in_ref, in_bias_ref, back_ref, out_grad_ref,
    layer_ref, grad_heads_ref, grad_second_ref, sums_ref, in_bias_grad_ref, kept_ref, sent_ref, straight_ref,
    attended, before, second, second_b, second_t, inner_b, slope, total, grad_last, grad_last_b,
    joined, sems,
):
    step = pl.program_id(0)
    rows, width = hidden_ref.shape
    chunk = in_ref.shape[1]
    chunks = pl.num_programs(0) // 2
    heads = width // HEAD_DIM
    shares = kept_ref.shape[0]
    lower = marks[clips + REP] == 0
    in_rows = width // shares
    back_rows = chunk * chunks // shares
    owners = chunk // back_rows

    first_blocks = 3 * chunks // 4

    def moves(half, place, sem, act):
        for keeps, target in ((lower, (kept_ref, sent_ref)[half]), (~lower, (sent_ref, kept_ref)[half])):

            @pl.when(keeps)
            def _():
                act(pltpu.make_async_copy(joined.at[half].at[place], target.at[place], sem))

    def in_moves(at, act):
        @pl.when(at < first_blocks)
        def _():
            place = (slice(None), pl.ds(pl.multiple_of(at * in_rows, 16), in_rows))
            moves(0, place, sems.at[0, at], act)

        @pl.when(at >= first_blocks)
        def _():
            place = (slice(None), pl.ds(pl.multiple_of((at - first_blocks) * in_rows, 16), in_rows))
            act(pltpu.make_async_copy(joined.at[2].at[place], straight_ref.at[place], sems.at[0, at]))

    def back_moves(at, act):
        mine = pl.ds(at * owners, owners)
        moves(1, (mine, pl.ds(0, back_rows)), sems.at[1, at], act)
        place = (mine, pl.ds((chunks - first_blocks) * in_rows, back_rows))
        act(pltpu.make_async_copy(joined.at[2].at[place], straight_ref.at[place], sems.at[2, at]))

    def out_moves(act):
        moves(1, (slice(None), pl.ds(back_rows, 2 * in_rows)), sems.at[3, 0], act)

    def go(copy):
        copy.start()

    def wait(copy):
        copy.wait()

    @pl.when(step == 0)
    def _():
        for head in range(heads):
            attended[head * HEAD_DIM : (head + 1) * HEAD_DIM] = heads_ref[head]
        value = hidden_ref[...] + over_rows_dot(attended[...], out_weight_ref[...]) + table_ref[8:9]
        before[...] = value
        unit, _ = norm_parts(value)
        value = unit * table_ref[1:2] + table_ref[9:10]
        second[...] = value
        second_b[...] = value.astype(BF)
        second_t[...] = value.T.astype(BF)
        total[...] = jnp.zeros_like(total)

    @pl.when(step < chunks)
    def _():
        at = pl.multiple_of(step * chunk, chunk)
        value, back = gelu_both(plain_dot(second_b[...], in_ref[...]) + in_bias_ref[:, pl.ds(at, chunk)])
        value_b = value.astype(BF)
        inner_b[step] = value_b
        slope[step] = back
        total[...] += plain_dot(value_b, back_ref[...])

    @pl.when(step == chunks - 1)
    def _():
        unit, inverse = norm_parts(second[...] + total[...] + table_ref[10:11])
        layer_ref[...] = (unit * table_ref[2:3] + table_ref[11:12]).astype(BF)
        back, gain, bias = norm_back(unit, inverse, table_ref[2:3], out_grad_ref[...].astype(jnp.float32))
        grad_last[...] = back
        grad_last_b[...] = back.astype(BF)
        total[...] = back
        sums_ref[0:1] = gain
        sums_ref[1:2] = bias
        sums_ref[2:3] = row_sum(back)

    @pl.when(step >= chunks)
    def _():
        turn = step - chunks
        at = pl.multiple_of(turn * chunk, chunk)
        grad = row_dot(grad_last_b[...], back_ref[...]) * slope[turn]
        in_bias_grad_ref[:, pl.ds(at, chunk)] = row_sum(grad)
        grad_b = grad.astype(BF)
        total[...] += row_dot(grad_b, in_ref[...])
        product = plain_dot(second_t[...], grad_b).astype(BF)
        straight = turn >= first_blocks
        row = pl.multiple_of(jnp.where(straight, turn - first_blocks, turn) * in_rows, 16)
        for share in range(shares):
            joined[jnp.where(straight, 2, 0), share, pl.ds(row, in_rows), :] = product[
                share * in_rows : (share + 1) * in_rows
            ]
        in_moves(turn, go)
        product = over_rows_dot(inner_b[turn], grad_last_b[...]).astype(BF)
        for owner in range(owners):
            for place in range(width // SHARE):
                begin = (chunks - first_blocks) * in_rows if place else 0
                joined[1 + place, turn * owners + owner, begin : begin + back_rows, :] = product[
                    owner * back_rows : (owner + 1) * back_rows, place * SHARE : (place + 1) * SHARE
                ]
        back_moves(turn, go)

    @pl.when(step == 2 * chunks - 1)
    def _():
        unit, inverse = norm_parts(before[...])
        back, gain, bias = norm_back(unit, inverse, table_ref[1:2], total[...])
        grad_second_ref[...] = back
        sums_ref[3:4] = row_sum(back)
        sums_ref[4:5] = gain
        sums_ref[5:6] = bias
        sums_ref[6:8] = jnp.zeros((2, width), jnp.float32)
        back_b = back.astype(BF)
        grads = row_dot(out_weight_ref[...], back_b).astype(BF)
        for head in range(heads):
            grad_heads_ref[head] = grads[head * HEAD_DIM : (head + 1) * HEAD_DIM]
        for head in range(heads, RING):
            grad_heads_ref[head] = jnp.zeros_like(grad_heads_ref[head])
        product = plain_dot(attended[...], back_b).astype(BF)
        for share in range(shares):
            for place in range(width // SHARE):
                begin = back_rows + place * in_rows
                joined[1, share, begin : begin + in_rows, :] = product[
                    share * in_rows : (share + 1) * in_rows, place * SHARE : (place + 1) * SHARE
                ]
        out_moves(go)

        def finish(at, carry):
            in_moves(at, wait)
            back_moves(at, wait)
            return carry

        lax.fori_loop(0, chunks, finish, 0)
        out_moves(wait)


def middle(marks, clips, heads, hidden, table, out_weight, ffn_in, in_bias, ffn_out, out_grad, count):
    rows, width = hidden.shape
    inner = ffn_in.shape[1]
    chunk = SHARE
    chunks = inner // chunk
    own = lambda shape: pl.BlockSpec(shape, lambda step: (0,) * len(shape))
    third = (2 * inner + width) * (width // count) // SHARE // 3
    outs = [
        like((rows, width), BF),
        like((RING, HEAD_DIM, rows), BF),
        like((rows, width)),
        like((8, width)),
        like((1, inner)),
        like((count, third, SHARE), BF),
        like((count, third, SHARE), BF),
        like((count, 2 * third, SHARE), BF),
    ]
    args = (marks, heads, hidden, table, out_weight, ffn_in, in_bias, ffn_out, out_grad)
    in_specs = [SMEM_WHOLE] + [own(a.shape) for a in args[1:]]
    in_specs[5] = pl.BlockSpec((width, chunk), lambda step: (0, step % chunks))
    in_specs[7] = pl.BlockSpec((chunk, width), lambda step: (step % chunks, 0))
    out_specs = [own(o.shape) for o in outs]
    out_specs[5] = out_specs[6] = out_specs[7] = pl.BlockSpec(memory_space=pl.ANY)
    scratch = [
        pltpu.VMEM((width, rows), BF),
        pltpu.VMEM((rows, width), jnp.float32),
        pltpu.VMEM((rows, width), jnp.float32),
        pltpu.VMEM((rows, width), BF),
        pltpu.VMEM((width, rows), BF),
        pltpu.VMEM((chunks, rows, chunk), BF),
        pltpu.VMEM((chunks, rows, chunk), jnp.float32),
        pltpu.VMEM((rows, width), jnp.float32),
        pltpu.VMEM((rows, width), jnp.float32),
        pltpu.VMEM((rows, width), BF),
        pltpu.VMEM((3,) + outs[5].shape, BF),
        pltpu.SemaphoreType.DMA((4, chunks)),
    ]
    return call(
        functools.partial(middle_kernel, clips), outs, scratch, args, "middle", 2 * 10**10, (2 * chunks,), in_specs, tuple(out_specs)
    )


def after_heads_kernel(
    whole, packed_ref, grad_second_ref, hidden_ref, conv_ref, start_ref, table_ref, weight_ref, *refs
):
    rows, width = hidden_ref.shape
    heads = width // HEAD_DIM
    if whole:
        mixed_ref, conv_b_ref, groups_ref, sums_ref, grads = refs
    else:
        mixed_ref, conv_b_ref, groups_ref, sums_ref, joined_ref, grads, hidden_t = refs
    for head in range(heads):
        for part in range(3):
            row = part * width + head * HEAD_DIM
            grads[row : row + HEAD_DIM] = packed_ref[head, part * HEAD_DIM : (part + 1) * HEAD_DIM]
    if not whole:
        shares = joined_ref.shape[0]
        own_rows = width // shares
        hidden_t[...] = hidden_ref[...].T.astype(BF)

        def weight_block(place, carry):
            row = pl.multiple_of(place * SHARE, SHARE)
            product = row_dot(hidden_t[...], grads[pl.ds(row, SHARE), :]).astype(BF)
            for share in range(shares):
                joined_ref[share, pl.ds(pl.multiple_of(place * own_rows, 16), own_rows), :] = product[
                    share * own_rows : (share + 1) * own_rows
                ]
            return carry

        lax.fori_loop(0, 3 * width // SHARE, weight_block, 0)
    back = grad_second_ref[...] + plain_dot(weight_ref[...], grads[...]).T
    value, slope = gelu_both(conv_ref[...] + table_ref[4:5])
    unit, inverse = norm_parts(start_ref[...] + value)
    mixed, gain, bias = norm_back(unit, inverse, table_ref[0:1], back)
    mixed_ref[...] = mixed
    conv = mixed * slope
    conv_b = conv.astype(BF)
    conv_b_ref[...] = conv_b
    store_turned(start_ref[...].astype(BF), groups_ref, 0)
    store_turned(conv_b, groups_ref, width // GROUPS)
    sums_ref[0:1] = gain
    sums_ref[1:2] = bias
    sums_ref[2:3] = row_sum(conv)
    ones = jnp.ones((8, rows), BF)
    sums_ref[3:4] = row_dot(ones, grads[:width])[0:1]
    sums_ref[4:5] = row_dot(ones, grads[2 * width :])[0:1]
    sums_ref[5:8] = jnp.zeros((3, width), jnp.float32)


def after_heads(packed, grad_second, hidden, conv_sum, start, table, weight, whole):
    rows, width = hidden.shape
    outs = [
        like((rows, width)),
        like((rows, width), BF),
        like((GROUPS, 2 * width // GROUPS, rows), BF),
        like((8, width)),
    ]
    scratch = [pltpu.VMEM((3 * width, rows), BF)]
    args = (packed, grad_second, hidden, conv_sum, start, table, weight)
    if not whole:
        outs.append(like((RING, width // RING * 3 * width // SHARE, SHARE), BF))
        scratch.append(pltpu.VMEM((width, rows), BF))
    return call(
        functools.partial(after_heads_kernel, whole), outs, scratch, args, "after_heads", 5 * 10**9
    )


def head_grads_kernel(clips, marks, packed_ref, hidden_ref, other_ref, kept_ref, sent_ref, turned):
    blocks, lines, block = packed_ref.shape
    core = marks[clips + CORE]
    width = hidden_ref.shape[2]

    def one(at, total):
        total = total + plain_dot(packed_ref[2 * at + core], hidden_ref[at])
        return total + plain_dot(packed_ref[2 * at + 1 - core], other_ref[at])

    total = lax.fori_loop(0, blocks // 2, one, jnp.zeros((lines, width), jnp.float32))
    turned[...] = jnp.concatenate([total, jnp.zeros((block - lines, width), jnp.float32)], axis=0).T.astype(BF)
    own = width // RING
    for piece in range(block // PIECE):
        store_pairs(
            (kept_ref, sent_ref),
            core == 0,
            slice(piece * own, (piece + 1) * own),
            [
                turned[share * own : (share + 1) * own, piece * PIECE : (piece + 1) * PIECE]
                for share in range(RING)
            ],
        )


def head_grads(marks, packed, hidden, other, clips):
    block = packed.shape[2]
    width = hidden.shape[2]
    return call(
        functools.partial(head_grads_kernel, clips),
        [like((RING // 2, block // PIECE * width // RING, PIECE), BF)] * 2,
        [pltpu.VMEM((width, block), BF)],
        (marks, packed, hidden, other),
        "head_grads",
        3 * 10**9,
    )


def weave_heads_kernel(own_ref, other_ref, out_ref):
    heads = own_ref.shape[0]
    rows = out_ref.shape[0]
    for part in range(3):
        piece, begin = divmod(part * HEAD_DIM, PIECE)
        place = (slice(piece * rows, (piece + 1) * rows), slice(begin, begin + HEAD_DIM))
        out_ref[:, part * heads * HEAD_DIM : (part + 1) * heads * HEAD_DIM] = jnp.concatenate(
            [
                own_ref[head][place].astype(jnp.float32) + other_ref[head][place].astype(jnp.float32)
                for head in range(heads)
            ],
            axis=1,
        )


def weave_heads(own, other):
    heads, rows = own.shape[0], own.shape[1] // 2
    return call(
        weave_heads_kernel, [like((rows, 3 * heads * HEAD_DIM))], [], (own, other), "weave_heads", 0
    )[0]


def stem_back_kernel(
    clips, marks, input_ref, mixed_ref, normed_ref, pre_ref, unfold_ref, weight_ref, gain_ref, proj_ref,
    middle_sums_ref, inner_sums_ref, after_sums_ref,
    samples_ref, carried_ref, *refs,
):
    rows, chans = pre_ref.shape
    width = input_ref.shape[1]
    joined_refs, (table, spread, woven) = refs[:-3], refs[-3:]
    shares = RING
    even_core = marks[clips + CORE] == 0
    start = mixed_ref[...] + input_ref[...]
    start_b = start.astype(BF)

    def share_out(product, begin):
        own, columns = product.shape[0] // shares, product.shape[1]
        for place in range(columns // PIECE):
            at = begin + place * own
            store_pairs(
                joined_refs,
                even_core,
                slice(at, at + own),
                [
                    product[share * own : (share + 1) * own, place * PIECE : (place + 1) * PIECE]
                    for share in range(shares)
                ],
            )
        return begin + own * columns // PIECE

    at = share_out(over_rows_dot(normed_ref[...], start_b).astype(BF), 0)
    value, slope = gelu_both(pre_ref[...])
    unit, inverse = norm_parts(value)
    feature, gain_sum, bias_sum = norm_back(
        unit, inverse, gain_ref[...], row_dot(start_b, proj_ref[...])
    )
    pre_b = (feature * slope).astype(BF)
    taps_t = over_rows_dot(unfold_ref[...], pre_b).astype(BF)
    at = share_out(taps_t, at)
    first = row_dot(pre_b, weight_ref[:chans])
    same = same_clip_next(marks, clips, rows)
    follow = jnp.where(same, row_dot(pre_b, weight_ref[2 * chans :]), 0.0)
    carried_ref[...] = follow[rows - 1 :]
    moved = pltpu.roll(follow, 1, 0)
    top = lax.broadcasted_iota(jnp.int32, (rows, 1), 0) == 0
    even = first + jnp.where(top, 0.0, moved)
    odd = row_dot(pre_b, weight_ref[chans : 2 * chans])
    for lane in range(0, chans, PIECE):
        woven[pl.ds(0, rows, stride=2), :] = even[:, lane : lane + PIECE]
        woven[pl.ds(1, rows, stride=2), :] = odd[:, lane : lane + PIECE]
        samples_ref[:, lane : lane + PIECE] = woven[...]
    table[0:1] = after_sums_ref[0:1]
    table[1:2] = middle_sums_ref[4:5]
    table[2:3] = middle_sums_ref[0:1]
    table[3:4] = row_sum(start)
    table[4:5] = after_sums_ref[2:3]
    table[5:6] = after_sums_ref[1:2]
    table[6:7] = after_sums_ref[3:4]
    table[7:8] = after_sums_ref[4:5]
    table[8:9] = middle_sums_ref[3:4]
    table[9:10] = middle_sums_ref[5:6]
    table[10:11] = middle_sums_ref[2:3]
    table[11:12] = middle_sums_ref[1:2]
    spread[...] = jnp.zeros_like(spread)
    own, own_chans = width // shares, chans // shares
    own_inner = inner_sums_ref.shape[1] // shares
    for share in range(shares):
        spread[share, 0:12, 0:own] = table[:, share * own : (share + 1) * own]
        for place in range(-(-own_inner // PIECE)):
            length = min(PIECE, own_inner - place * PIECE)
            begin = share * own_inner + place * PIECE
            spread[share, 12 + place : 13 + place, 0:length] = inner_sums_ref[:, begin : begin + length]
        lanes = slice(share * own_chans, (share + 1) * own_chans)
        spread[share, 14:15, 0:own_chans] = gain_sum[:, lanes]
        spread[share, 15:16, 0:own_chans] = bias_sum[:, lanes]
    store_pairs(
        joined_refs, even_core, slice(at, at + 32), [spread[share].astype(BF) for share in range(shares)]
    )


def stem_back(marks, input_grad, mixed, normed, pre, unfold, weight, gain, proj, sums, shares, clips):
    rows, chans = pre.shape
    width = input_grad.shape[1]
    pieces = (chans // RING * width + 3 * chans // RING * chans) // PIECE + 32
    return call(
        functools.partial(stem_back_kernel, clips),
        [like((2 * rows, chans)), like((1, chans))] + [like((n, pieces, PIECE), BF) for n in shares],
        [pltpu.VMEM((12, width), jnp.float32), pltpu.VMEM((RING, 32, PIECE), jnp.float32),
         pltpu.VMEM((2 * rows, PIECE), jnp.float32)],
        (marks, input_grad, mixed, normed, pre, unfold, weight, gain, proj) + sums,
        "stem_back",
        6 * 10**9,
    )


def from_behind(value, axis, steps):
    count = lax.axis_size(axis)
    initial, last = (max(0, -steps), min(count, count - steps))
    return lax.ppermute(value, axis, [(source, source + steps) for source in range(initial, last)])


def edges(value, width):
    length = value.shape[0]
    return from_behind(value[length - width :], "seq", 1), from_behind(value[:width], "seq", -1)


def near_groups():
    size = lax.axis_size("seq")
    return [[base + i for i in range(RING)] for base in range(0, size, RING)]


def swap(value):
    groups = None if lax.axis_size("seq") == RING else near_groups()
    return lax.all_to_all(value, "seq", 0, 0, axis_index_groups=groups)


def with_far_blocks(value, count):
    if lax.axis_size("seq") == RING or count == 0:
        return value
    before = from_behind(value[value.shape[0] - count :], "seq", RING)
    after = from_behind(value[:count], "seq", -RING)
    return jnp.concatenate([before, value, after], axis=0)


def fold_far_blocks(value, count):
    if lax.axis_size("seq") == RING or count == 0:
        return value
    own = value[count : value.shape[0] - count]
    to_before = from_behind(value[:count], "seq", -RING)
    to_after = from_behind(value[value.shape[0] - count :], "seq", RING)
    wide = own.astype(jnp.float32)
    wide = wide.at[wide.shape[0] - count :].add(to_before.astype(jnp.float32))
    wide = wide.at[:count].add(to_after.astype(jnp.float32))
    return wide.astype(value.dtype)


def other_stream(share):
    return lax.ppermute(share, "rep", [(0, 1), (1, 0)])


def sum_pair(share):
    return share.astype(jnp.float32) + other_stream(share).astype(jnp.float32)


def spread_out(total, sizes, lanes):
    out, at = [], 0
    for rows, columns in sizes:
        parts = []
        for _ in range(columns // lanes):
            parts.append(total[at : at + rows])
            at += rows
        out.append(jnp.concatenate(parts, axis=1))
    return out


def regroup(joined, blocks):
    count = lax.axis_size("seq")
    if count == RING:
        return joined
    parts = count // RING
    lanes = joined.shape[2]
    out, at = [], 0
    for number, rows in blocks:
        piece = joined[:, at : at + number * rows]
        at += number * rows
        piece = piece.reshape(RING, number, parts, rows // parts, lanes).transpose(0, 2, 1, 3, 4)
        out.append(piece.reshape(count, number * rows // parts, lanes))
    return jnp.concatenate(out, axis=1)


def regroup_small(small, widths):
    count = lax.axis_size("seq")
    if count == RING:
        return small
    parts = count // RING
    own, own_inner, own_chans = widths
    lanes = small.shape[2]
    table = small[:, :12, : own * parts].reshape(RING, 12, parts, own).transpose(0, 2, 1, 3)
    table = jnp.pad(table.reshape(count, 12, own), ((0, 0), (0, 0), (0, lanes - own)))
    wide = small[:, 12:14].reshape(RING, 2 * lanes)[:, : own_inner * parts].reshape(count, own_inner)
    wide = jnp.pad(wide, ((0, 0), (0, 2 * lanes - own_inner))).reshape(count, 2, lanes)
    stems = small[:, 14:16, : own_chans * parts].reshape(RING, 2, parts, own_chans).transpose(0, 2, 1, 3)
    stems = jnp.pad(stems.reshape(count, 2, own_chans), ((0, 0), (0, 0), (0, lanes - own_chans)))
    return jnp.concatenate([table, wide, stems], axis=1)


def over_seq(joined):
    return lax.psum_scatter(joined, "seq", scatter_dimension=0, tiled=False).astype(jnp.bfloat16)


def local(
    samples,
    clip_lengths,
    stem_weight,
    stem_gain,
    stem_bias,
    proj_weight,
    pos_weight,
    norm_gains,
    biases,
    attn_in,
    attn_out,
    ffn_in,
    ffn_in_bias,
    ffn_out,
    out_grad,
):
    rows_dev = out_grad.shape[1]
    width = attn_out.shape[0]
    chans = stem_weight.shape[1]
    inner = ffn_in.shape[1]
    group_width = width // GROUPS
    count = lax.axis_size("seq")
    place = lax.axis_index("seq")
    total = rows_dev * count
    begin = place * rows_dev
    ends = jnp.cumsum(clip_lengths[0])
    clips = ends.shape[0]
    half = KERNEL // 2
    far = 0 if count == RING else -(-MAXLEN // rows_dev)
    segment_begin = (place // RING) * RING * rows_dev
    active = jnp.where(place % RING < HEADS, 1, 0)
    marks = jnp.concatenate(
        [ends, jnp.stack([jnp.int32(total), begin, segment_begin, segment_begin - far * rows_dev, active, place % 2, lax.axis_index("rep") if count == RING else 0])]
    ).astype(jnp.int32)
    next_row = from_behind(samples[0, :1], "seq", -1)
    one_weights = conv_weights(False, pos_weight, 0, TURNS // 2)
    next_row, one_weights = lax.optimization_barrier((next_row, one_weights))
    start_x, start_b, stem_pre, normed_b, unfold, table = stem(
        marks, samples[0], next_row, stem_weight, stem_gain[None], stem_bias[None], proj_weight,
        norm_gains.T, biases.T, clips,
    )
    before, after = edges(start_b, half)
    rest_source, _ = lax.optimization_barrier((pos_weight, table))
    rest_weights = conv_weights(False, rest_source, TURNS // 2, TURNS // 2)
    before, after, rest_weights = lax.optimization_barrier((before, after, rest_weights))
    conv_sum = conv_rows(False, marks, before, start_b, after, (one_weights, rest_weights), clips)
    hidden, hidden_b, packed = project_heads(conv_sum, start_x, table, attn_in)
    pairs = [(i, i ^ 1) for i in range(count)]
    alike = [list(range(core, count, 2)) for core in range(2)]
    back_source, _ = lax.optimization_barrier((pos_weight, hidden))
    packed = with_far_blocks(swap(packed), far)
    back_weights = conv_weights(True, back_source, 0, TURNS)
    packed, back_weights = lax.optimization_barrier((packed, back_weights))
    attended_heads, wide, log_total = attend(marks, packed, clips, far)
    attended_heads, hidden_b = lax.optimization_barrier((attended_heads, hidden_b))
    if count == RING:
        gathered = lax.all_gather(hidden_b, "seq", axis=0, tiled=False, axis_index_groups=alike)
    layer_out, grad_heads, grad_pre_second, middle_sums, inner_sums, ffn_kept, ffn_sent, straight = middle(
        marks, clips, swap(attended_heads), hidden, table, attn_out, ffn_in, ffn_in_bias[None], ffn_out, out_grad[0],
        RING,
    )
    near_rows, near_chans, near_inner = width // RING, chans // RING, inner // RING
    if count == RING:
        ffn_other = other_stream(ffn_sent)
    grad_heads = swap(grad_heads)
    packed_grad = attend_back(marks, packed, grad_heads, wide, log_total, clips, far)
    if count == RING:
        packed_grad, gathered = lax.optimization_barrier((packed_grad, gathered))
        other_gathered = lax.ppermute(gathered, "seq", pairs)
        own_heads, sent_heads = head_grads(marks, packed_grad, gathered, other_gathered, clips)
    swapped = swap(fold_far_blocks(packed_grad, far))
    if count == RING:
        other_heads = lax.ppermute(sent_heads, "seq", pairs)
        ffn_other, own_heads = lax.optimization_barrier((ffn_other, own_heads))
        ffn_joined = add_below(ffn_kept, ffn_other, straight)
        swapped, own_heads, ffn_joined = lax.optimization_barrier((swapped, own_heads, ffn_joined))
    grad_mixed, grad_conv_b, grad_packed, after_sums, *attn_joined = after_heads(
        swapped, grad_pre_second, hidden, conv_sum, start_x, table, attn_in, count == RING
    )
    if count != RING:
        ffn_joined = jnp.concatenate([straight[:, : ffn_kept.shape[1]], ffn_kept, ffn_sent], axis=1)
        first_blocks = 3 * inner // SHARE // 4
        ffn_joined = regroup(
            ffn_joined,
            [
                (inner // SHARE - first_blocks, near_rows),
                (1, near_inner),
                (first_blocks, near_rows),
                (1, near_inner),
                (2, near_rows),
            ],
        )
    ffn_share = over_seq(ffn_joined)
    before, after = edges(grad_conv_b, half)
    before, after, grad_packed = lax.optimization_barrier((before, after, grad_packed))
    grad_groups = swap(grad_packed)
    input_grad = conv_rows(True, marks, before, grad_conv_b, after, (back_weights,), clips)
    shape = (RING // 2,) * 2 if count == RING else (RING,)
    sample_grad, carried, *stem_shares = stem_back(
        marks, input_grad, grad_mixed, normed_b, stem_pre, unfold, stem_weight, stem_gain[None],
        proj_weight, (middle_sums, inner_sums, after_sums), shape, clips,
    )
    carried = from_behind(carried, "seq", 1)
    own = width // count
    own_chans = chans // count
    own_taps = KERNEL // count

    def ffn_parts(share):
        other = other_stream(share)
        if count == RING:
            at = share.shape[0] // 2
            lower = lax.axis_index("rep") == 0
            share = jnp.concatenate(
                [
                    share[:at].astype(jnp.float32) + other[:at].astype(jnp.float32),
                    jnp.where(lower, share[at:], other[at:]).astype(jnp.float32),
                    jnp.where(lower, other[at:], share[at:]).astype(jnp.float32),
                ],
                axis=0,
            )
        else:
            share = share.astype(jnp.float32) + other.astype(jnp.float32)
        most = 3 * inner // 4
        sizes = [(own, inner - most), (inner // count, SHARE), (own, most), (inner // count, SHARE), (own, width)]
        in_end, back_end, in_start, back_start, out = spread_out(share, sizes, SHARE)
        return (
            jnp.concatenate([in_start, in_end], axis=1),
            jnp.concatenate([back_start, back_end], axis=1),
            out,
        )

    if count == RING:
        kept, sent = split_shares(marks, stem_shares[0], lax.ppermute(stem_shares[1], "seq", pairs), clips)
        other_sent = other_stream(sent)
        taps, sent_taps = taps_grad(marks, grad_groups, shape, clips, width)
        sample_grad = sample_grad.at[:1].add(carried)
        other_sent, taps, sent_taps, sample_grad = lax.optimization_barrier(
            (other_sent, taps, sent_taps, sample_grad)
        )
        stem_joined = join_stem(marks, kept, other_sent, own_heads, other_heads, clips)
        received = lax.all_to_all(stem_joined, "seq", 0, 0, axis_index_groups=alike)
        taps = join_pair(marks, taps, lax.ppermute(sent_taps, "seq", pairs), clips)
        taps = add_shares(taps, other_stream(taps))
        taps, received = lax.optimization_barrier((taps, received))
        by_head = received[:, kept.shape[1] :].reshape(RING, -1, PIECE)[:HEADS]
        received = received[:, : kept.shape[1]]
        grad_attn_in = weave_heads(by_head, other_stream(by_head))
        pos_pieces = lax.all_to_all(taps, "seq", 0, 0, axis_index_groups=alike)
        pos_pieces = pos_pieces.reshape(GROUPS, -1, PIECE)
    else:
        sample_grad = sample_grad.at[:1].add(carried)
        attn_share = over_seq(regroup(attn_joined[0], [(3 * width // SHARE, near_rows)]))
        (grad_attn_in,) = spread_out(sum_pair(attn_share), [(own, 3 * width)], SHARE)
        (taps,) = taps_grad(marks, with_far_blocks(grad_groups, 1), shape, clips, width)
        taps = add_shares(taps, other_stream(taps))
        stem_joined = stem_shares[0]
        stem_joined = jnp.concatenate(
            [
                regroup(
                    stem_joined[:, :-32],
                    [(width // PIECE, near_chans), (chans // PIECE, 3 * near_chans)],
                ),
                regroup_small(stem_joined[:, -32:-16], (own, inner // count, own_chans)),
            ],
            axis=1,
        )
        received = lax.all_to_all(stem_joined, "seq", 0, 0)
        segments = count // RING
        by_tap = taps.reshape(2 * TURNS, 3, group_width, PIECE).transpose(0, 2, 1, 3)
        by_tap = by_tap.reshape(2 * TURNS, group_width, TAPS // 2, group_width)
        by_tap = by_tap.transpose(0, 2, 1, 3).reshape(segments, -1, 2 * PIECE)
        across = [[low_at + RING * j for j in range(segments)] for low_at in range(RING)]
        by_tap = lax.all_to_all(by_tap, "seq", 0, 0, axis_index_groups=across)
        by_tap = jnp.sum(by_tap.astype(jnp.float32), axis=0).astype(jnp.bfloat16)
        by_tap = by_tap.reshape(RING, own_taps, group_width, group_width).transpose(0, 2, 1, 3)
        pos_pieces = swap(by_tap.reshape(RING, group_width, own_taps * group_width))
    pos_grad = weave_taps(pos_pieces, own_taps, group_width)
    stem_total = jnp.sum(received.astype(jnp.float32), axis=0).astype(jnp.bfloat16)
    if count == RING:
        other = other_stream(stem_total)
        lower = lax.axis_index("rep") == 0
        stem_total = jnp.concatenate(
            [jnp.where(lower, stem_total, other), jnp.where(lower, other, stem_total)], axis=0
        )[:-16].astype(jnp.float32)
    else:
        stem_total = sum_pair(stem_total)
    grad_proj, grad_stem = spread_out(
        stem_total[:-16], [(own_chans, width), (3 * own_chans, chans)], PIECE
    )
    small = stem_total[-16:]
    grad_ffn_in, grad_ffn_out, grad_attn_out = ffn_parts(ffn_share)
    return (
        layer_out[None],
        sample_grad[None],
        grad_stem,
        small[14, :own_chans],
        small[15, :own_chans],
        grad_proj,
        pos_grad,
        small[:3, :own].T,
        small[3:12, :own].T,
        grad_attn_in,
        grad_attn_out,
        grad_ffn_in,
        small[12:14].reshape(-1)[: inner // count],
        grad_ffn_out,
    )


def solution(mesh):
    streams = P("rep", "seq", None)
    rows = P("seq", None)
    return jax.shard_map(
        local,
        mesh=mesh,
        in_specs=(streams, P("rep", None)) + (P(),) * 12 + (streams,),
        out_specs=(streams, streams, rows, P("seq"), P("seq"))
        + (rows,) * 7
        + (P("seq"), rows),
        check_vma=False,
    )
```

```python
import functools

import jax
import jax.numpy as jnp
from jax import lax
from jax.experimental import pallas as pl
from jax.experimental.pallas import tpu as pltpu
from jax.sharding import PartitionSpec as P

HEADS = 12
KERNEL = 128
GROUPS = 16
MAXLEN = 1536
RING = 16
HEAD_DIM = 64
EPS = 1e-05
BF = jnp.bfloat16
VMEM_WHOLE = pl.BlockSpec(memory_space=pltpu.VMEM)
SMEM_WHOLE = pl.BlockSpec(memory_space=pltpu.SMEM)
TOTAL, BEGIN, SEGMENT, KEYS, ACTIVE, CORE, REP = range(7)


def row_dot(left, right):
    return lax.dot_general(left, right, (((1,), (1,)), ((), ())), preferred_element_type=jnp.float32)


def plain_dot(left, right):
    return lax.dot_general(left, right, (((1,), (0,)), ((), ())), preferred_element_type=jnp.float32)


def over_rows_dot(left, right):
    return lax.dot_general(left, right, (((0,), (0,)), ((), ())), preferred_element_type=jnp.float32)


def store_pairs(refs, even, rows, values):
    if len(refs) == 1:
        for share, value in enumerate(values):
            refs[0][share, rows, :] = value
        return
    kept, sent = refs
    for at in range(len(values) // 2):
        first, second = values[2 * at], values[2 * at + 1]
        kept[at, rows, :] = jnp.where(even, first, second)
        sent[at, rows, :] = jnp.where(even, second, first)


def over_clips(clips, step, state):
    if clips <= 8:
        for clip in range(clips):
            state = step(clip, state)
        return state
    return lax.fori_loop(0, clips, step, state)


def clip_bounds(marks, clips, places):
    def step(clip, state):
        first, end = state
        mark = marks[clip]
        return (
            jnp.maximum(first, jnp.where(mark <= places, mark, 0)),
            jnp.minimum(end, jnp.where(mark > places, mark, marks[clips + TOTAL])),
        )

    return over_clips(clips, step, (jnp.zeros_like(places), jnp.zeros_like(places) + marks[clips + TOTAL]))


def like(shape, dtype=jnp.float32):
    return jax.ShapeDtypeStruct(shape, dtype)


def call(
    kernel, outs, scratch, args, name, flops, grid=None, in_specs=None, out_specs=None, limit=56, aliases=None
):
    size = sum(a.size * a.dtype.itemsize for a in args)
    size += sum(o.size * o.dtype.itemsize for o in outs)
    extra = {} if grid is None else {"grid": grid}
    return pl.pallas_call(
        kernel,
        out_shape=tuple(outs),
        in_specs=in_specs or [SMEM_WHOLE if a.dtype == jnp.int32 else VMEM_WHOLE for a in args],
        out_specs=out_specs or (VMEM_WHOLE,) * len(outs),
        scratch_shapes=scratch,
        compiler_params=pltpu.CompilerParams(vmem_limit_bytes=limit << 20),
        cost_estimate=pl.CostEstimate(flops=flops, bytes_accessed=size, transcendentals=0),
        name=name,
        input_output_aliases=aliases or {},
        **extra,
    )(*args)


Q_TILE = 512
K_TILE = 512
LOW = -1e30
LOG2E = 1.4426950408889634


def unpack_heads(packed_ref, targets):
    blocks, _, block = packed_ref.shape

    def one(at, carry):
        here = pl.ds(pl.multiple_of(at * block, block), block)
        for place, (rows, columns) in enumerate(targets):
            piece = packed_ref[at, place * HEAD_DIM : (place + 1) * HEAD_DIM]
            if rows is not None:
                rows[here, :] = piece.T
            if columns is not None:
                columns[0:HEAD_DIM, here] = piece
        return carry

    lax.fori_loop(0, blocks, one, 0)


def tile_spans(marks, clips, index):
    first = marks[clips + SEGMENT] + index * Q_TILE
    begin = marks[clips + KEYS]
    low, low_end = clip_bounds(marks, clips, first)
    high_start, high = clip_bounds(marks, clips, first + Q_TILE - 1)
    low, low_end, high_start, high = (v - begin for v in (low, low_end, high_start, high))
    up = K_TILE - 1
    start = lax.div(low, K_TILE)
    stop = jnp.where(marks[clips + ACTIVE] > 0, lax.div(high + up, K_TILE), start)
    inner = lax.div(high_start + up, K_TILE)
    outer = lax.div(high, K_TILE)
    whole = (low == high_start) & (inner < outer) & (stop > start)
    inner = jnp.where(whole, inner, stop)
    outer = jnp.where(whole, outer, stop)
    places = first + lax.broadcasted_iota(jnp.int32, (1, Q_TILE), 1)
    starts, ends = clip_bounds(marks, clips, places)
    return (start, inner, outer, stop), starts - begin, ends - begin


def allowed(column, starts, ends):
    places = column + lax.broadcasted_iota(jnp.int32, (K_TILE, 1), 0)
    return (places >= starts) & (places < ends)


def over_spans(spans, step, state):
    for at in range(3):
        state = lax.fori_loop(spans[at], spans[at + 1], functools.partial(step, at != 1), state)
    return state


def attend_kernel(clips, halo, marks, packed_ref, out_ref, wide_ref, log_ref, query_t, keys, value_t):
    rows = wide_ref.shape[1]
    block = packed_ref.shape[2]
    more = value_t.shape[0] - HEAD_DIM
    value_t[HEAD_DIM:] = jnp.where(
        lax.broadcasted_iota(jnp.int32, (more, value_t.shape[1]), 0) == 0, 1.0, 0.0
    ).astype(BF)
    unpack_heads(packed_ref, ((None, query_t), (keys, None), (None, value_t)))
    factor = HEAD_DIM ** (-0.5) * LOG2E

    def query_tile(index, carry):
        first = pl.multiple_of(index * Q_TILE, Q_TILE)
        q = query_t[:, pl.ds(halo * block + first, Q_TILE)]
        spans, starts, ends = tile_spans(marks, clips, index)

        def key_tile(masked, at, state):
            top, total = state
            column = pl.multiple_of(at * K_TILE, K_TILE)
            scores = plain_dot(keys[pl.ds(column, K_TILE), :], q) * factor
            if masked:
                scores = jnp.where(allowed(column, starts, ends), scores, LOW)
            new_top = jnp.maximum(top, jnp.max(scores, axis=0, keepdims=True))
            weight = jnp.exp2(scores - new_top).astype(BF)
            total = total * jnp.exp2(top - new_top) + plain_dot(
                value_t[:, pl.ds(column, K_TILE)], weight
            )
            return new_top, total

        top, total = over_spans(
            spans,
            key_tile,
            (
                jnp.full((1, Q_TILE), 0.5 * LOW, jnp.float32),
                jnp.zeros((HEAD_DIM + more, Q_TILE), jnp.float32),
            ),
        )
        mass = jnp.maximum(total[HEAD_DIM : HEAD_DIM + 1], 1e-37)
        attended = total[:HEAD_DIM] / mass
        wide_ref[:, pl.ds(first, Q_TILE)] = attended
        log_ref[:, pl.ds(first, Q_TILE)] = top + jnp.log2(mass)
        narrow = attended.astype(BF)
        for inner in range(Q_TILE // block):
            out_ref[index * (Q_TILE // block) + inner] = narrow[:, inner * block : (inner + 1) * block]
        return carry

    lax.fori_loop(0, rows // Q_TILE, query_tile, 0)


def attend(marks, packed, clips, halo):
    blocks, _, block = packed.shape
    rows = (blocks - 2 * halo) * block
    key_rows = blocks * block
    return call(
        functools.partial(attend_kernel, clips, halo),
        [
            like((blocks - 2 * halo, HEAD_DIM, block), BF),
            like((HEAD_DIM, rows)),
            like((1, rows)),
        ],
        [
            pltpu.VMEM((HEAD_DIM, key_rows), BF),
            pltpu.VMEM((key_rows, HEAD_DIM), BF),
            pltpu.VMEM((HEAD_DIM + 16, key_rows), BF),
        ],
        (marks, packed),
        "attend",
        25 * 10**9,
    )


def attend_back_kernel(
    clips, halo, marks, packed_ref, grad_ref, wide_ref, log_ref, out_ref,
    query_t, keys, key_t, values, grad_t, key_grads, value_grads,
):
    unpack_heads(packed_ref, ((None, query_t), (keys, key_t), (values, None)))
    unpack_heads(grad_ref, ((None, grad_t),))
    blocks, _, block = packed_ref.shape
    rows = wide_ref.shape[1]
    scale = HEAD_DIM ** (-0.5)
    key_grads[...] = jnp.zeros_like(key_grads)
    value_grads[...] = jnp.zeros_like(value_grads)
    if halo:
        out_ref[...] = jnp.zeros_like(out_ref)

    def query_tile(index, carry):
        first = pl.multiple_of(index * Q_TILE, Q_TILE)
        own = pl.ds(halo * block + first, Q_TILE)
        q_t, g_t = query_t[:, own], grad_t[:, pl.ds(first, Q_TILE)]
        log_total = log_ref[:, pl.ds(first, Q_TILE)]
        delta = jnp.sum(
            g_t.astype(jnp.float32) * wide_ref[:, pl.ds(first, Q_TILE)], axis=0, keepdims=True
        )
        spans, starts, ends = tile_spans(marks, clips, index)

        def key_tile(masked, at, running):
            column = pl.multiple_of(at * K_TILE, K_TILE)
            here = pl.ds(column, K_TILE)
            probs = jnp.exp2(plain_dot(keys[here, :], q_t) * (scale * LOG2E) - log_total)
            if masked:
                probs = jnp.where(allowed(column, starts, ends), probs, 0.0)
            prob_grad = plain_dot(values[here, :], g_t)
            score_grad = (probs * (prob_grad - delta)).astype(BF)
            value_grads[:, here] += row_dot(g_t, probs.astype(BF))
            key_grads[:, here] += row_dot(q_t, score_grad)
            return running + plain_dot(key_t[:, here], score_grad)

        query_grad = over_spans(spans, key_tile, jnp.zeros((HEAD_DIM, Q_TILE), jnp.float32))
        query_grad = (query_grad * scale).astype(BF)
        for inner in range(Q_TILE // block):
            spot = halo + index * (Q_TILE // block) + inner
            out_ref[spot, 0:HEAD_DIM] = query_grad[:, inner * block : (inner + 1) * block]
        return carry

    lax.fori_loop(0, rows // Q_TILE, query_tile, 0)

    def finish(spot, carry):
        here = pl.ds(pl.multiple_of(spot * block, block), block)
        out_ref[spot, HEAD_DIM : 2 * HEAD_DIM] = (key_grads[:, here] * scale).astype(BF)
        out_ref[spot, 2 * HEAD_DIM :] = value_grads[:, here].astype(BF)
        return carry

    lax.fori_loop(0, blocks, finish, 0)


def attend_back(marks, packed, grad, wide, log_total, clips, halo):
    blocks, lanes, block = packed.shape
    rows = wide.shape[1]
    key_rows = blocks * block
    return call(
        functools.partial(attend_back_kernel, clips, halo),
        [like((blocks, lanes, block), BF)],
        [
            pltpu.VMEM((HEAD_DIM, key_rows), BF),
            pltpu.VMEM((key_rows, HEAD_DIM), BF),
            pltpu.VMEM((HEAD_DIM, key_rows), BF),
            pltpu.VMEM((key_rows, HEAD_DIM), BF),
            pltpu.VMEM((HEAD_DIM, rows), BF),
            pltpu.VMEM((HEAD_DIM, key_rows), jnp.float32),
            pltpu.VMEM((HEAD_DIM, key_rows), jnp.float32),
        ],
        (marks, packed, grad, wide, log_total),
        "attend_back",
        35 * 10**9,
        limit=60,
    )[0]


TAPS = 16
SHOT = 384
TURNS = KERNEL // TAPS


def conv_weights_kernel(back, weight_ref, out_ref):
    group_width = out_ref.shape[1]
    if back:
        for group in range(GROUPS):
            lanes = slice(group_width * group, group_width * (group + 1))
            out_ref[group] = jnp.concatenate(
                [weight_ref[group_width * tap : group_width * (tap + 1), lanes] for tap in range(TAPS)],
                axis=1,
            )
    else:
        turned = weight_ref[...].T
        for group in range(GROUPS):
            out_ref[group] = turned[group_width * group : group_width * (group + 1)]


def conv_weights(back, weight, first, turns):
    width = weight.shape[1]
    group_width = width // GROUPS
    return call(
        functools.partial(conv_weights_kernel, back),
        [like((GROUPS, turns * group_width, TAPS * group_width), weight.dtype)],
        [],
        (weight,),
        "conv_weights_back" if back else "conv_weights",
        0,
        (turns,),
        [pl.BlockSpec((TAPS * group_width, width), lambda turn: (turn + first, 0))],
        (pl.BlockSpec((GROUPS, group_width, TAPS * group_width), lambda turn: (0, turn, 0)),),
    )[0]


def conv_kernel(back, clips, parts, marks, before_ref, rows_ref, after_ref, *refs):
    weight_refs, (out_ref, spaced, total) = refs[:parts], refs[parts:]
    group = pl.program_id(0)
    rows, width = rows_ref.shape
    half = KERNEL // 2
    long = rows + 2 * half
    group_width = width // GROUPS
    room = spaced.shape[1]
    places = marks[clips + BEGIN] - half + lax.broadcasted_iota(jnp.int32, (1, long), 1)
    ids = over_clips(
        clips,
        lambda clip, found: found + jnp.where(places >= marks[clip], 1, 0),
        jnp.zeros((1, long), jnp.int32),
    )
    ids = jnp.where((places >= 0) & (places < marks[clips + TOTAL]), ids, -1)

    def number_of(place):
        step = lambda clip, found: found + jnp.where(place >= marks[clip], 1, 0)
        return over_clips(clips, step, jnp.int32(0))

    first = number_of(marks[clips + BEGIN])
    count = number_of(marks[clips + BEGIN] + rows - 1) - first + 1

    @pl.when(group == 0)
    def _():
        turned = jnp.concatenate(
            [before_ref[...], rows_ref[...], after_ref[...]], axis=0
        ).astype(jnp.float32).T
        rest = jnp.zeros((width, room - long), jnp.float32)

        def of_clip(clip):
            return jnp.concatenate([jnp.where(ids == first + clip, turned, 0.0), rest], axis=1)

        spaced[...] = of_clip(0).astype(BF)

        def place(clip, carry):
            spaced[...] += pltpu.roll(of_clip(clip), clip * half, 1).astype(BF)
            return carry

        lax.fori_loop(1, count, place, 0)

    row = pl.multiple_of(group * group_width, group_width)
    shots = lax.div(rows + half * (count - 1) + SHOT - 1, SHOT)

    def shot(index, carry):
        base = pl.multiple_of(index * SHOT, 128)
        tile = spaced[pl.ds(row, group_width), pl.ds(base, SHOT + 2 * KERNEL)]
        moved = []
        for tap in range(TAPS):
            begin = TAPS - tap if back else tap
            moved.append(tile[:, begin : begin + SHOT + KERNEL])
        moved = jnp.concatenate(moved, axis=0)
        result = None
        turn = 0
        for weight_ref in weight_refs:
            product = plain_dot(weight_ref[0], moved)
            for inner in range(product.shape[0] // group_width):
                begin = (TURNS - 1 - turn if back else turn) * TAPS
                piece = product[inner * group_width : (inner + 1) * group_width, begin : begin + SHOT]
                result = piece if result is None else result + piece
                turn += 1
        total[pl.ds(row, group_width), pl.ds(base, SHOT)] = result
        return carry

    lax.fori_loop(0, shots, shot, 0)

    @pl.when(group == GROUPS - 1)
    def _():
        wide = total.shape[1]
        own = ids[:, half : half + rows]

        def collect(clip, carry):
            moved = pltpu.roll(total[...], lax.rem(wide - clip * half, wide), 1)[:, :rows]
            total[:, :rows] = jnp.where(own == first + clip, moved, total[:, :rows])
            return carry

        lax.fori_loop(1, count, collect, 0)
        out_ref[...] = total[:, :rows].T


def conv_rows(back, marks, before, value, after, weights, clips):
    rows, width = value.shape
    shots = -(-(rows + KERNEL // 2 * (clips - 1)) // SHOT)
    whole = lambda a: pl.BlockSpec(a.shape, lambda group: (0, 0))
    return call(
        functools.partial(conv_kernel, back, clips, len(weights)),
        [like((rows, width))],
        [
            pltpu.VMEM((width, SHOT * shots + 2 * KERNEL), BF),
            pltpu.VMEM((width, SHOT * shots), jnp.float32),
        ],
        (marks, before, value, after) + tuple(weights),
        "conv_back" if back else "conv",
        15 * 10**9,
        (GROUPS,),
        [SMEM_WHOLE, whole(before), whole(value), whole(after)]
        + [pl.BlockSpec((1,) + weight.shape[1:], lambda group: (group, 0, 0)) for weight in weights],
        (pl.BlockSpec((rows, width), lambda group: (0, 0)),),
        limit=48,
    )[0]


def taps_grad_kernel(
    clips, marks, both_ref, *refs
):
    half = KERNEL // 2
    out_refs, (inputs, spaced, input_cols, grad_cols) = refs[:-4], refs[-4:]
    group_width = inputs.shape[0]
    long = inputs.shape[1]
    blocks, _, block = both_ref.shape
    halo = (blocks - RING) // 2
    halo_rows = halo * block
    first = over_clips(
        clips,
        lambda clip, found: found + jnp.where(marks[clips + SEGMENT] >= marks[clip], 1, 0),
        jnp.int32(0),
    )
    origin = half + halo_rows
    span = input_cols.shape[1]

    def lay(first_row, begin_block, number, target, reach):
        for at in range(number):
            target[:, at * block : (at + 1) * block] = both_ref[
                begin_block + at, first_row : first_row + group_width
            ].astype(jnp.float32)
        target[:, number * block :] = jnp.zeros((group_width, long - number * block), jnp.float32)
        lanes = lax.broadcasted_iota(jnp.int32, (1, long), 1)
        places = marks[clips + SEGMENT] - reach + lanes
        held = lanes < number * block
        spaced[...] = jnp.zeros_like(spaced)

        def place(clip, carry):
            begin = jnp.where(clip > 0, marks[jnp.maximum(clip - 1, 0)], 0)
            keep = (places >= begin) & (places < marks[clip]) & held
            spaced[...] += pltpu.roll(
                jnp.where(keep, target[...], 0.0), origin - reach + half * (clip - first), 1
            )
            return carry

        lax.fori_loop(first, clips, place, 0)
        return spaced[...]

    laid = lay(0, 0, blocks, inputs, halo_rows)
    for turn in range(TURNS):
        begin = origin - half + turn * TAPS
        input_cols[turn * group_width : (turn + 1) * group_width, :] = laid[
            :, begin : begin + span
        ].astype(BF)
    laid = lay(group_width, halo, RING, inputs, 0)
    for tap in range(TAPS):
        grad_cols[tap * group_width : (tap + 1) * group_width, :] = laid[
            :, origin - tap : origin - tap + span
        ].astype(BF)
    result = row_dot(input_cols[...], grad_cols[...]).astype(BF)
    side_lanes = TAPS * group_width // 2
    even_core = marks[clips + CORE] == 0
    for piece in range(side_lanes // 128):
        values = []
        for place_at in range(2 * TURNS):
            turn, begin = place_at // 2, place_at % 2 * side_lanes + piece * 128
            values.append(result[turn * group_width : (turn + 1) * group_width, begin : begin + 128])
        store_pairs(out_refs, even_core, slice(piece * group_width, (piece + 1) * group_width), values)


def taps_grad(marks, both, shape, clips, width):
    blocks, _, block = both.shape
    group_width = width // GROUPS
    half = KERNEL // 2
    halo_rows = (blocks - RING) // 2 * block
    span = -(-(RING * block + half * clips) // 128) * 128
    long = span + 2 * halo_rows + half + 2 * KERNEL
    long = -(-long // 128) * 128
    more = TAPS * group_width // 2 // 128 * group_width
    return call(
        functools.partial(taps_grad_kernel, clips),
        [like((n, more, 128), BF) for n in shape],
        [
            pltpu.VMEM((group_width, long), jnp.float32),
            pltpu.VMEM((group_width, long), jnp.float32),
            pltpu.VMEM((TURNS * group_width, span), BF),
            pltpu.VMEM((TAPS * group_width, span), BF),
        ],
        (marks, both),
        "taps_grad",
        10**10,
        limit=60,
    )


def weave_taps_kernel(own_ref, out_ref):
    group_width = out_ref.shape[1] // GROUPS
    taps = out_ref.shape[0] // group_width
    pieces = own_ref.shape[1] // group_width
    both = []
    for group in range(GROUPS):
        rows = own_ref[group].astype(jnp.float32)
        both.append(
            jnp.concatenate([rows[at * group_width : (at + 1) * group_width] for at in range(pieces)], axis=1)
        )
    for tap in range(taps):
        lanes = slice(tap * group_width, (tap + 1) * group_width)
        out_ref[tap * group_width : (tap + 1) * group_width, :] = jnp.concatenate(
            [value[:, lanes] for value in both], axis=1
        )


def weave_taps(own, taps, group_width):
    return call(
        weave_taps_kernel, [like((taps * group_width, GROUPS * group_width))], [], (own,), "weave_taps", 0
    )[0]


def add_shares_kernel(own_ref, other_ref, out_ref):
    out_ref[...] = (own_ref[...].astype(jnp.float32) + other_ref[...].astype(jnp.float32)).astype(BF)


def add_shares(own, other):
    block = pl.BlockSpec((2,) + other.shape[1:], lambda at: (at, 0, 0))
    return call(
        add_shares_kernel,
        [like(other.shape, BF)],
        [],
        (own, other),
        "add_shares",
        0,
        (other.shape[0] // 2,),
        [block] * 2,
        (block,),
    )[0]


def split_shares_kernel(clips, marks, own_ref, other_ref, kept_ref, sent_ref):
    total = (own_ref[...].astype(jnp.float32) + other_ref[...].astype(jnp.float32)).astype(BF)
    rows = kept_ref.shape[1]
    lower = marks[clips + REP] == 0
    kept_ref[...] = jnp.where(lower, total[:, :rows], total[:, rows:])
    sent_ref[...] = jnp.where(lower, total[:, rows:], total[:, :rows])


def split_shares(marks, own, other, clips):
    shares, rows, lanes = own.shape
    return call(
        functools.partial(split_shares_kernel, clips),
        [like((shares, rows // 2, lanes), BF)] * 2,
        [],
        (marks, own, other),
        "split_shares",
        0,
    )


def join_stem_kernel(clips, marks, own_ref, other_ref, heads_ref, other_heads_ref, out_ref):
    below, rows = own_ref.shape[1], heads_ref.shape[1]
    out_ref[:, :below] = (own_ref[...].astype(jnp.float32) + other_ref[...].astype(jnp.float32)).astype(BF)
    first = marks[clips + CORE] == 0
    out_ref[:, below : below + rows] = jnp.where(first, heads_ref[...], other_heads_ref[...])
    out_ref[:, below + rows :] = jnp.where(first, other_heads_ref[...], heads_ref[...])


def join_stem(marks, own, other, heads, other_heads, clips):
    chips, below, lanes = own.shape
    return call(
        functools.partial(join_stem_kernel, clips),
        [like((chips, below + 2 * heads.shape[1], lanes), BF)],
        [],
        (marks, own, other, heads, other_heads),
        "join_stem",
        0,
    )[0]


def add_below_kernel(own_ref, other_ref, _, out_ref):
    add_shares_kernel(own_ref, other_ref, out_ref)


def add_below(own, other, straight):
    block = pl.BlockSpec((2,) + own.shape[1:], lambda at: (at, 0, 0))
    return call(
        add_below_kernel,
        [like(straight.shape, BF)],
        [],
        (own, other, straight),
        "add_below",
        0,
        (own.shape[0] // 2,),
        [block, block, pl.BlockSpec(memory_space=pl.ANY)],
        (pl.BlockSpec((2,) + own.shape[1:], lambda at: (at, 1, 0)),),
        aliases={2: 0},
    )[0]


def join_pair_kernel(clips, marks, taps_ref, other_ref, out_ref):
    rows = taps_ref.shape[1]
    first = marks[clips + CORE] == 0
    out_ref[:, :rows] = jnp.where(first, taps_ref[...], other_ref[...])
    out_ref[:, rows:] = jnp.where(first, other_ref[...], taps_ref[...])


def join_pair(marks, taps, other, clips):
    chips, rows, lanes = taps.shape
    return call(
        functools.partial(join_pair_kernel, clips),
        [like((chips, 2 * rows, lanes), BF)],
        [],
        (marks, taps, other),
        "join_pair",
        0,
    )[0]


SHARE = 384
PIECE = 128


def norm_parts(values):
    center = values - jnp.mean(values, axis=-1, keepdims=True)
    inverse = lax.rsqrt(jnp.mean(center * center, axis=-1, keepdims=True) + EPS)
    return center * inverse, inverse


def norm_back(unit, inverse, scales, grad):
    scaled = grad * scales
    back = inverse * (
        scaled
        - jnp.mean(scaled, axis=-1, keepdims=True)
        - unit * jnp.mean(scaled * unit, axis=-1, keepdims=True)
    )
    return back, row_sum(grad * unit), row_sum(grad)


def row_sum(values):
    return jnp.sum(values, axis=0, keepdims=True)


def gelu_both(values):
    below = 0.5 + 0.5 * lax.erf(values * 0.7071067811865476)
    bell = jnp.exp(-0.5 * values * values) * 0.3989422804014327
    return values * below, below + values * bell


def store_turned(values_b, out_ref, first):
    group_width = values_b.shape[1] // GROUPS
    turned = values_b.T
    for group in range(GROUPS):
        out_ref[group, first : first + group_width] = turned[group * group_width : (group + 1) * group_width]


def same_clip_next(marks, clips, rows):
    following = marks[clips + BEGIN] + 1 + lax.broadcasted_iota(jnp.int32, (rows, 1), 0)
    step = lambda clip, other: jnp.maximum(other, jnp.where(following == marks[clip], 1, 0))
    return over_clips(clips, step, jnp.zeros((rows, 1), jnp.int32)) == 0


def stem_kernel(
    clips, marks, samples_ref, next_ref, weight_ref, gain_ref, bias_ref, proj_ref, gains_ref, biases_ref,
    start_ref, start_b_ref, top_ref, bottom_ref, pre_ref, normed_ref, unfold_ref, table_ref, wide,
):
    rows, chans = pre_ref.shape
    table_ref[0:3] = gains_ref[...]
    table_ref[3:12] = biases_ref[...]
    last = lax.broadcasted_iota(jnp.int32, (rows, 1), 0) == rows - 1
    same = same_clip_next(marks, clips, rows)
    for lane in range(0, chans, PIECE):
        lanes = slice(lane, lane + PIECE)
        wide[...] = samples_ref[:, lanes].astype(jnp.float32)
        even = wide[pl.ds(0, rows, stride=2), :]
        unfold_ref[:, lanes] = even.astype(BF)
        unfold_ref[:, chans + lane : chans + lane + PIECE] = wide[pl.ds(1, rows, stride=2), :].astype(BF)
        moved = jnp.where(last, next_ref[:, lanes].astype(jnp.float32), pltpu.roll(even, rows - 1, 0))
        unfold_ref[:, 2 * chans + lane : 2 * chans + lane + PIECE] = jnp.where(same, moved, 0.0).astype(BF)
    pre = plain_dot(unfold_ref[...], weight_ref[...])
    pre_ref[...] = pre
    unit, _ = norm_parts(gelu_both(pre)[0])
    normed = (unit * gain_ref[...] + bias_ref[...]).astype(BF)
    normed_ref[...] = normed
    start = plain_dot(normed, proj_ref[...]) + table_ref[3:4]
    start_ref[...] = start
    start_b = start.astype(BF)
    start_b_ref[...] = start_b
    edge = top_ref.shape[0]
    top_ref[...] = start_b[:edge]
    bottom_ref[...] = start_b[rows - edge :]


def stem(marks, samples, next_row, weight, gain, bias, proj, gains, biases, clips):
    rows = samples.shape[0] // 2
    chans, width = proj.shape
    return call(
        functools.partial(stem_kernel, clips),
        [
            like((rows, width)), like((rows, width), BF),
            like((KERNEL // 2, width), BF), like((KERNEL // 2, width), BF),
            like((rows, chans)), like((rows, chans), BF), like((rows, 3 * chans), BF), like((12, width)),
        ],
        [pltpu.VMEM((2 * rows, PIECE), jnp.float32)],
        (marks, samples, next_row, weight, gain, bias, proj, gains, biases),
        "stem",
        6 * 10**9,
    )


def project_kernel(conv_ref, start_ref, table_ref, weight_ref, hidden_ref, hidden_b_ref, packed_ref):
    rows, width = start_ref.shape
    mixed = start_ref[...] + gelu_both(conv_ref[...] + table_ref[4:5])[0]
    unit, _ = norm_parts(mixed)
    hidden = unit * table_ref[0:1] + table_ref[5:6]
    hidden_ref[...] = hidden
    hidden_b = hidden.astype(BF)
    hidden_b_ref[...] = hidden_b
    shifts = (table_ref[6:7], jnp.zeros((1, width), jnp.float32), table_ref[7:8])
    heads = width // HEAD_DIM
    for at, shift in enumerate(shifts):
        part = plain_dot(hidden_b, weight_ref[:, at * width : (at + 1) * width]) + shift
        turned = part.astype(BF).T
        for head in range(heads):
            packed_ref[head, at * HEAD_DIM : (at + 1) * HEAD_DIM] = turned[
                head * HEAD_DIM : (head + 1) * HEAD_DIM
            ]
    for head in range(heads, RING):
        packed_ref[head] = jnp.zeros_like(packed_ref[head])


def project_heads(conv_sum, start, table, weight):
    rows, width = start.shape
    return call(
        project_kernel,
        [like((rows, width)), like((rows, width), BF), like((RING, 3 * HEAD_DIM, rows), BF)],
        [],
        (conv_sum, start, table, weight),
        "project_heads",
        6 * 10**9,
    )


def middle_kernel(
    clips, marks, heads_ref, hidden_ref, table_ref, out_weight_ref, in_ref, in_bias_ref, back_ref, out_grad_ref,
    layer_ref, grad_heads_ref, grad_second_ref, sums_ref, in_bias_grad_ref, kept_ref, sent_ref, straight_ref,
    attended, before, second, second_b, second_t, inner_b, slope, total, grad_last, grad_last_b,
    joined, sems,
):
    step = pl.program_id(0)
    rows, width = hidden_ref.shape
    chunk = in_ref.shape[1]
    chunks = pl.num_programs(0) // 2
    heads = width // HEAD_DIM
    shares = kept_ref.shape[0]
    lower = marks[clips + REP] == 0
    in_rows = width // shares
    back_rows = chunk * chunks // shares
    owners = chunk // back_rows

    first_blocks = 3 * chunks // 4

    def moves(half, place, sem, act):
        for keeps, target in ((lower, (kept_ref, sent_ref)[half]), (~lower, (sent_ref, kept_ref)[half])):

            @pl.when(keeps)
            def _():
                act(pltpu.make_async_copy(joined.at[half].at[place], target.at[place], sem))

    def in_moves(at, act):
        @pl.when(at < first_blocks)
        def _():
            place = (slice(None), pl.ds(pl.multiple_of(at * in_rows, 16), in_rows))
            moves(0, place, sems.at[0, at], act)

        @pl.when(at >= first_blocks)
        def _():
            place = (slice(None), pl.ds(pl.multiple_of((at - first_blocks) * in_rows, 16), in_rows))
            act(pltpu.make_async_copy(joined.at[2].at[place], straight_ref.at[place], sems.at[0, at]))

    def back_moves(at, act):
        mine = pl.ds(at * owners, owners)
        moves(1, (mine, pl.ds(0, back_rows)), sems.at[1, at], act)
        place = (mine, pl.ds((chunks - first_blocks) * in_rows, back_rows))
        act(pltpu.make_async_copy(joined.at[2].at[place], straight_ref.at[place], sems.at[2, at]))

    def out_moves(act):
        moves(1, (slice(None), pl.ds(back_rows, 2 * in_rows)), sems.at[3, 0], act)

    def go(copy):
        copy.start()

    def wait(copy):
        copy.wait()

    @pl.when(step == 0)
    def _():
        for head in range(heads):
            attended[head * HEAD_DIM : (head + 1) * HEAD_DIM] = heads_ref[head]
        value = hidden_ref[...] + over_rows_dot(attended[...], out_weight_ref[...]) + table_ref[8:9]
        before[...] = value
        unit, _ = norm_parts(value)
        value = unit * table_ref[1:2] + table_ref[9:10]
        second[...] = value
        second_b[...] = value.astype(BF)
        second_t[...] = value.T.astype(BF)
        total[...] = jnp.zeros_like(total)

    @pl.when(step < chunks)
    def _():
        at = pl.multiple_of(step * chunk, chunk)
        value, back = gelu_both(plain_dot(second_b[...], in_ref[...]) + in_bias_ref[:, pl.ds(at, chunk)])
        value_b = value.astype(BF)
        inner_b[step] = value_b
        slope[step] = back
        total[...] += plain_dot(value_b, back_ref[...])

    @pl.when(step == chunks - 1)
    def _():
        unit, inverse = norm_parts(second[...] + total[...] + table_ref[10:11])
        layer_ref[...] = (unit * table_ref[2:3] + table_ref[11:12]).astype(BF)
        back, gain, bias = norm_back(unit, inverse, table_ref[2:3], out_grad_ref[...].astype(jnp.float32))
        grad_last[...] = back
        grad_last_b[...] = back.astype(BF)
        total[...] = back
        sums_ref[0:1] = gain
        sums_ref[1:2] = bias
        sums_ref[2:3] = row_sum(back)

    @pl.when(step >= chunks)
    def _():
        turn = step - chunks
        at = pl.multiple_of(turn * chunk, chunk)
        grad = row_dot(grad_last_b[...], back_ref[...]) * slope[turn]
        in_bias_grad_ref[:, pl.ds(at, chunk)] = row_sum(grad)
        grad_b = grad.astype(BF)
        total[...] += row_dot(grad_b, in_ref[...])
        product = plain_dot(second_t[...], grad_b).astype(BF)
        straight = turn >= first_blocks
        row = pl.multiple_of(jnp.where(straight, turn - first_blocks, turn) * in_rows, 16)
        for share in range(shares):
            joined[jnp.where(straight, 2, 0), share, pl.ds(row, in_rows), :] = product[
                share * in_rows : (share + 1) * in_rows
            ]
        in_moves(turn, go)
        product = over_rows_dot(inner_b[turn], grad_last_b[...]).astype(BF)
        for owner in range(owners):
            for place in range(width // SHARE):
                begin = (chunks - first_blocks) * in_rows if place else 0
                joined[1 + place, turn * owners + owner, begin : begin + back_rows, :] = product[
                    owner * back_rows : (owner + 1) * back_rows, place * SHARE : (place + 1) * SHARE
                ]
        back_moves(turn, go)

    @pl.when(step == 2 * chunks - 1)
    def _():
        unit, inverse = norm_parts(before[...])
        back, gain, bias = norm_back(unit, inverse, table_ref[1:2], total[...])
        grad_second_ref[...] = back
        sums_ref[3:4] = row_sum(back)
        sums_ref[4:5] = gain
        sums_ref[5:6] = bias
        sums_ref[6:8] = jnp.zeros((2, width), jnp.float32)
        back_b = back.astype(BF)
        grads = row_dot(out_weight_ref[...], back_b).astype(BF)
        for head in range(heads):
            grad_heads_ref[head] = grads[head * HEAD_DIM : (head + 1) * HEAD_DIM]
        for head in range(heads, RING):
            grad_heads_ref[head] = jnp.zeros_like(grad_heads_ref[head])
        product = plain_dot(attended[...], back_b).astype(BF)
        for share in range(shares):
            for place in range(width // SHARE):
                begin = back_rows + place * in_rows
                joined[1, share, begin : begin + in_rows, :] = product[
                    share * in_rows : (share + 1) * in_rows, place * SHARE : (place + 1) * SHARE
                ]
        out_moves(go)

        def finish(at, carry):
            in_moves(at, wait)
            back_moves(at, wait)
            return carry

        lax.fori_loop(0, chunks, finish, 0)
        out_moves(wait)


def middle(marks, clips, heads, hidden, table, out_weight, ffn_in, in_bias, ffn_out, out_grad, count):
    rows, width = hidden.shape
    inner = ffn_in.shape[1]
    chunk = SHARE
    chunks = inner // chunk
    own = lambda shape: pl.BlockSpec(shape, lambda step: (0,) * len(shape))
    third = (2 * inner + width) * (width // count) // SHARE // 3
    outs = [
        like((rows, width), BF),
        like((RING, HEAD_DIM, rows), BF),
        like((rows, width)),
        like((8, width)),
        like((1, inner)),
        like((count, third, SHARE), BF),
        like((count, third, SHARE), BF),
        like((count, 2 * third, SHARE), BF),
    ]
    args = (marks, heads, hidden, table, out_weight, ffn_in, in_bias, ffn_out, out_grad)
    in_specs = [SMEM_WHOLE] + [own(a.shape) for a in args[1:]]
    in_specs[5] = pl.BlockSpec((width, chunk), lambda step: (0, step % chunks))
    in_specs[7] = pl.BlockSpec((chunk, width), lambda step: (step % chunks, 0))
    out_specs = [own(o.shape) for o in outs]
    out_specs[5] = out_specs[6] = out_specs[7] = pl.BlockSpec(memory_space=pl.ANY)
    scratch = [
        pltpu.VMEM((width, rows), BF),
        pltpu.VMEM((rows, width), jnp.float32),
        pltpu.VMEM((rows, width), jnp.float32),
        pltpu.VMEM((rows, width), BF),
        pltpu.VMEM((width, rows), BF),
        pltpu.VMEM((chunks, rows, chunk), BF),
        pltpu.VMEM((chunks, rows, chunk), jnp.float32),
        pltpu.VMEM((rows, width), jnp.float32),
        pltpu.VMEM((rows, width), jnp.float32),
        pltpu.VMEM((rows, width), BF),
        pltpu.VMEM((3,) + outs[5].shape, BF),
        pltpu.SemaphoreType.DMA((4, chunks)),
    ]
    return call(
        functools.partial(middle_kernel, clips), outs, scratch, args, "middle", 2 * 10**10, (2 * chunks,), in_specs, tuple(out_specs)
    )


def after_heads_kernel(
    whole, packed_ref, grad_second_ref, hidden_ref, conv_ref, start_ref, table_ref, weight_ref, *refs
):
    rows, width = hidden_ref.shape
    heads = width // HEAD_DIM
    if whole:
        mixed_ref, conv_b_ref, top_ref, bottom_ref, groups_ref, sums_ref, grads = refs
    else:
        mixed_ref, conv_b_ref, top_ref, bottom_ref, groups_ref, sums_ref, joined_ref, grads, hidden_t = refs
    for head in range(heads):
        for part in range(3):
            row = part * width + head * HEAD_DIM
            grads[row : row + HEAD_DIM] = packed_ref[head, part * HEAD_DIM : (part + 1) * HEAD_DIM]
    if not whole:
        shares = joined_ref.shape[0]
        own_rows = width // shares
        hidden_t[...] = hidden_ref[...].T.astype(BF)

        def weight_block(place, carry):
            row = pl.multiple_of(place * SHARE, SHARE)
            product = row_dot(hidden_t[...], grads[pl.ds(row, SHARE), :]).astype(BF)
            for share in range(shares):
                joined_ref[share, pl.ds(pl.multiple_of(place * own_rows, 16), own_rows), :] = product[
                    share * own_rows : (share + 1) * own_rows
                ]
            return carry

        lax.fori_loop(0, 3 * width // SHARE, weight_block, 0)
    back = grad_second_ref[...] + plain_dot(weight_ref[...], grads[...]).T
    value, slope = gelu_both(conv_ref[...] + table_ref[4:5])
    unit, inverse = norm_parts(start_ref[...] + value)
    mixed, gain, bias = norm_back(unit, inverse, table_ref[0:1], back)
    mixed_ref[...] = mixed
    conv = mixed * slope
    conv_b = conv.astype(BF)
    conv_b_ref[...] = conv_b
    edge = top_ref.shape[0]
    top_ref[...] = conv_b[:edge]
    bottom_ref[...] = conv_b[rows - edge :]
    store_turned(start_ref[...].astype(BF), groups_ref, 0)
    store_turned(conv_b, groups_ref, width // GROUPS)
    sums_ref[0:1] = gain
    sums_ref[1:2] = bias
    sums_ref[2:3] = row_sum(conv)
    ones = jnp.ones((8, rows), BF)
    sums_ref[3:4] = row_dot(ones, grads[:width])[0:1]
    sums_ref[4:5] = row_dot(ones, grads[2 * width :])[0:1]
    sums_ref[5:8] = jnp.zeros((3, width), jnp.float32)


def after_heads(packed, grad_second, hidden, conv_sum, start, table, weight, whole):
    rows, width = hidden.shape
    outs = [
        like((rows, width)),
        like((rows, width), BF),
        like((KERNEL // 2, width), BF),
        like((KERNEL // 2, width), BF),
        like((GROUPS, 2 * width // GROUPS, rows), BF),
        like((8, width)),
    ]
    scratch = [pltpu.VMEM((3 * width, rows), BF)]
    args = (packed, grad_second, hidden, conv_sum, start, table, weight)
    if not whole:
        outs.append(like((RING, width // RING * 3 * width // SHARE, SHARE), BF))
        scratch.append(pltpu.VMEM((width, rows), BF))
    return call(
        functools.partial(after_heads_kernel, whole), outs, scratch, args, "after_heads", 5 * 10**9
    )


def head_grads_kernel(clips, marks, packed_ref, hidden_ref, other_ref, kept_ref, sent_ref, turned):
    blocks, lines, block = packed_ref.shape
    core = marks[clips + CORE]
    width = hidden_ref.shape[2]

    def one(at, total):
        total = total + plain_dot(packed_ref[2 * at + core], hidden_ref[at])
        return total + plain_dot(packed_ref[2 * at + 1 - core], other_ref[at])

    total = lax.fori_loop(0, blocks // 2, one, jnp.zeros((lines, width), jnp.float32))
    turned[...] = jnp.concatenate([total, jnp.zeros((block - lines, width), jnp.float32)], axis=0).T.astype(BF)
    own = width // RING
    for piece in range(block // PIECE):
        store_pairs(
            (kept_ref, sent_ref),
            core == 0,
            slice(piece * own, (piece + 1) * own),
            [
                turned[share * own : (share + 1) * own, piece * PIECE : (piece + 1) * PIECE]
                for share in range(RING)
            ],
        )


def head_grads(marks, packed, hidden, other, clips):
    block = packed.shape[2]
    width = hidden.shape[2]
    return call(
        functools.partial(head_grads_kernel, clips),
        [like((RING // 2, block // PIECE * width // RING, PIECE), BF)] * 2,
        [pltpu.VMEM((width, block), BF)],
        (marks, packed, hidden, other),
        "head_grads",
        3 * 10**9,
    )


def weave_heads_kernel(own_ref, other_ref, out_ref):
    heads = own_ref.shape[0]
    rows = out_ref.shape[0]
    for part in range(3):
        piece, begin = divmod(part * HEAD_DIM, PIECE)
        place = (slice(piece * rows, (piece + 1) * rows), slice(begin, begin + HEAD_DIM))
        out_ref[:, part * heads * HEAD_DIM : (part + 1) * heads * HEAD_DIM] = jnp.concatenate(
            [
                own_ref[head][place].astype(jnp.float32) + other_ref[head][place].astype(jnp.float32)
                for head in range(heads)
            ],
            axis=1,
        )


def weave_heads(own, other):
    heads, rows = own.shape[0], own.shape[1] // 2
    return call(
        weave_heads_kernel, [like((rows, 3 * heads * HEAD_DIM))], [], (own, other), "weave_heads", 0
    )[0]


def stem_back_kernel(
    clips, marks, input_ref, mixed_ref, normed_ref, pre_ref, unfold_ref, weight_ref, gain_ref, proj_ref,
    middle_sums_ref, inner_sums_ref, after_sums_ref,
    samples_ref, carried_ref, *refs,
):
    rows, chans = pre_ref.shape
    width = input_ref.shape[1]
    joined_refs, (table, spread, woven) = refs[:-3], refs[-3:]
    shares = RING
    even_core = marks[clips + CORE] == 0
    start = mixed_ref[...] + input_ref[...]
    start_b = start.astype(BF)

    def share_out(product, begin):
        own, columns = product.shape[0] // shares, product.shape[1]
        for place in range(columns // PIECE):
            at = begin + place * own
            store_pairs(
                joined_refs,
                even_core,
                slice(at, at + own),
                [
                    product[share * own : (share + 1) * own, place * PIECE : (place + 1) * PIECE]
                    for share in range(shares)
                ],
            )
        return begin + own * columns // PIECE

    at = share_out(over_rows_dot(normed_ref[...], start_b).astype(BF), 0)
    value, slope = gelu_both(pre_ref[...])
    unit, inverse = norm_parts(value)
    feature, gain_sum, bias_sum = norm_back(
        unit, inverse, gain_ref[...], row_dot(start_b, proj_ref[...])
    )
    pre_b = (feature * slope).astype(BF)
    taps_t = over_rows_dot(unfold_ref[...], pre_b).astype(BF)
    at = share_out(taps_t, at)
    first = row_dot(pre_b, weight_ref[:chans])
    same = same_clip_next(marks, clips, rows)
    follow = jnp.where(same, row_dot(pre_b, weight_ref[2 * chans :]), 0.0)
    carried_ref[...] = follow[rows - 1 :]
    moved = pltpu.roll(follow, 1, 0)
    top = lax.broadcasted_iota(jnp.int32, (rows, 1), 0) == 0
    even = first + jnp.where(top, 0.0, moved)
    odd = row_dot(pre_b, weight_ref[chans : 2 * chans])
    for lane in range(0, chans, PIECE):
        woven[pl.ds(0, rows, stride=2), :] = even[:, lane : lane + PIECE]
        woven[pl.ds(1, rows, stride=2), :] = odd[:, lane : lane + PIECE]
        samples_ref[:, lane : lane + PIECE] = woven[...]
    table[0:1] = after_sums_ref[0:1]
    table[1:2] = middle_sums_ref[4:5]
    table[2:3] = middle_sums_ref[0:1]
    table[3:4] = row_sum(start)
    table[4:5] = after_sums_ref[2:3]
    table[5:6] = after_sums_ref[1:2]
    table[6:7] = after_sums_ref[3:4]
    table[7:8] = after_sums_ref[4:5]
    table[8:9] = middle_sums_ref[3:4]
    table[9:10] = middle_sums_ref[5:6]
    table[10:11] = middle_sums_ref[2:3]
    table[11:12] = middle_sums_ref[1:2]
    spread[...] = jnp.zeros_like(spread)
    own, own_chans = width // shares, chans // shares
    own_inner = inner_sums_ref.shape[1] // shares
    for share in range(shares):
        spread[share, 0:12, 0:own] = table[:, share * own : (share + 1) * own]
        for place in range(-(-own_inner // PIECE)):
            length = min(PIECE, own_inner - place * PIECE)
            begin = share * own_inner + place * PIECE
            spread[share, 12 + place : 13 + place, 0:length] = inner_sums_ref[:, begin : begin + length]
        lanes = slice(share * own_chans, (share + 1) * own_chans)
        spread[share, 14:15, 0:own_chans] = gain_sum[:, lanes]
        spread[share, 15:16, 0:own_chans] = bias_sum[:, lanes]
    store_pairs(
        joined_refs, even_core, slice(at, at + 32), [spread[share].astype(BF) for share in range(shares)]
    )


def stem_back(marks, input_grad, mixed, normed, pre, unfold, weight, gain, proj, sums, shares, clips):
    rows, chans = pre.shape
    width = input_grad.shape[1]
    pieces = (chans // RING * width + 3 * chans // RING * chans) // PIECE + 32
    return call(
        functools.partial(stem_back_kernel, clips),
        [like((2 * rows, chans)), like((1, chans))] + [like((n, pieces, PIECE), BF) for n in shares],
        [pltpu.VMEM((12, width), jnp.float32), pltpu.VMEM((RING, 32, PIECE), jnp.float32),
         pltpu.VMEM((2 * rows, PIECE), jnp.float32)],
        (marks, input_grad, mixed, normed, pre, unfold, weight, gain, proj) + sums,
        "stem_back",
        6 * 10**9,
    )


def from_behind(value, axis, steps):
    count = lax.axis_size(axis)
    initial, last = (max(0, -steps), min(count, count - steps))
    return lax.ppermute(value, axis, [(source, source + steps) for source in range(initial, last)])


def edges(top, bottom):
    return from_behind(bottom, "seq", 1), from_behind(top, "seq", -1)


def near_groups():
    size = lax.axis_size("seq")
    return [[base + i for i in range(RING)] for base in range(0, size, RING)]


def swap(value):
    groups = None if lax.axis_size("seq") == RING else near_groups()
    return lax.all_to_all(value, "seq", 0, 0, axis_index_groups=groups)


def with_far_blocks(value, count):
    if lax.axis_size("seq") == RING or count == 0:
        return value
    before = from_behind(value[value.shape[0] - count :], "seq", RING)
    after = from_behind(value[:count], "seq", -RING)
    return jnp.concatenate([before, value, after], axis=0)


def fold_far_blocks(value, count):
    if lax.axis_size("seq") == RING or count == 0:
        return value
    own = value[count : value.shape[0] - count]
    to_before = from_behind(value[:count], "seq", -RING)
    to_after = from_behind(value[value.shape[0] - count :], "seq", RING)
    wide = own.astype(jnp.float32)
    wide = wide.at[wide.shape[0] - count :].add(to_before.astype(jnp.float32))
    wide = wide.at[:count].add(to_after.astype(jnp.float32))
    return wide.astype(value.dtype)


def other_stream(share):
    return lax.ppermute(share, "rep", [(0, 1), (1, 0)])


def sum_pair(share):
    return share.astype(jnp.float32) + other_stream(share).astype(jnp.float32)


def spread_out(total, sizes, lanes):
    out, at = [], 0
    for rows, columns in sizes:
        parts = []
        for _ in range(columns // lanes):
            parts.append(total[at : at + rows])
            at += rows
        out.append(jnp.concatenate(parts, axis=1))
    return out


def regroup(joined, blocks):
    count = lax.axis_size("seq")
    if count == RING:
        return joined
    parts = count // RING
    lanes = joined.shape[2]
    out, at = [], 0
    for number, rows in blocks:
        piece = joined[:, at : at + number * rows]
        at += number * rows
        piece = piece.reshape(RING, number, parts, rows // parts, lanes).transpose(0, 2, 1, 3, 4)
        out.append(piece.reshape(count, number * rows // parts, lanes))
    return jnp.concatenate(out, axis=1)


def regroup_small(small, widths):
    count = lax.axis_size("seq")
    if count == RING:
        return small
    parts = count // RING
    own, own_inner, own_chans = widths
    lanes = small.shape[2]
    table = small[:, :12, : own * parts].reshape(RING, 12, parts, own).transpose(0, 2, 1, 3)
    table = jnp.pad(table.reshape(count, 12, own), ((0, 0), (0, 0), (0, lanes - own)))
    wide = small[:, 12:14].reshape(RING, 2 * lanes)[:, : own_inner * parts].reshape(count, own_inner)
    wide = jnp.pad(wide, ((0, 0), (0, 2 * lanes - own_inner))).reshape(count, 2, lanes)
    stems = small[:, 14:16, : own_chans * parts].reshape(RING, 2, parts, own_chans).transpose(0, 2, 1, 3)
    stems = jnp.pad(stems.reshape(count, 2, own_chans), ((0, 0), (0, 0), (0, lanes - own_chans)))
    return jnp.concatenate([table, wide, stems], axis=1)


def over_seq(joined):
    return lax.psum_scatter(joined, "seq", scatter_dimension=0, tiled=False).astype(jnp.bfloat16)


def local(
    samples,
    clip_lengths,
    stem_weight,
    stem_gain,
    stem_bias,
    proj_weight,
    pos_weight,
    norm_gains,
    biases,
    attn_in,
    attn_out,
    ffn_in,
    ffn_in_bias,
    ffn_out,
    out_grad,
):
    rows_dev = out_grad.shape[1]
    width = attn_out.shape[0]
    chans = stem_weight.shape[1]
    inner = ffn_in.shape[1]
    group_width = width // GROUPS
    count = lax.axis_size("seq")
    place = lax.axis_index("seq")
    total = rows_dev * count
    begin = place * rows_dev
    clips = clip_lengths.shape[1]
    upto = jnp.arange(clips)[:, None] >= jnp.arange(clips)[None]
    ends = jnp.sum(jnp.where(upto, clip_lengths, 0), axis=1)
    far = 0 if count == RING else -(-MAXLEN // rows_dev)
    segment_begin = (place // RING) * RING * rows_dev
    active = jnp.where(place % RING < HEADS, 1, 0)
    marks = jnp.concatenate(
        [ends, jnp.stack([jnp.int32(total), begin, segment_begin, segment_begin - far * rows_dev, active, place % 2, lax.axis_index("rep") if count == RING else 0])]
    ).astype(jnp.int32)
    next_row = from_behind(samples[0, :1], "seq", -1)
    one_weights = conv_weights(False, pos_weight, 0, TURNS // 2)
    next_row, one_weights = lax.optimization_barrier((next_row, one_weights))
    start_x, start_b, top, bottom, stem_pre, normed_b, unfold, table = stem(
        marks, samples[0], next_row, stem_weight, stem_gain[None], stem_bias[None], proj_weight,
        norm_gains.T, biases.T, clips,
    )
    before, after = edges(top, bottom)
    rest_source, _ = lax.optimization_barrier((pos_weight, table))
    rest_weights = conv_weights(False, rest_source, TURNS // 2, TURNS // 2)
    before, after, rest_weights = lax.optimization_barrier((before, after, rest_weights))
    conv_sum = conv_rows(False, marks, before, start_b, after, (one_weights, rest_weights), clips)
    hidden, hidden_b, packed = project_heads(conv_sum, start_x, table, attn_in)
    pairs = [(i, i ^ 1) for i in range(count)]
    alike = [list(range(core, count, 2)) for core in range(2)]
    back_source, _ = lax.optimization_barrier((pos_weight, hidden))
    packed = with_far_blocks(swap(packed), far)
    back_weights = conv_weights(True, back_source, 0, TURNS)
    packed, back_weights = lax.optimization_barrier((packed, back_weights))
    attended_heads, wide, log_total = attend(marks, packed, clips, far)
    attended_heads, hidden_b = lax.optimization_barrier((attended_heads, hidden_b))
    if count == RING:
        gathered = lax.all_gather(hidden_b, "seq", axis=0, tiled=False, axis_index_groups=alike)
    layer_out, grad_heads, grad_pre_second, middle_sums, inner_sums, ffn_kept, ffn_sent, straight = middle(
        marks, clips, swap(attended_heads), hidden, table, attn_out, ffn_in, ffn_in_bias[None], ffn_out, out_grad[0],
        RING,
    )
    near_rows, near_chans, near_inner = width // RING, chans // RING, inner // RING
    if count == RING:
        ffn_other = other_stream(ffn_sent)
    grad_heads = swap(grad_heads)
    packed_grad = attend_back(marks, packed, grad_heads, wide, log_total, clips, far)
    if count == RING:
        packed_grad, gathered = lax.optimization_barrier((packed_grad, gathered))
        other_gathered = lax.ppermute(gathered, "seq", pairs)
        own_heads, sent_heads = head_grads(marks, packed_grad, gathered, other_gathered, clips)
    swapped = swap(fold_far_blocks(packed_grad, far))
    if count == RING:
        other_heads = lax.ppermute(sent_heads, "seq", pairs)
        ffn_other, own_heads = lax.optimization_barrier((ffn_other, own_heads))
        ffn_joined = add_below(ffn_kept, ffn_other, straight)
        swapped, own_heads, _ = lax.optimization_barrier((swapped, own_heads, ffn_joined))
    grad_mixed, grad_conv_b, top, bottom, grad_packed, after_sums, *attn_joined = after_heads(
        swapped, grad_pre_second, hidden, conv_sum, start_x, table, attn_in, count == RING
    )
    if count != RING:
        ffn_joined = jnp.concatenate([straight[:, : ffn_kept.shape[1]], ffn_kept, ffn_sent], axis=1)
        first_blocks = 3 * inner // SHARE // 4
        ffn_joined = regroup(
            ffn_joined,
            [
                (inner // SHARE - first_blocks, near_rows),
                (1, near_inner),
                (first_blocks, near_rows),
                (1, near_inner),
                (2, near_rows),
            ],
        )
    ffn_share = over_seq(ffn_joined)
    before, after = edges(top, bottom)
    before, after, grad_packed = lax.optimization_barrier((before, after, grad_packed))
    grad_groups = swap(grad_packed)
    input_grad = conv_rows(True, marks, before, grad_conv_b, after, (back_weights,), clips)
    shape = (RING // 2,) * 2 if count == RING else (RING,)
    sample_grad, carried, *stem_shares = stem_back(
        marks, input_grad, grad_mixed, normed_b, stem_pre, unfold, stem_weight, stem_gain[None],
        proj_weight, (middle_sums, inner_sums, after_sums), shape, clips,
    )
    carried = from_behind(carried, "seq", 1)
    own = width // count
    own_chans = chans // count
    own_taps = KERNEL // count

    def ffn_parts(share):
        other = other_stream(share)
        if count == RING:
            at = share.shape[0] // 2
            lower = lax.axis_index("rep") == 0
            share = jnp.concatenate(
                [
                    share[:at].astype(jnp.float32) + other[:at].astype(jnp.float32),
                    jnp.where(lower, share[at:], other[at:]).astype(jnp.float32),
                    jnp.where(lower, other[at:], share[at:]).astype(jnp.float32),
                ],
                axis=0,
            )
        else:
            share = share.astype(jnp.float32) + other.astype(jnp.float32)
        most = 3 * inner // 4
        sizes = [(own, inner - most), (inner // count, SHARE), (own, most), (inner // count, SHARE), (own, width)]
        in_end, back_end, in_start, back_start, out = spread_out(share, sizes, SHARE)
        return (
            jnp.concatenate([in_start, in_end], axis=1),
            jnp.concatenate([back_start, back_end], axis=1),
            out,
        )

    if count == RING:
        kept, sent = split_shares(marks, stem_shares[0], lax.ppermute(stem_shares[1], "seq", pairs), clips)
        other_sent = other_stream(sent)
        taps, sent_taps = taps_grad(marks, grad_groups, shape, clips, width)
        sample_grad = sample_grad.at[:1].add(carried)
        other_sent, taps, sent_taps, sample_grad = lax.optimization_barrier(
            (other_sent, taps, sent_taps, sample_grad)
        )
        stem_joined = join_stem(marks, kept, other_sent, own_heads, other_heads, clips)
        received = lax.all_to_all(stem_joined, "seq", 0, 0, axis_index_groups=alike)
        taps = join_pair(marks, taps, lax.ppermute(sent_taps, "seq", pairs), clips)
        taps = add_shares(taps, other_stream(taps))
        taps, received = lax.optimization_barrier((taps, received))
        by_head = received[:, kept.shape[1] :].reshape(RING, -1, PIECE)[:HEADS]
        received = received[:, : kept.shape[1]]
        grad_attn_in = weave_heads(by_head, other_stream(by_head))
        pos_pieces = lax.all_to_all(taps, "seq", 0, 0, axis_index_groups=alike)
        pos_pieces = pos_pieces.reshape(GROUPS, -1, PIECE)
    else:
        sample_grad = sample_grad.at[:1].add(carried)
        attn_share = over_seq(regroup(attn_joined[0], [(3 * width // SHARE, near_rows)]))
        (grad_attn_in,) = spread_out(sum_pair(attn_share), [(own, 3 * width)], SHARE)
        (taps,) = taps_grad(marks, with_far_blocks(grad_groups, 1), shape, clips, width)
        taps = add_shares(taps, other_stream(taps))
        stem_joined = stem_shares[0]
        stem_joined = jnp.concatenate(
            [
                regroup(
                    stem_joined[:, :-32],
                    [(width // PIECE, near_chans), (chans // PIECE, 3 * near_chans)],
                ),
                regroup_small(stem_joined[:, -32:-16], (own, inner // count, own_chans)),
            ],
            axis=1,
        )
        received = lax.all_to_all(stem_joined, "seq", 0, 0)
        segments = count // RING
        by_tap = taps.reshape(2 * TURNS, 3, group_width, PIECE).transpose(0, 2, 1, 3)
        by_tap = by_tap.reshape(2 * TURNS, group_width, TAPS // 2, group_width)
        by_tap = by_tap.transpose(0, 2, 1, 3).reshape(segments, -1, 2 * PIECE)
        across = [[low_at + RING * j for j in range(segments)] for low_at in range(RING)]
        by_tap = lax.all_to_all(by_tap, "seq", 0, 0, axis_index_groups=across)
        by_tap = jnp.sum(by_tap.astype(jnp.float32), axis=0).astype(jnp.bfloat16)
        by_tap = by_tap.reshape(RING, own_taps, group_width, group_width).transpose(0, 2, 1, 3)
        pos_pieces = swap(by_tap.reshape(RING, group_width, own_taps * group_width))
    pos_grad = weave_taps(pos_pieces, own_taps, group_width)
    stem_total = jnp.sum(received.astype(jnp.float32), axis=0).astype(jnp.bfloat16)
    if count == RING:
        other = other_stream(stem_total)
        lower = lax.axis_index("rep") == 0
        stem_total = jnp.concatenate(
            [jnp.where(lower, stem_total, other), jnp.where(lower, other, stem_total)], axis=0
        )[:-16].astype(jnp.float32)
    else:
        stem_total = sum_pair(stem_total)
    grad_proj, grad_stem = spread_out(
        stem_total[:-16], [(own_chans, width), (3 * own_chans, chans)], PIECE
    )
    small = stem_total[-16:]
    grad_ffn_in, grad_ffn_out, grad_attn_out = ffn_parts(ffn_share)
    return (
        layer_out[None],
        sample_grad[None],
        grad_stem,
        small[14, :own_chans],
        small[15, :own_chans],
        grad_proj,
        pos_grad,
        small[:3, :own].T,
        small[3:12, :own].T,
        grad_attn_in,
        grad_attn_out,
        grad_ffn_in,
        small[12:14].reshape(-1)[: inner // count],
        grad_ffn_out,
    )


def solution(mesh):
    streams = P("rep", "seq", None)
    rows = P("seq", None)
    return jax.shard_map(
        local,
        mesh=mesh,
        in_specs=(streams, P("rep", None)) + (P(),) * 12 + (streams,),
        out_specs=(streams, streams, rows, P("seq"), P("seq"))
        + (rows,) * 7
        + (P("seq"), rows),
        check_vma=False,
    )
```
